128 devices in a mesh: dp: 16 (over y_hi, x, core), row: 4 (over z), col: 2 (over y_lo).
Axes of the slice: x: 4, y: 4 (y_hi: 2, y_lo: 2; y = y_hi * 2 + y_lo), z: 4, core: 2. Of those that a mesh axis runs over, the one named last changes fastest.
Arguments:
- x_in: bfloat16 [8192, 1024], P('dp', 'row'), may hold values from -24 to 24
- segments: int32 [16, 512], P('dp'), may hold values from 0 to 3, never falling along the last dimension, each value on 1 to 256 neighbouring positions
- expert_ids: int32 [8192, 8], P('dp'), may hold values from 0 to 31, all different within a row; in each aligned block of 512 rows (0 to 511, 512 to 1023, ...) at most 160 rows name the same one
- cotangent: bfloat16 [8192, 1024], P('dp', 'row'), may hold values from -6 to 6
- norm_gain1: float32 [1024], P('row'), may hold values from 0.5 to 1.5
- w_query: bfloat16 [1024, 1024], P('row', 'col'), may hold values from -12 to 12
- w_key: bfloat16 [1024, 512], P('row', 'col'), may hold values from -1 to 1
- w_value: bfloat16 [1024, 512], P('row', 'col'), may hold values from -0.1875 to 0.1875
- w_out: bfloat16 [1024, 1024], P('col', 'row'), may hold values from -1.5 to 1.5
- norm_gain2: float32 [1024], P('row'), may hold values from 0.5 to 1.5
- w_router: bfloat16 [1024, 32], P('row'), may hold values from -24 to 24
- w_gate: bfloat16 [32, 1024, 512], P(None, 'row', 'col'), may hold values from -0.1875 to 0.1875
- w_up: bfloat16 [32, 1024, 512], P(None, 'row', 'col'), may hold values from -0.1875 to 0.1875
- w_down: bfloat16 [32, 512, 1024], P(None, 'col', 'row'), may hold values from -0.25 to 0.25
Outputs:
- block_out: bfloat16 [8192, 1024], P('dp', 'row')
- grad_input: bfloat16 [8192, 1024], P('dp', 'row')
- grad_query: float32 [1024, 1024], P('row', 'col')
- grad_key: float32 [1024, 512], P('row', 'col')
- grad_value: float32 [1024, 512], P('row', 'col')
- grad_out: float32 [1024, 1024], P('col', 'row')
- grad_router: float32 [1024, 32], P('row')
- grad_gate: float32 [32, 1024, 512], P('dp', 'row', 'col')
- grad_up: float32 [32, 1024, 512], P('dp', 'row', 'col')
- grad_down: float32 [32, 512, 1024], P('dp', 'col', 'row')
- grad_gain1: float32 [1024], P('row')
- grad_gain2: float32 [1024], P('row')
The draws below stay inside these ranges and needn't reach their ends.
Inputs may be any that keep to these rules, and one draw needn't show every extreme that they name: `expert_ids`: each token names 8 different experts; within one sequence no expert is named by more than 160 tokens, and in some sequence one is named by exactly 160. `segments`: segment numbers never fall along a sequence; a segment holds at most 256 tokens, and some segment holds exactly that many.
All inputs are finite; a program needn't handle non-finite values.
Results may differ from the reference program's by a relative error of at most 0.0117.
The reference program's roundings to bfloat16 on the way count: a program that leaves them out, or rounds other values in their place, can miss the bound.
Values may be sent and summed in bfloat16 or wider, within the bound.
A program may use at most 192 MiB of HBM per device.

```python
import math
import jax
import jax.numpy as jnp
import numpy as np
from jax import lax

D = 1024
HEADS = 16
KV_HEADS = 8
HEAD_DIM = 64
EXPERTS = 32
TOPK = 8
FF = 512
LENGTH = 512
DOCS = 4
CAP = 160
NSEQ = 16
TOKENS = 8192


def draw_x_in(key, part):
    key_base = jax.random.fold_in(key, 1)
    column_rise = jnp.arange(D).astype(jnp.float32) / D
    field_values = jax.random.normal(key_base, (TOKENS, D), jnp.float32) * (0.5 + column_rise)
    return jnp.clip(field_values, -24.0, 24.0).astype(jnp.bfloat16)


def attention_pair(key):
    key_keys = jax.random.fold_in(key, 11)
    key_query = jax.random.fold_in(key, 12)
    scale_in = D ** (-0.5)
    key_weight = jax.random.normal(key_keys, (D, KV_HEADS * HEAD_DIM), jnp.float32) * scale_in
    query_weight = jax.random.normal(key_query, (D, HEADS * HEAD_DIM), jnp.float32) * scale_in
    return (jnp.clip(query_weight, -12.0, 12.0), jnp.clip(key_weight, -1.0, 1.0))


def draw_w_query(key, part):
    return attention_pair(key)[0].astype(jnp.bfloat16)


def draw_w_key(key, part):
    return attention_pair(key)[1].astype(jnp.bfloat16)


def draw_w_router(key, part):
    weight_base = jax.random.normal(jax.random.fold_in(key, 21), (D, EXPERTS), jnp.float32) * D ** (-0.5)
    return jnp.clip(weight_base, -24.0, 24.0).astype(jnp.bfloat16)


def steps_of(stream_key, extent, split, smallest, largest):
    level, own = 1.0, jax.random.fold_in(stream_key, 6)
    for axis_at, blocks in split:
        steps = jnp.exp(jax.random.uniform(jax.random.fold_in(own, axis_at), (blocks,), jnp.float32, smallest / len(split), largest / len(split)))
        level = level * jnp.repeat(steps, extent[axis_at] // blocks).reshape([-1 if axis == axis_at else 1 for axis in range(len(extent))])
    return level


def profile(number_of, total, bound, lean):
    weights = [(1 << 20) // math.isqrt(grade ** lean) + 1 for grade in range(2, number_of + 1)]
    surplus, counts = total - bound - (number_of - 1), [1] * (number_of - 1)
    while surplus > 0:
        movable = [i for i in range(number_of - 1) if counts[i] < bound]
        pool, remaining = sum([weights[i] for i in movable]), surplus
        for i in movable:
            more = min(bound - counts[i], max(1, remaining * weights[i] // pool), surplus)
            counts[i] = counts[i] + more
            surplus = surplus - more
    return np.array([bound] + counts)


def uneven_parts(own_key, amount, total, bound, slope):
    if amount == 2:
        one = jax.random.randint(own_key, (), max(1, total - bound), min(bound, total - 1) + 1)
        return jnp.stack([one, total - one])
    lengths = jnp.asarray(profile(amount, total, bound, slope), jnp.int32)
    pairs = (amount - 1) // 2
    giver, sink = lengths[1:1 + 2 * pairs:2], lengths[2:2 + 2 * pairs:2]
    room = jnp.minimum(giver - 1, bound - sink)
    shifted = jax.random.randint(jax.random.fold_in(own_key, 1), (pairs,), 0, 1 << 20) % (room + 1)
    lengths = lengths.at[1:1 + 2 * pairs:2].set(giver - shifted).at[2:2 + 2 * pairs:2].set(sink + shifted)
    return lengths[jax.random.permutation(jax.random.fold_in(own_key, 2), amount)]


def shared_out(stream_key, own, number, rows, amount, top, bound, slope):
    ranking = jax.random.permutation(stream_key, amount)
    packed, ordinary = load_shares(amount, rows * top, bound, slope, True), load_shares(amount, rows * top, bound, slope, False)
    places = jnp.arange(amount)

    def named(sizes, turn):
        used = int((sizes > 0).sum())
        fixed = max(1, used // 4)
        shifted = fixed + (places - fixed + turn * (used - fixed)) % max(1, amount - fixed)
        return jnp.zeros((amount,), jnp.int32).at[ranking[jnp.where(places < fixed, places, shifted)]].set(jnp.asarray(sizes, jnp.int32))

    sizes = jnp.where(number % 4 == 0, named(packed, number // 4), named(ordinary, number - number // 4 - 1))
    mixed = jax.random.permutation(jax.random.fold_in(own, 3), amount)
    giver, sink = mixed[0:amount // 2 * 2:2], mixed[1:amount // 2 * 2:2]
    slack = jnp.minimum(sizes[giver] - 1, bound - sizes[sink]) // 2
    slack = jnp.where((giver == ranking[0]) | (sink == ranking[0]) | (sizes[sink] == 0), 0, jnp.maximum(slack, 0))
    shifted = jax.random.randint(jax.random.fold_in(own, 4), (amount // 2,), 0, 1 << 20) % (slack + 1)
    sizes = sizes.at[giver].add(-shifted).at[sink].add(shifted)
    items = jnp.searchsorted(jnp.cumsum(sizes), jnp.arange(rows * top), side="right").astype(jnp.int32)
    table = items.reshape(top, rows).T
    table = table[jax.random.permutation(jax.random.fold_in(own, 1), rows)]
    turn = jax.random.randint(jax.random.fold_in(own, 2), (rows, 1), 0, top)
    return jnp.take_along_axis(table, (jnp.arange(top)[None, :] + turn) % top, axis=1)


def load_shares(count, total, bound, lean, full):
    loads = [(1 << 20) // math.isqrt(rank ** lean) + 1 for rank in range(1, count + 1)]
    largest = bound if full else min(bound, max(-(-total // count), total * loads[0] // sum(loads)))
    least = 1 if total - largest >= count - 1 else 0
    holding, rest = [largest] + [least] * (count - 1), total - largest - least * (count - 1)
    while rest > 0:
        free = [i for i in range(1, count) if holding[i] < largest] or [i for i in range(1, count) if holding[i] < bound]
        whole, remaining = sum([loads[i] for i in free]), rest
        for i in free:
            extra = min(bound - holding[i], max(1, remaining * loads[i] // whole), rest)
            holding[i] = holding[i] + extra
            rest = rest - extra
    return np.array(holding)


def centred(rng, extent, width, bound, shards=(), kind=jnp.bfloat16):
    entries = width * jax.random.normal(rng, extent, jnp.float32)
    if shards:
        entries = entries * steps_of(rng, extent, shards, -0.22, 0.18)
    return jnp.clip(entries, -bound, bound).astype(kind)


def setup_inputs(seed: int = 0) -> dict:
    key_of = jax.random.split(jax.random.key(seed), 15)
    x_in = draw_x_in(jax.random.fold_in(key_of[14], 71), 0)
    segments = jax.vmap(lambda own: jnp.searchsorted(jnp.cumsum(uneven_parts(own, DOCS, LENGTH, LENGTH // 2, 2)), jnp.arange(LENGTH), side="right"))(jax.random.split(key_of[1], NSEQ)).reshape((NSEQ, LENGTH)).astype(jnp.int32)
    expert_ids_keys = jax.random.split(jax.random.fold_in(key_of[2], 1), TOKENS // LENGTH)
    expert_ids_turns = jax.random.permutation(jax.random.fold_in(key_of[2], 3), TOKENS // LENGTH)
    expert_ids = jax.vmap(lambda own, number: shared_out(jax.random.fold_in(key_of[2], 2), own, number, LENGTH, EXPERTS, TOPK, CAP, 1))(expert_ids_keys, expert_ids_turns).reshape((TOKENS, TOPK))
    cotangent = centred(key_of[3], (TOKENS, D), 1.0, 6.0, ((0, 16), (1, 4)))
    norm_gain1 = jnp.clip(1.0 + 0.1 * jax.random.normal(key_of[4], (D,), jnp.float32), 0.5, 1.5)
    w_query = draw_w_query(jax.random.fold_in(key_of[14], 71), 0)
    w_key = draw_w_key(jax.random.fold_in(key_of[14], 71), 0)
    w_value = centred(key_of[7], (D, KV_HEADS * HEAD_DIM), D ** -0.5, 0.1875, ((0, 4), (1, 2)))
    w_out = centred(key_of[8], (HEADS * HEAD_DIM, D), (HEADS * HEAD_DIM // 64) ** -0.5, 1.5, ((0, 2), (1, 4)))
    norm_gain2 = jnp.clip(1.0 + 0.1 * jax.random.normal(key_of[9], (D,), jnp.float32), 0.5, 1.5)
    w_router = draw_w_router(jax.random.fold_in(key_of[14], 71), 0)
    w_gate = centred(key_of[11], (EXPERTS, D, FF), D ** -0.5, 0.1875, ((1, 4), (2, 2)))
    w_up = centred(key_of[12], (EXPERTS, D, FF), D ** -0.5, 0.1875, ((1, 4), (2, 2)))
    w_down = centred(key_of[13], (EXPERTS, FF, D), FF ** -0.5, 0.25, ((1, 2), (2, 4)))
    return {"x_in": x_in, "segments": segments, "expert_ids": expert_ids, "cotangent": cotangent, "norm_gain1": norm_gain1, "w_query": w_query, "w_key": w_key, "w_value": w_value, "w_out": w_out, "norm_gain2": norm_gain2, "w_router": w_router, "w_gate": w_gate, "w_up": w_up, "w_down": w_down}


EPSILON = 1e-06
ROPE_BASE = 10000.0
MASKED = -1e+30

def rope_tables(positions):
    half_dim = HEAD_DIM // 2
    exponent = jnp.arange(half_dim).astype(jnp.float32) * (2.0 / HEAD_DIM)
    angles = positions.astype(jnp.float32)[:, None] * (ROPE_BASE ** (-exponent))[None, :]
    return (jnp.cos(angles)[:, None, :], jnp.sin(angles)[:, None, :])

def rotate(values_in, cosine, sine_part):
    half_dim = values_in.shape[-1] // 2
    low_half = values_in[..., :half_dim]
    high_half = values_in[..., half_dim:]
    return jnp.concatenate([low_half * cosine - high_half * sine_part, high_half * cosine + low_half * sine_part], axis=-1)

def slot_tables(route_rows):
    count_pairs = route_rows.shape[0] * route_rows.shape[1]
    flat_routes = route_rows.reshape(-1).astype(jnp.int32)
    expert_hits = (flat_routes[:, None] == jnp.arange(EXPERTS, dtype=jnp.int32)[None, :]).astype(jnp.int32)
    running = jnp.cumsum(expert_hits, axis=0).astype(jnp.int32)
    before = lax.optimization_barrier(jnp.sum((running - 1) * expert_hits, axis=1)).astype(jnp.int32)
    slot_of = (flat_routes * CAP + before).astype(jnp.int32)
    pair_of = jnp.full((EXPERTS * CAP,), count_pairs, jnp.int32).at[slot_of].set(jnp.arange(count_pairs, dtype=jnp.int32))
    return (slot_of, pair_of)

def norm_inverse(residual):
    return lax.rsqrt(lax.optimization_barrier(jnp.mean(residual * residual, axis=1, keepdims=True)) + EPSILON)

def norm_backward(residual, inverse, gain, grad_normed):
    weighted = grad_normed * gain
    project = lax.optimization_barrier(jnp.mean(weighted * residual, axis=1, keepdims=True))
    grad_residual = inverse * weighted - residual * inverse ** 3 * project
    grad_gain = lax.optimization_barrier(jnp.sum(grad_normed * residual * inverse, axis=0))
    return (grad_residual, grad_gain)

def one_sequence(tokens_in, segment_row, route_rows, cotangent_rows, norm_gain1, w_query, w_key, w_value, w_out, norm_gain2, w_router, w_gate, w_up, w_down):
    f32 = jnp.float32
    low = jnp.bfloat16
    length = tokens_in.shape[0]
    score_scale = HEAD_DIM ** (-0.5)
    group_size = HEADS // KV_HEADS
    residual = tokens_in.astype(f32)
    scale_attn = norm_inverse(residual)
    normed_attn = (residual * scale_attn * norm_gain1).astype(low)
    cosine, sine_part = rope_tables(jnp.arange(length, dtype=jnp.int32))
    queries = rotate(jnp.dot(normed_attn, w_query, preferred_element_type=f32).reshape(length, HEADS, HEAD_DIM), cosine, sine_part).astype(low)
    keys_all = rotate(jnp.dot(normed_attn, w_key, preferred_element_type=f32).reshape(length, KV_HEADS, HEAD_DIM), cosine, sine_part).astype(low)
    values = jnp.dot(normed_attn, w_value, preferred_element_type=f32).reshape(length, KV_HEADS, HEAD_DIM).astype(low)
    keys_wide = jnp.repeat(keys_all, group_size, axis=1)
    values_wide = jnp.repeat(values, group_size, axis=1)
    places = jnp.arange(length, dtype=jnp.int32)
    allowed = (places[None, :] <= places[:, None]) & (segment_row[None, :] == segment_row[:, None])
    scores = jnp.einsum('qhd,khd->hqk', queries.astype(f32), keys_wide.astype(f32)) * score_scale
    scores = jnp.where(allowed[None], scores, MASKED)
    top_score = lax.optimization_barrier(jnp.max(scores, axis=2, keepdims=True))
    log_total = top_score + jnp.log(lax.optimization_barrier(jnp.sum(jnp.exp(scores - top_score), axis=2, keepdims=True)))
    weights = jnp.exp(scores - log_total)
    weights_low = weights.astype(low)
    attended = jnp.einsum('hqk,khd->qhd', weights_low.astype(f32), values_wide.astype(f32)).astype(low)
    attended_flat = attended.reshape(length, HEADS * HEAD_DIM)
    resid_mid = residual + jnp.dot(attended_flat, w_out, preferred_element_type=f32)
    scale_ffn = norm_inverse(resid_mid)
    normed_ffn = (resid_mid * scale_ffn * norm_gain2).astype(low)
    logits = jnp.dot(normed_ffn, w_router, preferred_element_type=f32)
    gate_probs = jax.nn.softmax(jnp.take_along_axis(logits, route_rows, axis=1), axis=1)
    slot_of, pair_of = slot_tables(route_rows)
    owner_row = pair_of // TOPK
    padded = jnp.concatenate([normed_ffn, jnp.zeros((1, D), low)], axis=0)
    dispatched = jnp.take(padded, owner_row, axis=0).reshape(EXPERTS, CAP, D)
    gate_act = jnp.einsum('ecd,edf->ecf', dispatched.astype(f32), w_gate.astype(f32))
    up_act = jnp.einsum('ecd,edf->ecf', dispatched.astype(f32), w_up.astype(f32))
    sigmoid_gate = jax.nn.sigmoid(gate_act)
    hidden = (gate_act * sigmoid_gate * up_act).astype(low)
    expert_out = jnp.einsum('ecf,efd->ecd', hidden.astype(f32), w_down.astype(f32)).reshape(EXPERTS * CAP, D)
    picked = jnp.take(expert_out, slot_of, axis=0).reshape(length, TOPK, D)
    resid_out = resid_mid + lax.optimization_barrier(jnp.sum(gate_probs[:, :, None] * picked, axis=1))
    block_rows = resid_out.astype(low)
    grad_top = cotangent_rows.astype(f32)
    grad_prob = lax.optimization_barrier(jnp.sum(grad_top[:, None, :] * picked, axis=2))
    grad_chosen = gate_probs * (grad_prob - lax.optimization_barrier(jnp.sum(gate_probs * grad_prob, axis=1, keepdims=True)))
    expert_hits = (route_rows[:, :, None] == jnp.arange(EXPERTS, dtype=jnp.int32)[None, None, :]).astype(f32)
    grad_logits = lax.optimization_barrier(jnp.sum(expert_hits * grad_chosen[:, :, None], axis=1)).astype(low)
    grad_router = jnp.dot(normed_ffn.T, grad_logits, preferred_element_type=f32)
    spread = (gate_probs[:, :, None] * grad_top[:, None, :]).reshape(length * TOPK, D)
    spread = jnp.concatenate([spread, jnp.zeros((1, D), f32)], axis=0)
    slot_grad = jnp.take(spread, pair_of, axis=0).astype(low).reshape(EXPERTS, CAP, D)
    grad_down = jnp.einsum('ecf,ecd->efd', hidden.astype(f32), slot_grad.astype(f32))
    hidden_grad = jnp.einsum('ecd,efd->ecf', slot_grad.astype(f32), w_down.astype(f32))
    grad_gate_act = (hidden_grad * up_act * sigmoid_gate * (1.0 + gate_act * (1.0 - sigmoid_gate))).astype(low)
    grad_up_act = (hidden_grad * gate_act * sigmoid_gate).astype(low)
    grad_gate = jnp.einsum('ecd,ecf->edf', dispatched.astype(f32), grad_gate_act.astype(f32))
    grad_up = jnp.einsum('ecd,ecf->edf', dispatched.astype(f32), grad_up_act.astype(f32))
    slot_input = jnp.einsum('ecf,edf->ecd', grad_gate_act.astype(f32), w_gate.astype(f32))
    slot_input = slot_input + jnp.einsum('ecf,edf->ecd', grad_up_act.astype(f32), w_up.astype(f32))
    slot_input = slot_input.reshape(EXPERTS * CAP, D)
    grad_normed_ffn = lax.optimization_barrier(jnp.sum(jnp.take(slot_input, slot_of, axis=0).reshape(length, TOPK, D), axis=1))
    grad_normed_ffn = grad_normed_ffn + jnp.dot(grad_logits, w_router.T, preferred_element_type=f32)
    grad_ffn_in, grad_gain2 = norm_backward(resid_mid, scale_ffn, norm_gain2, grad_normed_ffn)
    grad_mid = grad_top + grad_ffn_in
    grad_mid_low = grad_mid.astype(low)
    grad_out = jnp.dot(attended_flat.T, grad_mid_low, preferred_element_type=f32)
    grad_attended = jnp.dot(grad_mid_low, w_out.T, preferred_element_type=f32).astype(low).reshape(length, HEADS, HEAD_DIM)
    delta_sum = lax.optimization_barrier(jnp.sum(grad_attended.astype(f32) * attended.astype(f32), axis=2)).T[:, :, None]
    grad_weights = jnp.einsum('qhd,khd->hqk', grad_attended.astype(f32), values_wide.astype(f32))
    grad_scores = (weights * (grad_weights - delta_sum)).astype(low)
    grad_q = jnp.einsum('hqk,khd->qhd', grad_scores.astype(f32), keys_wide.astype(f32)) * score_scale
    grad_k = jnp.einsum('hqk,qhd->khd', grad_scores.astype(f32), queries.astype(f32)) * score_scale
    grad_v = jnp.einsum('hqk,qhd->khd', weights_low.astype(f32), grad_attended.astype(f32))
    grad_k = lax.optimization_barrier(jnp.sum(grad_k.reshape(length, KV_HEADS, group_size, HEAD_DIM), axis=2))
    grad_v = lax.optimization_barrier(jnp.sum(grad_v.reshape(length, KV_HEADS, group_size, HEAD_DIM), axis=2))
    grad_queries = rotate(grad_q, cosine, -sine_part).astype(low).reshape(length, HEADS * HEAD_DIM)
    grad_keys = rotate(grad_k, cosine, -sine_part).astype(low).reshape(length, KV_HEADS * HEAD_DIM)
    grad_values = grad_v.astype(low).reshape(length, KV_HEADS * HEAD_DIM)
    grad_query = jnp.dot(normed_attn.T, grad_queries, preferred_element_type=f32)
    grad_key = jnp.dot(normed_attn.T, grad_keys, preferred_element_type=f32)
    grad_value = jnp.dot(normed_attn.T, grad_values, preferred_element_type=f32)
    grad_normed_attn = jnp.dot(grad_queries, w_query.T, preferred_element_type=f32)
    grad_normed_attn = grad_normed_attn + jnp.dot(grad_keys, w_key.T, preferred_element_type=f32)
    grad_normed_attn = grad_normed_attn + jnp.dot(grad_values, w_value.T, preferred_element_type=f32)
    grad_attn_in, grad_gain1 = norm_backward(residual, scale_attn, norm_gain1, grad_normed_attn)
    grad_rows = (grad_mid + grad_attn_in).astype(low)
    grads = (grad_query, grad_key, grad_value, grad_out, grad_router, grad_gate, grad_up, grad_down, grad_gain1, grad_gain2)
    return (block_rows, grad_rows, grads)

def add_pair(left_sum, right_sum):
    return left_sum + right_sum

def reference(x_in, segments, expert_ids, cotangent, norm_gain1, w_query, w_key, w_value, w_out, norm_gain2, w_router, w_gate, w_up, w_down):
    f32 = jnp.float32
    weights_all = (norm_gain1, w_query, w_key, w_value, w_out, norm_gain2, w_router, w_gate, w_up, w_down)
    starting = (jnp.zeros((D, HEADS * HEAD_DIM), f32), jnp.zeros((D, KV_HEADS * HEAD_DIM), f32), jnp.zeros((D, KV_HEADS * HEAD_DIM), f32), jnp.zeros((HEADS * HEAD_DIM, D), f32), jnp.zeros((D, EXPERTS), f32), jnp.zeros((EXPERTS, D, FF), f32), jnp.zeros((EXPERTS, D, FF), f32), jnp.zeros((EXPERTS, FF, D), f32), jnp.zeros((D,), f32), jnp.zeros((D,), f32))

    def step_fn(totals, inputs):
        tokens_in, segment_row, route_rows, cotangent_rows = inputs
        block_rows, grad_rows, grads = one_sequence(tokens_in, segment_row, route_rows, cotangent_rows, *weights_all)
        return (jax.tree.map(add_pair, totals, grads), (block_rows, grad_rows))
    totals, (outs_all, grads_all) = lax.scan(step_fn, starting, (x_in.reshape(-1, LENGTH, D), segments, expert_ids.reshape(-1, LENGTH, TOPK), cotangent.reshape(-1, LENGTH, D)))
    return (outs_all.reshape(-1, D), grads_all.reshape(-1, D), totals[0], totals[1], totals[2], totals[3], totals[4], totals[5], totals[6], totals[7], totals[8], totals[9])
```

```python
import jax
import jax.numpy as jnp
from jax import lax
from jax.experimental import pallas as pl
from jax.experimental.pallas import tpu as pltpu
from jax.sharding import PartitionSpec as P

D = 1024
HEAD_DIM = 64
EXPERTS = 32
CAP = 160
LENGTH = 512

EPSILON = 1e-06
ROPE_BASE = 10000.0
MASKED = -1e30
F32 = jnp.float32
LOW = jnp.bfloat16
MESH = pl.DeviceIdType.MESH

AXES = ("dp", "row", "col")
CORE = ("dp", 1, 2)
X = ("dp", 2, 4)
Y_HI = ("dp", 8, 2)
Z = ("row", 1, 4)
SIDE = ("col", 1, 2)
TEAM = (Z, SIDE)
PLANE = (Z, X)
ALL_DP = (CORE, X, Y_HI)


def size_of(group):
    n = 1
    for _, _, size in group:
        n *= size
    return n


def at(direction):
    axis, weight, size = direction
    return (lax.axis_index(axis) // weight) % size


def member(group):
    index, scale = 0, 1
    for direction in group:
        index = index + at(direction) * scale
        scale *= direction[2]
    return index


def steps_of(group):
    moves = [()]
    for direction in group:
        moves = [m + (k,) for m in moves for k in range(direction[2])]

    def way(move):
        return sum(
            min(k, d[2] - k) * (2 if d == Y_HI else 1) for d, k in zip(group, move)
        )

    return sorted([m for m in moves if any(m)], key=lambda m: -way(m))


def goal(group, move):
    index, scale = 0, 1
    place = {a: lax.axis_index(a) for a in AXES}
    for direction, k in zip(group, move):
        axis, weight, size = direction
        here = at(direction)
        there = (here + k) % size
        place[axis] = place[axis] + weight * (there - here)
        index = index + there * scale
        scale *= size
    return index, place


def expert_of(x, z, c):
    return c * 16 + x * 4 + z


def exchange(number, *items):
    modes = [i[0] for i in items]
    groups = [i[1] for i in items]
    arrays = [i[2] for i in items]
    count = len(items)
    most = max([8] + [size_of(g) for g in groups])
    moves = {}
    for g in groups:
        for move in steps_of(g):
            full = {d: k for d, k in zip(g, move) if k}
            moves[tuple(sorted(full.items()))] = (g, move)
    delivers = "deliver" in modes

    def kernel(*refs):
        ins, outs = refs[:count], refs[count : 2 * count]
        send, recv, local = refs[2 * count :]
        dp, z, c = (lax.axis_index(a) for a in AXES)
        y_hi, x, core = dp // 8, (dp // 2) % 4, dp % 2
        barrier = pltpu.get_barrier_semaphore()
        owner = c * 8 + x * 2 + z // 2
        slot = (z % 2) * 4 + y_hi * 2 + core
        for g, move in moves.values():
            pl.semaphore_signal(
                barrier, inc=1, device_id=goal(g, move)[1], device_id_type=MESH
            )
        sources = []
        if delivers:
            for i in range(8):
                place = {
                    "dp": ((i // 2) % 2) * 8 + x * 2 + i % 2,
                    "row": core * 2 + i // 4,
                    "col": y_hi,
                }
                mine = (place["dp"] == dp) & (place["row"] == z) & (place["col"] == c)
                sources.append((place, mine))

                @pl.when(jnp.logical_not(mine))
                def _(place=place):
                    pl.semaphore_signal(
                        barrier, inc=1, device_id=place, device_id_type=MESH
                    )

            @pl.when(owner == dp)
            def _():
                pl.semaphore_wait(barrier, len(moves) + 7)

            @pl.when(owner != dp)
            def _():
                pl.semaphore_wait(barrier, len(moves) + 8)

        else:
            pl.semaphore_wait(barrier, len(moves))

        def block(a, index, place):
            if modes[a] == "split":
                return ins[a].at[index]
            if modes[a] == "expert":
                e = expert_of(x, place["row"], place["col"])
                return ins[a].at[e, pl.ds(pl.multiple_of(core * 128, 128), 128), :]
            return ins[a]

        copies = []
        for a in range(count):
            if modes[a] == "deliver":
                continue
            me = member(groups[a])
            for step, move in enumerate(steps_of(groups[a])):
                index, place = goal(groups[a], move)
                copies.append(
                    pltpu.make_async_remote_copy(
                        src_ref=block(a, index, place),
                        dst_ref=outs[a] if modes[a] == "swap" else outs[a].at[me],
                        send_sem=send.at[a, step],
                        recv_sem=recv.at[a, step],
                        device_id=place,
                        device_id_type=MESH,
                    )
                )
                copies[-1].start()
        for a in range(count):
            if modes[a] not in ("swap", "deliver"):
                me = member(groups[a])
                source = block(a, me, {"row": z, "col": c})
                copies.append(pltpu.make_async_copy(source, outs[a].at[me], local.at[a]))
                copies[-1].start()
        for a in range(count):
            if modes[a] == "deliver":

                def remote(j, a=a):
                    return pltpu.make_async_remote_copy(
                        src_ref=ins[a].at[j],
                        dst_ref=outs[a].at[slot],
                        send_sem=send.at[a, j],
                        recv_sem=recv.at[a, slot],
                        device_id={"dp": owner, "row": j % 4, "col": j // 4},
                        device_id_type=MESH,
                    )

                def own(j):
                    return (owner == dp) & (z == j % 4) & (c == j // 4)

                for kz, kc in ((2, 1), (2, 0), (1, 1), (3, 1), (1, 0), (3, 0), (0, 1), (0, 0)):
                    j = (z + kz) % 4 + 4 * ((c + kc) % 2)

                    @pl.when(own(j))
                    def _(j=j, a=a):
                        copy = pltpu.make_async_copy(
                            ins[a].at[j], outs[a].at[slot], local.at[a]
                        )
                        copy.start()
                        copy.wait()

                    @pl.when(jnp.logical_not(own(j)))
                    def _(j=j):
                        remote(j).start()

                for j in range(8):

                    @pl.when(jnp.logical_not(own(j)))
                    def _(j=j):
                        remote(j).wait_send()

                for i in range(8):

                    @pl.when(jnp.logical_not(sources[i][1]))
                    def _(i=i, a=a):
                        pltpu.make_async_remote_copy(
                            src_ref=ins[a].at[0],
                            dst_ref=outs[a].at[i],
                            send_sem=send.at[a, 0],
                            recv_sem=recv.at[a, i],
                            device_id={"dp": owner, "row": 0, "col": 0},
                            device_id_type=MESH,
                        ).wait_recv()

        for copy in copies:
            copy.wait()

    def result(m, g, v):
        shape = v.shape
        if m == "share":
            shape = (size_of(g),) + shape
        elif m == "expert":
            shape = (8, 128, 256)
        return jax.ShapeDtypeStruct(shape, v.dtype)

    spec = pl.BlockSpec(memory_space=pltpu.VMEM)
    far = pl.BlockSpec(memory_space=pl.ANY)
    return pl.pallas_call(
        kernel,
        out_shape=[result(m, g, v) for m, g, v in items],
        in_specs=[far if m == "expert" else spec for m in modes],
        out_specs=[spec] * count,
        scratch_shapes=[
            pltpu.SemaphoreType.DMA((count, most)),
            pltpu.SemaphoreType.DMA((count, most)),
            pltpu.SemaphoreType.DMA((count,)),
        ],
        compiler_params=pltpu.CompilerParams(
            collective_id=number, has_side_effects=True, vmem_limit_bytes=60 * 1024 * 1024
        ),
        name=f"exchange{number}",
    )(*arrays)


def expert_kernel(
    sent_x, sent_top, sent_p, near0, near1, near2,
    returned, gains_back, scaled0, scaled1, total,
    slots_x, slots_top, slots_p, far0, far1, far2, pulled, gains,
    gate_w, up_w, down_w, rows_in, rows_top, hidden_s, gate_s, up_s, out_s, gate_g, up_g,
    block_s, kept, given, other,
    send, recv, send_back, recv_back, send_core, recv_core, local,
):
    dp, z, c = (lax.axis_index(a) for a in AXES)
    x, core = (dp // 2) % 4, dp % 2
    me = member(PLANE)
    near, far = (near0, near1, near2), (far0, far1, far2)
    barrier = pltpu.get_barrier_semaphore()
    steps = steps_of(PLANE)
    mate = goal((CORE,), (1,))[1]
    for move in steps:
        pl.semaphore_signal(
            barrier, inc=1, device_id=goal(PLANE, move)[1], device_id_type=MESH
        )
    pl.semaphore_signal(barrier, inc=1, device_id=mate, device_id_type=MESH)
    pl.semaphore_wait(barrier, len(steps) + 1)

    def to_mate(source, target, k):
        return pltpu.make_async_remote_copy(
            src_ref=source,
            dst_ref=target,
            send_sem=send_core.at[k],
            recv_sem=recv_core.at[k],
            device_id=mate,
            device_id_type=MESH,
        )

    swaps = [to_mate(near[i], far[i], 8 + i) for i in range(3)]
    for copy in swaps:
        copy.start()
    out_going = []
    for k, (source, target) in enumerate(
        ((sent_x, slots_x), (sent_p, slots_p), (sent_top, slots_top))
    ):
        group = []
        for i, move in enumerate(steps):
            index, place = goal(PLANE, move)
            group.append(
                pltpu.make_async_remote_copy(
                    src_ref=source.at[index],
                    dst_ref=target.at[me],
                    send_sem=send.at[k, i],
                    recv_sem=recv.at[k, i],
                    device_id=place,
                    device_id_type=MESH,
                )
            )
            group[-1].start()
        group.append(pltpu.make_async_copy(source.at[me], target.at[me], local.at[k]))
        group[-1].start()
        out_going.append(group)

    for copy in swaps:
        copy.wait()
    for which in range(3):
        for zs in range(4):
            for cs in range(2):
                for half in range(2):
                    part = jnp.where(
                        core == half, near[which][zs + 4 * cs], far[which][zs + 4 * cs]
                    )
                    if which < 2:
                        (gate_w, up_w)[which][
                            zs * 256 + half * 128 : zs * 256 + half * 128 + 128,
                            cs * 256 : cs * 256 + 256,
                        ] = part
                    else:
                        down_w[
                            cs * 256 + half * 128 : cs * 256 + half * 128 + 128,
                            zs * 256 : zs * 256 + 256,
                        ] = part
    for copy in out_going[0]:
        copy.wait()

    def forward(s, _):
        span = pl.ds(pl.multiple_of(s * CAP, CAP), CAP)
        x_rows = jnp.concatenate([slots_x[4 * s + j] for j in range(4)], axis=1)
        gate_act = dot(x_rows, gate_w[...], ((1,), (0,)))
        up_act = dot(x_rows, up_w[...], ((1,), (0,)))
        hidden = (gate_act * jax.nn.sigmoid(gate_act) * up_act).astype(LOW)
        out_s[span, :] = dot(hidden, down_w[...], ((1,), (0,)))
        rows_in[span, :] = x_rows
        hidden_s[span, :] = hidden
        gate_s[span, :] = gate_act
        up_s[span, :] = up_act
        return 0

    lax.fori_loop(0, 4, forward, 0)
    for copy in out_going[1] + out_going[2]:
        copy.wait()

    def home_of(s, j):
        place = {"dp": dp + 2 * (s - x), "row": j, "col": c}
        return place, 4 * s + j

    def go_back(s, j, from_x, from_g):
        place, index = home_of(s, j)
        return [
            pltpu.make_async_remote_copy(
                src_ref=source,
                dst_ref=target.at[me],
                send_sem=send_back.at[k, index],
                recv_sem=recv_back.at[k, me],
                device_id=place,
                device_id_type=MESH,
            )
            for k, (source, target) in enumerate(((from_x, returned), (from_g, gains_back)))
        ]

    def backward(i, _):
        s = (x + 2 + i) % 4
        span = pl.ds(pl.multiple_of(s * CAP, CAP), CAP)
        top = jnp.concatenate([slots_top[4 * s + j] for j in range(4)], axis=1).astype(F32)
        p = jnp.transpose(slots_p[4 * s])[:CAP, :1]
        gate_act, up_act, out = gate_s[span, :], up_s[span, :], out_s[span, :]
        sig = jax.nn.sigmoid(gate_act)
        slot_grad = (p * top).astype(LOW)
        hidden_grad = dot(slot_grad, down_w[...], ((1,), (1,)))
        grad_gate = (hidden_grad * up_act * sig * (1.0 + gate_act * (1.0 - sig))).astype(LOW)
        grad_up = (hidden_grad * gate_act * sig).astype(LOW)
        pull = dot(grad_gate, gate_w[...], ((1,), (1,)))
        pull = (pull + dot(grad_up, up_w[...], ((1,), (1,)))).astype(LOW)
        gain = jnp.sum(top * out, axis=1, keepdims=True)
        gains[s] = jnp.zeros((8, 256), F32)
        gains[s, :, :CAP] = jnp.transpose(jnp.broadcast_to(gain, (CAP, 128)))[:8]
        for j in range(4):
            pulled[j, s] = pull[:, j * 256 : j * 256 + 256]
        rows_top[span, :] = slot_grad
        gate_g[span, :] = grad_gate
        up_g[span, :] = grad_up
        out = (p * out).astype(LOW)
        for j in range(4):
            scaled0[4 * s + j] = out[: CAP // 2, j * 256 : j * 256 + 256]
            scaled1[4 * s + j] = out[CAP // 2 :, j * 256 : j * 256 + 256]
        for kz in (2, 1, 3, 0):
            j = (z + kz) % 4

            @pl.when((s != x) | (j != z))
            def _(j=j):
                for copy in go_back(s, j, pulled.at[j, s], gains.at[s]):
                    copy.start()

        return 0

    lax.fori_loop(0, 4, backward, 0)
    near_rows = pl.ds(pl.multiple_of(core * 128, 128), 128)
    far_rows = pl.ds(pl.multiple_of((1 - core) * 128, 128), 128)

    def block(m, _):
        wide = pl.ds(pl.multiple_of((m % 4) * 256, 256), 256)
        narrow = pl.ds(pl.multiple_of((m // 4) * 256, 256), 256)
        for which in range(3):
            if which < 2:
                left, right = rows_in[:, wide], (gate_g, up_g)[which][:, narrow]
            else:
                left, right = hidden_s[:, narrow], rows_top[:, wide]
            block_s[...] = dot(left, right, ((0,), (0,)))
            given[m, which] = block_s[far_rows, :].astype(LOW)
            kept[m, which] = block_s[near_rows, :]
        to_mate(given.at[m], other.at[m], m).start()
        return 0

    lax.fori_loop(0, 8, block, 0)
    returned[me] = pulled[z, x]
    gains_back[me] = gains[x]

    def add(m, _):
        to_mate(given.at[m], other.at[m], m).wait()
        total[m] = (kept[m] + other[m].astype(F32)).astype(LOW)
        return 0

    lax.fori_loop(0, 8, add, 0)
    for move in steps:
        index, place = goal(PLANE, move)
        for k, (source, target) in enumerate(
            ((pulled.at[0, 0], returned), (gains.at[0], gains_back))
        ):
            copy = pltpu.make_async_remote_copy(
                src_ref=source,
                dst_ref=target.at[index],
                send_sem=send_back.at[k, index],
                recv_sem=recv_back.at[k, index],
                device_id=place,
                device_id_type=MESH,
            )
            copy.wait_send()
            copy.wait_recv()


def expert_step(number, *operands):
    spec = pl.BlockSpec(memory_space=pltpu.VMEM)
    rows_of = jax.ShapeDtypeStruct((16, CAP, 256), LOW)
    return pl.pallas_call(
        expert_kernel,
        out_shape=[
            rows_of,
            jax.ShapeDtypeStruct((16, 8, 256), F32),
            jax.ShapeDtypeStruct((16, CAP // 2, 256), LOW),
            jax.ShapeDtypeStruct((16, CAP // 2, 256), LOW),
            jax.ShapeDtypeStruct((8, 3, 128, 256), LOW),
        ],
        in_specs=[spec] * 6,
        out_specs=[spec] * 5,
        scratch_shapes=[
            pltpu.VMEM((16, CAP, 256), LOW),
            pltpu.VMEM((16, CAP, 256), LOW),
            pltpu.VMEM((16, 8, 256), F32),
            pltpu.VMEM((8, 128, 256), LOW),
            pltpu.VMEM((8, 128, 256), LOW),
            pltpu.VMEM((8, 128, 256), LOW),
            pltpu.VMEM((4, 4, CAP, 256), LOW),
            pltpu.VMEM((4, 8, 256), F32),
            pltpu.VMEM((D, 512), LOW),
            pltpu.VMEM((D, 512), LOW),
            pltpu.VMEM((512, D), LOW),
            pltpu.VMEM((640, D), LOW),
            pltpu.VMEM((640, D), LOW),
            pltpu.VMEM((640, 512), LOW),
            pltpu.VMEM((640, 512), F32),
            pltpu.VMEM((640, 512), F32),
            pltpu.VMEM((640, D), F32),
            pltpu.VMEM((640, 512), LOW),
            pltpu.VMEM((640, 512), LOW),
            pltpu.VMEM((256, 256), F32),
            pltpu.VMEM((8, 3, 128, 256), F32),
            pltpu.VMEM((8, 3, 128, 256), LOW),
            pltpu.VMEM((8, 3, 128, 256), LOW),
            pltpu.SemaphoreType.DMA((3, 15)),
            pltpu.SemaphoreType.DMA((3, 15)),
            pltpu.SemaphoreType.DMA((2, 16)),
            pltpu.SemaphoreType.DMA((2, 16)),
            pltpu.SemaphoreType.DMA((11,)),
            pltpu.SemaphoreType.DMA((11,)),
            pltpu.SemaphoreType.DMA((3,)),
        ],
        compiler_params=pltpu.CompilerParams(
            collective_id=number, has_side_effects=True, vmem_limit_bytes=60 * 1024 * 1024
        ),
        name="expert",
    )(*operands)


TAIL_OUT = (
    ((8, 3, 128, 256), LOW),
    ((16, 32, 256), LOW),
    ((16, 8, 256), F32),
    ((16, 16, 1024), LOW),
    ((16, 8, 256), F32),
    ((512, 256), LOW),
    ((512, 256), LOW),
)
TAIL_SCRATCH = (
    ((512, 256), LOW),
    ((2, 16, 512), F32),
    ((8, 8, 512), F32),
    ((4, 32, 512), F32),
    ((4, 128, 256), LOW),
    ((16, 80, 256), LOW),
    ((16, 80, 256), LOW),
    ((512, 256), LOW),
    ((4, 512, 256), LOW),
    ((512, 256), F32),
    ((512, 256), LOW),
    ((16, 32, 256), LOW),
    ((32, 256), LOW),
    ((16, 8, 256), F32),
    ((16, 8, 256), F32),
    ((8, 256), F32),
    ((512, 256), LOW),
    ((4, 512, 256), LOW),
    ((512, 1024), LOW),
    ((512, 256), LOW),
    ((512, 256), LOW),
    ((8, 512), F32),
    ((8, 8, 512), F32),
    ((256, 1024), LOW),
    ((16, 16, 1024), LOW),
    ((16, 1024), LOW),
    ((8, 256), F32),
    ((512, 256), F32),
    ((512, 256), LOW),
    ((512, 256), LOW),
)
TAIL_SEMS = 224


def as_row(column):
    return jnp.transpose(jnp.broadcast_to(column, (512, 128)))[:8]


def as_column(row):
    return jnp.transpose(jnp.broadcast_to(row, (8, 512)))[:, :1]


def tail_kernel(
    home_ref, gain_own_ref, pull_ref, router_gain_ref, w_out_ref, scaled0_ref, scaled1_ref,
    kept_ref, resid_mid_ref, cot_ref, scale_ffn_ref, gain2_ref, probs_ref, router_ref,
    normed_ffn_ref, attended_all_ref, attended_ref, queries_ref, keys_ref, values_ref,
    weights_ref, cos_q_ref, sin_q_ref, cos_kv_ref, sin_kv_ref, whole_ref, normed_own_ref,
    x_in_ref, scale_attn_ref, gain1_ref, own_rank_ref, owned_ref, out_sum_ref,
    router_sum_ref, joined_sum_ref, gains_ref, block_out_ref, grad_input_ref, home2_ref,
    gain_pair_ref, pulls_ref, router_pull_ref, out_heads_ref, back0_ref, back1_ref, mid_ref,
    mid_all_ref, grad_mid_ref, g_out_ref, out_parts_ref, out_chunk_ref, g_router_ref,
    router_parts_ref, router_chunk_ref, proj_ref, proj_all_ref, flat_ref, gn_ref, gn2_ref,
    pull2_ref, pulls2_ref, g_joined_ref, joined_parts_ref, joined_chunk_ref, gains_own_ref,
    moe_sum_ref, moe_ref, moe2_ref, send, recv,
):
    dp, z, c = (lax.axis_index(a) for a in AXES)
    y_hi, x, core = dp // 8, (dp // 2) % 4, dp % 2
    owner = c * 8 + x * 2 + z // 2
    slot = (z % 2) * 4 + y_hi * 2 + core
    barrier = pltpu.get_barrier_semaphore()
    moves = {}
    for g in (TEAM, PLANE, ALL_DP):
        for move in steps_of(g):
            full = {d: k for d, k in zip(g, move) if k}
            moves[tuple(sorted(full.items()))] = (g, move)
    for g, move in moves.values():
        pl.semaphore_signal(barrier, inc=1, device_id=goal(g, move)[1], device_id_type=MESH)
    sources = []
    for i in range(8):
        place = {
            "dp": ((i // 2) % 2) * 8 + x * 2 + i % 2,
            "row": core * 2 + i // 4,
            "col": y_hi,
        }
        mine = (place["dp"] == dp) & (place["row"] == z) & (place["col"] == c)
        sources.append(mine)

        @pl.when(jnp.logical_not(mine))
        def _(place=place):
            pl.semaphore_signal(barrier, inc=1, device_id=place, device_id_type=MESH)

    @pl.when(owner == dp)
    def _():
        pl.semaphore_wait(barrier, len(moves) + 7)

    @pl.when(owner != dp)
    def _():
        pl.semaphore_wait(barrier, len(moves) + 8)

    used = [0]

    def begin(mode, group, source, target):
        me = member(group)
        copies = []
        for move in steps_of(group):
            index, place = goal(group, move)
            copies.append(
                pltpu.make_async_remote_copy(
                    src_ref=source(index) if mode == "split" else source,
                    dst_ref=target if mode == "swap" else target.at[me],
                    send_sem=send.at[used[0]],
                    recv_sem=recv.at[used[0]],
                    device_id=place,
                    device_id_type=MESH,
                )
            )
            used[0] += 1
            copies[-1].start()
        if mode != "swap":
            target[me] = source(me)[...] if mode == "split" else source[...]
        return copies

    def wait(copies):
        for copy in copies:
            copy.wait()

    kept, owned = kept_ref, owned_ref
    first_deliver = TAIL_SEMS - 24

    def parcel(which, j, to_slot):
        return pltpu.make_async_remote_copy(
            src_ref=kept.at[j, which],
            dst_ref=owned.at[to_slot, which],
            send_sem=send.at[first_deliver + which * 8 + j],
            recv_sem=recv.at[first_deliver + which * 8 + to_slot],
            device_id={"dp": owner, "row": j % 4, "col": j // 4},
            device_id_type=MESH,
        )

    def own(j):
        return (owner == dp) & (z == j % 4) & (c == j // 4)

    def deliver(which):
        for kz, kc in ((2, 1), (2, 0), (1, 1), (3, 1), (1, 0), (3, 0), (0, 1), (0, 0)):
            j = (z + kz) % 4 + 4 * ((c + kc) % 2)

            @pl.when(own(j))
            def _(j=j):
                owned[slot, which] = kept[j, which]

            @pl.when(jnp.logical_not(own(j)))
            def _(j=j):
                parcel(which, j, slot).start()

    first = begin("swap", (SIDE,), home_ref, home2_ref)
    first += begin("share", (SIDE,), gain_own_ref, gain_pair_ref)
    first += begin("share", TEAM, pull_ref, pulls_ref)
    first += begin("share", (Z,), router_gain_ref, router_pull_ref)
    heads = begin("split", (Z,), lambda j: w_out_ref.at[j], out_heads_ref)
    back0 = begin("split", PLANE, lambda j: scaled0_ref.at[j], back0_ref)
    wait(first)
    home = home_ref[...].astype(F32) + home2_ref[...].astype(F32)
    grad_prob = jnp.concatenate([gain_pair_ref[0], gain_pair_ref[1]], axis=0)
    probs = probs_ref[...]
    inner = jnp.sum(probs * grad_prob, axis=0, keepdims=True)
    grad_logits = (probs * (grad_prob - inner)).astype(LOW)
    router_pull = (router_pull_ref[0] + router_pull_ref[1]) + (
        router_pull_ref[2] + router_pull_ref[3]
    )
    row = jnp.sum(grad_logits.astype(F32) * router_pull, axis=0, keepdims=True)
    for i in range(8):
        row = row + pulls_ref[i, :1]
    project = as_column(row) / D
    grad_normed = home + dot(grad_logits, router_ref[...], ((0,), (0,)))
    resid_mid, scale = resid_mid_ref[...], scale_ffn_ref[...]
    weighted = grad_normed * gain2_ref[...]
    grad_mid = (
        cot_ref[...].astype(F32) + scale * weighted - resid_mid * scale**3 * project
    )
    mid_ref[...] = grad_mid.astype(LOW)
    grad_mid_ref[...] = grad_mid
    gains_own_ref[...] = jnp.zeros((8, 256), F32)
    gains_own_ref[1:2] = jnp.sum(grad_normed * resid_mid * scale, axis=0, keepdims=True)
    middle = begin("share", (Z,), mid_ref, mid_all_ref)
    grad_router = dot(grad_logits, normed_ffn_ref[...], ((1,), (0,)))
    g_router_ref[...] = jnp.zeros((16, 8, 256), F32)
    for j in range(16):
        g_router_ref[j, :2] = grad_router[2 * j : 2 * j + 2]
    for j in range(4):
        g_out_ref[j * 128 : j * 128 + 128] = dot(
            attended_all_ref[4 * c + j], mid_ref[...], ((0,), (0,))
        ).astype(LOW)
    sums = begin(
        "split",
        ALL_DP,
        lambda j: g_out_ref.at[pl.ds(pl.multiple_of(j * 32, 32), 32)],
        out_parts_ref,
    )
    sums += begin("split", ALL_DP, lambda j: g_router_ref.at[j], router_parts_ref)
    deliver(0)

    wait(heads)
    wait(middle)
    grad_att = dot(mid_all_ref[0], out_heads_ref[0], ((1,), (1,)))
    for j in range(1, 4):
        grad_att = grad_att + dot(mid_all_ref[j], out_heads_ref[j], ((1,), (1,)))
    grad_att = grad_att.astype(LOW)
    product = grad_att.astype(F32) * attended_ref[...].astype(F32)
    keys, values = keys_ref[...], values_ref[...]
    grad_q = []
    grad_k = jnp.zeros((512, HEAD_DIM), F32)
    grad_v = jnp.zeros((512, HEAD_DIM), F32)
    for h in range(2):
        span = slice(h * HEAD_DIM, h * HEAD_DIM + HEAD_DIM)
        grad_h = grad_att[:, span]
        weights = weights_ref[h]
        delta = jnp.sum(product[:, span], axis=1, keepdims=True)
        grad_weights = dot(grad_h, values, ((1,), (1,)))
        grad_scores = (weights * (grad_weights - delta)).astype(LOW)
        grad_q.append(dot(grad_scores, keys, ((1,), (0,))))
        grad_k = grad_k + dot(grad_scores, queries_ref[:, span], ((0,), (0,)))
        grad_v = grad_v + dot(weights.astype(LOW), grad_h, ((0,), (0,)))
    score_scale = HEAD_DIM ** (-0.5)
    low_lane = lax.broadcasted_iota(jnp.int32, (512, 128), 1) % 64 < 32

    def turn(value, cosine, sine_part):
        other = jnp.where(low_lane, pltpu.roll(value, 96, 1), pltpu.roll(value, 32, 1))
        return (value * cosine + other * sine_part).astype(LOW)

    both = jnp.concatenate(grad_q, axis=1) * score_scale
    proj_ref[:, :128] = turn(both, cos_q_ref[...], sin_q_ref[...])
    both = jnp.concatenate([grad_k * score_scale, grad_v], axis=1)
    proj_ref[:, 128:] = turn(both, cos_kv_ref[...], sin_kv_ref[...])
    projected = begin("share", (Z,), proj_ref, proj_all_ref)
    back1 = begin("split", PLANE, lambda j: scaled1_ref.at[j], back1_ref)

    wait(sums)
    total = out_parts_ref[0].astype(F32)
    routed = router_parts_ref[0]
    for j in range(1, 16):
        total = total + out_parts_ref[j].astype(F32)
        routed = routed + router_parts_ref[j]
    out_chunk_ref[...] = total.astype(LOW)
    router_chunk_ref[...] = routed
    rest = begin("share", ALL_DP, out_chunk_ref, out_sum_ref)
    rest += begin("share", ALL_DP, router_chunk_ref, router_sum_ref)
    moe_sum_ref[...] = jnp.zeros((512, 256), F32)

    def add_half(rows_of, start):
        def one(e, _):
            places = lax.broadcasted_iota(jnp.int32, (80, 512), 0) + start
            taken = (own_rank_ref[e] == places).astype(F32).astype(LOW)
            moe_sum_ref[...] += dot(taken, rows_of[e], ((0,), (0,)))
            return 0

        lax.fori_loop(0, 16, one, 0)

    wait(back0)
    add_half(back0_ref, 0)

    wait(projected)
    for j in range(4):
        flat_ref[:, j * 128 : j * 128 + 128] = proj_all_ref[j, :, :128]
        flat_ref[:, 512 + j * 64 : 576 + j * 64] = proj_all_ref[j, :, 128:192]
        flat_ref[:, 768 + j * 64 : 832 + j * 64] = proj_all_ref[j, :, 192:]
    grad_low = dot(flat_ref[...], whole_ref[...], ((1,), (1,))).astype(LOW)
    residual, gain1 = x_in_ref[...].astype(F32), gain1_ref[...]
    gn_ref[...] = grad_low
    pull = jnp.sum(grad_low.astype(F32) * gain1 * residual, axis=1, keepdims=True)
    pull2_ref[...] = as_row(pull)
    meet = begin("swap", (SIDE,), gn_ref, gn2_ref)
    meet += begin("share", TEAM, pull2_ref, pulls2_ref)
    g_joined_ref[...] = dot(normed_own_ref[...], flat_ref[...], ((0,), (0,))).astype(LOW)
    joined = begin(
        "split",
        ALL_DP,
        lambda j: g_joined_ref.at[pl.ds(pl.multiple_of(j * 16, 16), 16)],
        joined_parts_ref,
    )
    deliver(1)
    wait(back1)
    add_half(back1_ref, 80)
    moe_ref[...] = moe_sum_ref[...].astype(LOW)
    moe = begin("swap", (SIDE,), moe_ref, moe2_ref)
    wait(meet)
    grad_normed = gn_ref[...].astype(F32) + gn2_ref[...].astype(F32)
    row = pulls2_ref[0, :1]
    for i in range(1, 8):
        row = row + pulls2_ref[i, :1]
    project = as_column(row) / D
    weighted = grad_normed * gain1
    scale = scale_attn_ref[...]
    grad_input_ref[...] = (
        grad_mid_ref[...] + scale * weighted - residual * scale**3 * project
    ).astype(LOW)
    gains_own_ref[0:1] = jnp.sum(grad_normed * residual * scale, axis=0, keepdims=True)
    wait(joined)
    total = joined_parts_ref[0].astype(F32)
    for j in range(1, 16):
        total = total + joined_parts_ref[j].astype(F32)
    joined_chunk_ref[...] = total.astype(LOW)
    rest += begin("share", ALL_DP, joined_chunk_ref, joined_sum_ref)
    rest += begin("share", ALL_DP, gains_own_ref, gains_ref)
    deliver(2)
    wait(moe)
    block_out_ref[...] = (
        resid_mid + (moe_ref[...].astype(F32) + moe2_ref[...].astype(F32))
    ).astype(LOW)
    wait(rest)
    for which in range(3):
        for j in range(8):

            @pl.when(jnp.logical_not(own(j)))
            def _(j=j, which=which):
                parcel(which, j, slot).wait_send()

            @pl.when(jnp.logical_not(sources[j]))
            def _(j=j, which=which):
                parcel(which, 0, j).wait_recv()


def tail_step(number, *operands):
    spec = pl.BlockSpec(memory_space=pltpu.VMEM)
    return pl.pallas_call(
        tail_kernel,
        out_shape=[jax.ShapeDtypeStruct(*v) for v in TAIL_OUT],
        in_specs=[spec] * len(operands),
        out_specs=[spec] * len(TAIL_OUT),
        scratch_shapes=[pltpu.VMEM(*v) for v in TAIL_SCRATCH]
        + [pltpu.SemaphoreType.DMA((TAIL_SEMS,)), pltpu.SemaphoreType.DMA((TAIL_SEMS,))],
        compiler_params=pltpu.CompilerParams(
            collective_id=number, has_side_effects=True, vmem_limit_bytes=60 * 1024 * 1024
        ),
        name="tail",
    )(*operands)


def rope_tables(positions):
    half_dim = HEAD_DIM // 2
    exponent = jnp.arange(half_dim).astype(F32) * (2.0 / HEAD_DIM)
    angles = positions.astype(F32)[:, None] * (ROPE_BASE ** (-exponent))[None, :]
    return (jnp.cos(angles)[:, None, :], jnp.sin(angles)[:, None, :])


def rotate(values_in, cosine, sine_part):
    half_dim = values_in.shape[-1] // 2
    low_half = values_in[..., :half_dim]
    high_half = values_in[..., half_dim:]
    return jnp.concatenate(
        [low_half * cosine - high_half * sine_part, high_half * cosine + low_half * sine_part],
        axis=-1,
    )


def dot(a, b, dims):
    return lax.dot_general(a, b, (dims, ((), ())), preferred_element_type=F32)


def rows(vector):
    return vector.reshape(4, 128)


def on_device(
    x_in,
    segments,
    expert_ids,
    cotangent,
    norm_gain1,
    w_query,
    w_key,
    w_value,
    w_out,
    norm_gain2,
    w_router,
    w_gate,
    w_up,
    w_down,
):
    dp, z, c = (lax.axis_index(a) for a in ("dp", "row", "col"))
    score_scale = HEAD_DIM ** (-0.5)

    joined = jnp.concatenate(
        [
            w_query.reshape(256, 4, 128),
            w_key.reshape(256, 4, 64),
            w_value.reshape(256, 4, 64),
        ],
        axis=2,
    )
    x_all, head_weights, gain_all, out_all = exchange(
        2,
        ("share", (Z,), x_in),
        ("split", (Z,), joined.transpose(1, 0, 2)),
        ("share", (Z,), norm_gain1.reshape(2, 128)),
        ("share", (SIDE,), w_out),
    )
    out_all = out_all.reshape(1024, 256)
    residual_all = x_all.astype(F32)
    scale_attn = lax.rsqrt(jnp.sum(residual_all * residual_all, axis=(0, 2)) / D + EPSILON)[
        :, None
    ]
    normed_all = (residual_all * scale_attn[None] * gain_all.reshape(4, 1, 256)).astype(LOW)
    normed_flat = normed_all.transpose(1, 0, 2).reshape(LENGTH, D)
    projected = dot(normed_flat, head_weights.reshape(D, 256), ((1,), (0,)))
    cosine, sine_part = rope_tables(jnp.arange(LENGTH, dtype=jnp.int32))
    queries = rotate(projected[:, :128].reshape(LENGTH, 2, HEAD_DIM), cosine, sine_part)
    queries = queries.astype(LOW)
    keys = rotate(projected[:, 128:192].reshape(LENGTH, 1, HEAD_DIM), cosine, sine_part)
    keys = keys.astype(LOW)[:, 0]
    values = projected[:, 192:].astype(LOW)
    places = jnp.arange(LENGTH, dtype=jnp.int32)
    segment_row = segments.reshape(-1)
    allowed = (places[None, :] <= places[:, None]) & (
        segment_row[None, :] == segment_row[:, None]
    )
    scores = jnp.einsum("qhd,kd->hqk", queries, keys, preferred_element_type=F32) * score_scale
    scores = jnp.where(allowed[None], scores, MASKED)
    top_score = jnp.max(scores, axis=2, keepdims=True)
    log_total = top_score + jnp.log(jnp.sum(jnp.exp(scores - top_score), axis=2, keepdims=True))
    weights = jnp.exp(scores - log_total)
    weights_low = weights.astype(LOW)
    attended = jnp.einsum("hqk,kd->qhd", weights_low, values, preferred_element_type=F32)
    attended = attended.astype(LOW).reshape(LENGTH, 128)

    attended_all, near_gate = exchange(
        4, ("share", TEAM, attended), ("expert", TEAM, w_gate)
    )
    attended_flat = attended_all.transpose(1, 0, 2).reshape(LENGTH, 1024)
    residual = x_in.astype(F32)
    resid_mid = residual + dot(attended_flat, out_all, ((1,), (0,)))
    square_parts, near_up = exchange(
        5,
        ("share", (Z,), rows(jnp.sum(resid_mid * resid_mid, axis=1))),
        ("expert", TEAM, w_up),
    )
    squares = jnp.sum(square_parts, axis=0).reshape(LENGTH)
    scale_ffn = lax.rsqrt(squares / D + EPSILON)[:, None]
    normed_ffn = (resid_mid * scale_ffn * norm_gain2).astype(LOW)
    router = w_router.T
    router_gain = lax.dot_general(
        router.astype(F32),
        resid_mid * norm_gain2,
        (((1,), (1,)), ((), ())),
        precision=lax.Precision.HIGHEST,
        preferred_element_type=F32,
    )
    logit_parts, near_down = exchange(
        6,
        ("share", (Z,), dot(router, normed_ffn, ((1,), (1,)))),
        ("expert", TEAM, w_down),
    )
    logits = jnp.sum(logit_parts, axis=0)

    experts = jnp.arange(EXPERTS, dtype=jnp.int32)[:, None]
    hits = jnp.any(expert_ids.T[None, :, :] == experts[:, :, None], axis=1)
    chosen = jnp.where(hits, logits, MASKED)
    chosen = jnp.where(hits, jnp.exp(chosen - jnp.max(chosen, axis=0, keepdims=True)), 0.0)
    probs = chosen / jnp.sum(chosen, axis=0, keepdims=True)
    earlier = (places[:, None] < places[None, :]).astype(LOW)
    rank = dot(hits.astype(LOW), earlier, ((1,), (0,)))
    rank = jnp.where(hits, rank, -1.0).astype(jnp.int32)
    own_rank = lax.dynamic_slice(rank, (c * 16, 0), (16, LENGTH))
    own_probs = lax.dynamic_slice(probs, (c * 16, 0), (16, LENGTH))
    taken = own_rank[:, None, :] == jnp.arange(CAP, dtype=jnp.int32)[None, :, None]
    pick = taken.astype(LOW)
    sent_x = jnp.einsum("est,td->esd", pick, normed_ffn, preferred_element_type=F32)
    sent_top = jnp.einsum("est,td->esd", pick, cotangent, preferred_element_type=F32)
    slot_probs = jnp.sum(jnp.where(taken, own_probs[:, None, :], 0.0), axis=2)
    slot_probs = jnp.pad(slot_probs, ((0, 0), (0, 96)))
    slot_probs = jnp.broadcast_to(slot_probs[:, None, :], (16, 8, 256))
    pulled, gain_rows, scaled0, scaled1, kept = expert_step(
        7, sent_x.astype(LOW), sent_top.astype(LOW), slot_probs, near_gate, near_up, near_down
    )

    home = jnp.einsum("est,esd->td", pick, pulled, preferred_element_type=F32).astype(LOW)
    gain_rows = gain_rows[:, 0, :CAP]
    own_gain = jnp.sum(jnp.where(taken, gain_rows[:, :, None], 0.0), axis=1)
    pull = jnp.sum(home.astype(F32) * norm_gain2 * resid_mid, axis=1)
    cos_part, sin_part = cosine[:, 0], sine_part[:, 0]
    idle = jnp.zeros((LENGTH, HEAD_DIM), F32)
    owned, out_sum, router_sum, joined_sum, gains, block_out, grad_input = tail_step(
        11,
        home,
        own_gain,
        jnp.broadcast_to(pull[None], (8, LENGTH)),
        router_gain,
        w_out.reshape(4, 128, 256),
        scaled0,
        scaled1,
        kept,
        resid_mid,
        cotangent,
        scale_ffn,
        norm_gain2.reshape(1, 256),
        probs,
        router,
        normed_ffn,
        attended_all,
        attended,
        queries.reshape(LENGTH, 128),
        keys,
        values,
        weights,
        jnp.concatenate([cos_part] * 4, axis=1),
        jnp.concatenate([sin_part, -sin_part] * 2, axis=1),
        jnp.concatenate([cos_part, cos_part, idle + 1.0], axis=1),
        jnp.concatenate([sin_part, -sin_part, idle], axis=1),
        jnp.concatenate([w_query, w_key, w_value], axis=1),
        (residual * scale_attn * norm_gain1).astype(LOW),
        x_in,
        scale_attn,
        norm_gain1.reshape(1, 256),
        own_rank.reshape(16, 1, LENGTH),
    )
    joined_sum = joined_sum.reshape(256, 1024).astype(F32)
    gain_sum = jnp.sum(gains, axis=0)
    owned = jnp.sum(owned.astype(F32).reshape(2, 2, 2, 3, 128, 256), axis=1)
    owned = owned.transpose(2, 0, 1, 3, 4).reshape(3, 2, 256, 256)
    return (
        block_out,
        grad_input,
        joined_sum[:, :512],
        joined_sum[:, 512:768],
        joined_sum[:, 768:],
        out_sum.reshape(512, 256).astype(F32),
        router_sum[:, :2].reshape(EXPERTS, 256).T,
        owned[0],
        owned[1],
        owned[2],
        gain_sum[0],
        gain_sum[1],
    )


def solution(mesh):
    placed = (
        P("dp", "row"),
        P("dp", None),
        P("dp", None),
        P("dp", "row"),
        P("row"),
        P("row", "col"),
        P("row", "col"),
        P("row", "col"),
        P("col", "row"),
        P("row"),
        P("row", None),
        P(None, "row", "col"),
        P(None, "row", "col"),
        P(None, "col", "row"),
    )
    return jax.shard_map(
        on_device,
        mesh=mesh,
        in_specs=placed,
        out_specs=(
            P("dp", "row"),
            P("dp", "row"),
            P("row", "col"),
            P("row", "col"),
            P("row", "col"),
            P("col", "row"),
            P("row", None),
            P("dp", "row", "col"),
            P("dp", "row", "col"),
            P("dp", "col", "row"),
            P("row"),
            P("row"),
        ),
        check_vma=False,
    )
```

```python
import jax
import jax.numpy as jnp
from jax import lax
from jax.experimental import pallas as pl
from jax.experimental.pallas import tpu as pltpu
from jax.sharding import PartitionSpec as P

D = 1024
HEAD_DIM = 64
EXPERTS = 32
CAP = 160
LENGTH = 512

EPSILON = 1e-06
ROPE_BASE = 10000.0
MASKED = -1e30
F32 = jnp.float32
LOW = jnp.bfloat16
MESH = pl.DeviceIdType.MESH

AXES = ("dp", "row", "col")
CORE = ("dp", 1, 2)
X = ("dp", 2, 4)
Y_HI = ("dp", 8, 2)
Z = ("row", 1, 4)
SIDE = ("col", 1, 2)
TEAM = (Z, SIDE)
PLANE = (Z, X)
ALL_DP = (CORE, X, Y_HI)


def size_of(group):
    n = 1
    for _, _, size in group:
        n *= size
    return n


def at(direction):
    axis, weight, size = direction
    return (lax.axis_index(axis) // weight) % size


def member(group):
    index, scale = 0, 1
    for direction in group:
        index = index + at(direction) * scale
        scale *= direction[2]
    return index


def steps_of(group):
    moves = [()]
    for direction in group:
        moves = [m + (k,) for m in moves for k in range(direction[2])]

    def way(move):
        return sum(
            min(k, d[2] - k) * (2 if d == Y_HI else 1) for d, k in zip(group, move)
        )

    return sorted([m for m in moves if any(m)], key=lambda m: -way(m))


def goal(group, move):
    index, scale = 0, 1
    place = {a: lax.axis_index(a) for a in AXES}
    for direction, k in zip(group, move):
        axis, weight, size = direction
        here = at(direction)
        there = (here + k) % size
        place[axis] = place[axis] + weight * (there - here)
        index = index + there * scale
        scale *= size
    return index, place


def expert_of(x, z, c):
    return c * 16 + x * 4 + z


def expert_kernel(
    sent_x, sent_top, sent_p, near0, near1, near2,
    returned, gains_back, scaled0, scaled1, total,
    slots_x, slots_top, slots_p, far0, far1, far2, pulled, gains,
    gate_w, up_w, down_w, rows_in, rows_top, hidden_s, gate_s, up_s, out_s, gate_g, up_g,
    block_s, kept, given, other,
    send, recv, send_back, recv_back, send_core, recv_core, local,
):
    dp, z, c = (lax.axis_index(a) for a in AXES)
    x, core = (dp // 2) % 4, dp % 2
    me = member(PLANE)
    near, far = (near0, near1, near2), (far0, far1, far2)
    barrier = pltpu.get_barrier_semaphore()
    steps = steps_of(PLANE)
    mate = goal((CORE,), (1,))[1]
    for move in steps:
        pl.semaphore_signal(
            barrier, inc=1, device_id=goal(PLANE, move)[1], device_id_type=MESH
        )
    pl.semaphore_signal(barrier, inc=1, device_id=mate, device_id_type=MESH)
    pl.semaphore_wait(barrier, len(steps) + 1)

    def to_mate(source, target, k):
        return pltpu.make_async_remote_copy(
            src_ref=source,
            dst_ref=target,
            send_sem=send_core.at[k],
            recv_sem=recv_core.at[k],
            device_id=mate,
            device_id_type=MESH,
        )

    swaps = [to_mate(near[i], far[i], 8 + i) for i in range(3)]
    for copy in swaps:
        copy.start()
    out_going = []
    for k, (source, target) in enumerate(
        ((sent_x, slots_x), (sent_p, slots_p), (sent_top, slots_top))
    ):
        group = []
        for i, move in enumerate(steps):
            index, place = goal(PLANE, move)
            group.append(
                pltpu.make_async_remote_copy(
                    src_ref=source.at[index],
                    dst_ref=target.at[me],
                    send_sem=send.at[k, i],
                    recv_sem=recv.at[k, i],
                    device_id=place,
                    device_id_type=MESH,
                )
            )
            group[-1].start()
        group.append(pltpu.make_async_copy(source.at[me], target.at[me], local.at[k]))
        group[-1].start()
        out_going.append(group)

    for copy in swaps:
        copy.wait()
    for which in range(3):
        for zs in range(4):
            for cs in range(2):
                for half in range(2):
                    part = jnp.where(
                        core == half, near[which][zs + 4 * cs], far[which][zs + 4 * cs]
                    )
                    if which < 2:
                        (gate_w, up_w)[which][
                            zs * 256 + half * 128 : zs * 256 + half * 128 + 128,
                            cs * 256 : cs * 256 + 256,
                        ] = part
                    else:
                        down_w[
                            cs * 256 + half * 128 : cs * 256 + half * 128 + 128,
                            zs * 256 : zs * 256 + 256,
                        ] = part
    for copy in out_going[0]:
        copy.wait()

    def forward(s, _):
        span = pl.ds(pl.multiple_of(s * CAP, CAP), CAP)
        x_rows = jnp.concatenate([slots_x[4 * s + j] for j in range(4)], axis=1)
        gate_act = dot(x_rows, gate_w[...], ((1,), (0,)))
        up_act = dot(x_rows, up_w[...], ((1,), (0,)))
        hidden = (gate_act * jax.nn.sigmoid(gate_act) * up_act).astype(LOW)
        out_s[span, :] = dot(hidden, down_w[...], ((1,), (0,)))
        rows_in[span, :] = x_rows
        hidden_s[span, :] = hidden
        gate_s[span, :] = gate_act
        up_s[span, :] = up_act
        return 0

    lax.fori_loop(0, 4, forward, 0)
    for copy in out_going[1] + out_going[2]:
        copy.wait()

    def home_of(s, j):
        place = {"dp": dp + 2 * (s - x), "row": j, "col": c}
        return place, 4 * s + j

    def go_back(s, j, from_x, from_g):
        place, index = home_of(s, j)
        return [
            pltpu.make_async_remote_copy(
                src_ref=source,
                dst_ref=target.at[me],
                send_sem=send_back.at[k, index],
                recv_sem=recv_back.at[k, me],
                device_id=place,
                device_id_type=MESH,
            )
            for k, (source, target) in enumerate(((from_x, returned), (from_g, gains_back)))
        ]

    def backward(i, _):
        s = (x + 2 + i) % 4
        span = pl.ds(pl.multiple_of(s * CAP, CAP), CAP)
        top = jnp.concatenate([slots_top[4 * s + j] for j in range(4)], axis=1).astype(F32)
        p = jnp.transpose(slots_p[4 * s])[:CAP, :1]
        gate_act, up_act, out = gate_s[span, :], up_s[span, :], out_s[span, :]
        sig = jax.nn.sigmoid(gate_act)
        slot_grad = (p * top).astype(LOW)
        hidden_grad = dot(slot_grad, down_w[...], ((1,), (1,)))
        grad_gate = (hidden_grad * up_act * sig * (1.0 + gate_act * (1.0 - sig))).astype(LOW)
        grad_up = (hidden_grad * gate_act * sig).astype(LOW)
        pull = dot(grad_gate, gate_w[...], ((1,), (1,)))
        pull = (pull + dot(grad_up, up_w[...], ((1,), (1,)))).astype(LOW)
        gain = jnp.sum(top * out, axis=1, keepdims=True)
        gains[s] = jnp.zeros((8, 256), F32)
        gains[s, :, :CAP] = jnp.transpose(jnp.broadcast_to(gain, (CAP, 128)))[:8]
        for j in range(4):
            pulled[j, s] = pull[:, j * 256 : j * 256 + 256]
        rows_top[span, :] = slot_grad
        gate_g[span, :] = grad_gate
        up_g[span, :] = grad_up
        out = (p * out).astype(LOW)
        for j in range(4):
            scaled0[4 * s + j] = out[: CAP // 2, j * 256 : j * 256 + 256]
            scaled1[4 * s + j] = out[CAP // 2 :, j * 256 : j * 256 + 256]
        for kz in (2, 1, 3, 0):
            j = (z + kz) % 4

            @pl.when((s != x) | (j != z))
            def _(j=j):
                for copy in go_back(s, j, pulled.at[j, s], gains.at[s]):
                    copy.start()

        return 0

    lax.fori_loop(0, 4, backward, 0)
    near_rows = pl.ds(pl.multiple_of(core * 128, 128), 128)
    far_rows = pl.ds(pl.multiple_of((1 - core) * 128, 128), 128)

    def block(m, _):
        wide = pl.ds(pl.multiple_of((m % 4) * 256, 256), 256)
        narrow = pl.ds(pl.multiple_of((m // 4) * 256, 256), 256)
        for which in range(3):
            if which < 2:
                left, right = rows_in[:, wide], (gate_g, up_g)[which][:, narrow]
            else:
                left, right = hidden_s[:, narrow], rows_top[:, wide]
            block_s[...] = dot(left, right, ((0,), (0,)))
            given[m, which] = block_s[far_rows, :].astype(LOW)
            kept[m, which] = block_s[near_rows, :]
        to_mate(given.at[m], other.at[m], m).start()
        return 0

    lax.fori_loop(0, 8, block, 0)
    returned[me] = pulled[z, x]
    gains_back[me] = gains[x]

    def add(m, _):
        to_mate(given.at[m], other.at[m], m).wait()
        total[m] = (kept[m] + other[m].astype(F32)).astype(LOW)
        return 0

    lax.fori_loop(0, 8, add, 0)
    for move in steps:
        index, place = goal(PLANE, move)
        for k, (source, target) in enumerate(
            ((pulled.at[0, 0], returned), (gains.at[0], gains_back))
        ):
            copy = pltpu.make_async_remote_copy(
                src_ref=source,
                dst_ref=target.at[index],
                send_sem=send_back.at[k, index],
                recv_sem=recv_back.at[k, index],
                device_id=place,
                device_id_type=MESH,
            )
            copy.wait_send()
            copy.wait_recv()


def expert_step(number, *operands):
    spec = pl.BlockSpec(memory_space=pltpu.VMEM)
    rows_of = jax.ShapeDtypeStruct((16, CAP, 256), LOW)
    return pl.pallas_call(
        expert_kernel,
        out_shape=[
            rows_of,
            jax.ShapeDtypeStruct((16, 8, 256), F32),
            jax.ShapeDtypeStruct((16, CAP // 2, 256), LOW),
            jax.ShapeDtypeStruct((16, CAP // 2, 256), LOW),
            jax.ShapeDtypeStruct((8, 3, 128, 256), LOW),
        ],
        in_specs=[spec] * 6,
        out_specs=[spec] * 5,
        scratch_shapes=[
            pltpu.VMEM((16, CAP, 256), LOW),
            pltpu.VMEM((16, CAP, 256), LOW),
            pltpu.VMEM((16, 8, 256), F32),
            pltpu.VMEM((8, 128, 256), LOW),
            pltpu.VMEM((8, 128, 256), LOW),
            pltpu.VMEM((8, 128, 256), LOW),
            pltpu.VMEM((4, 4, CAP, 256), LOW),
            pltpu.VMEM((4, 8, 256), F32),
            pltpu.VMEM((D, 512), LOW),
            pltpu.VMEM((D, 512), LOW),
            pltpu.VMEM((512, D), LOW),
            pltpu.VMEM((640, D), LOW),
            pltpu.VMEM((640, D), LOW),
            pltpu.VMEM((640, 512), LOW),
            pltpu.VMEM((640, 512), F32),
            pltpu.VMEM((640, 512), F32),
            pltpu.VMEM((640, D), F32),
            pltpu.VMEM((640, 512), LOW),
            pltpu.VMEM((640, 512), LOW),
            pltpu.VMEM((256, 256), F32),
            pltpu.VMEM((8, 3, 128, 256), F32),
            pltpu.VMEM((8, 3, 128, 256), LOW),
            pltpu.VMEM((8, 3, 128, 256), LOW),
            pltpu.SemaphoreType.DMA((3, 15)),
            pltpu.SemaphoreType.DMA((3, 15)),
            pltpu.SemaphoreType.DMA((2, 16)),
            pltpu.SemaphoreType.DMA((2, 16)),
            pltpu.SemaphoreType.DMA((11,)),
            pltpu.SemaphoreType.DMA((11,)),
            pltpu.SemaphoreType.DMA((3,)),
        ],
        compiler_params=pltpu.CompilerParams(
            collective_id=number, has_side_effects=True, vmem_limit_bytes=60 * 1024 * 1024
        ),
        name="expert",
    )(*operands)


def as_row(column):
    return jnp.transpose(jnp.broadcast_to(column, (512, 128)))[:8]


def as_column(row):
    return jnp.transpose(jnp.broadcast_to(row, (8, 512)))[:, :1]


def launch(send, recv, used, mode, group, source, target):
    me = member(group)
    copies = []
    for move in steps_of(group):
        index, place = goal(group, move)
        copies.append(
            pltpu.make_async_remote_copy(
                src_ref=source(index) if mode == "split" else source,
                dst_ref=target if mode == "swap" else target.at[me],
                send_sem=send.at[used[0]],
                recv_sem=recv.at[used[0]],
                device_id=place,
                device_id_type=MESH,
            )
        )
        used[0] += 1
        copies[-1].start()
    if mode != "swap":
        target[me] = source(me)[...] if mode == "split" else source[...]
    return copies


HEAD_OUT = (
    ((8, 512, 128), LOW),
    ((8, 128, 256), LOW),
    ((8, 128, 256), LOW),
    ((8, 128, 256), LOW),
    ((2, 512, 512), F32),
    ((512, 128), LOW),
    ((512, 128), LOW),
    ((512, 128), LOW),
    ((512, 1), F32),
    ((512, 256), LOW),
    ((512, 256), F32),
    ((512, 1), F32),
    ((512, 256), LOW),
    ((32, 512), F32),
    ((32, 512), F32),
    ((16, 1, 512), jnp.int32),
    ((16, CAP, 256), LOW),
    ((16, CAP, 256), LOW),
    ((16, 8, 256), F32),
)
HEAD_SCRATCH = (
    ((4, 512, 256), LOW),
    ((8, 256), F32),
    ((4, 8, 256), F32),
    ((4, 256, 128), LOW),
    ((4, 256, 128), LOW),
    ((4, 256, 128), LOW),
    ((2, 512, 256), LOW),
    ((8, 512), F32),
    ((4, 8, 512), F32),
    ((32, 512), F32),
    ((4, 32, 512), F32),
    ((32, 512), jnp.int32),
)


def head_kernel(
    x_in, gain1, gain2, w_query, w_key, w_value, w_out, router, ids, segment, cot,
    cos_q, sin_q, cos_kv, sin_kv, w_gate, w_up, w_down,
    attended_all, near0, near1, near2, weights_ref, attended, queries, kv, scale_attn,
    normed_own, resid_ref, scale_ffn, normed_ffn, router_gain, probs_ref, own_rank,
    sent_x, sent_top, sent_p,
    x_all, gain, gain_all, kv_w, q_all, kv_all, out_all, square, squares, logit, logits,
    rank_ref, send, recv, local,
):
    dp, z, c = (lax.axis_index(a) for a in AXES)
    x, core = (dp // 2) % 4, dp % 2
    barrier = pltpu.get_barrier_semaphore()
    team = steps_of(TEAM)
    for move in team:
        pl.semaphore_signal(
            barrier, inc=1, device_id=goal(TEAM, move)[1], device_id_type=MESH
        )
    pl.semaphore_wait(barrier, len(team))
    used = [0]

    def begin(mode, group, source, target):
        return launch(send, recv, used, mode, group, source, target)

    def wait(copies):
        for copy in copies:
            copy.wait()

    def shards(w, target, k):
        half = pl.ds(pl.multiple_of(core * 128, 128), 128)
        me = member(TEAM)
        copies = []
        for move in team:
            place = goal(TEAM, move)[1]
            copies.append(
                pltpu.make_async_remote_copy(
                    src_ref=w.at[expert_of(x, place["row"], place["col"]), half, :],
                    dst_ref=target.at[me],
                    send_sem=send.at[used[0]],
                    recv_sem=recv.at[used[0]],
                    device_id=place,
                    device_id_type=MESH,
                )
            )
            used[0] += 1
        copies.append(
            pltpu.make_async_copy(
                w.at[expert_of(x, z, c), half, :], target.at[me], local.at[k]
            )
        )
        for copy in copies:
            copy.start()
        return copies

    gain[...] = jnp.broadcast_to(gain1[...], (8, 256))
    for j in range(4):
        kv_w[j, :, :64] = w_key[:, j * 64 : j * 64 + 64]
        kv_w[j, :, 64:] = w_value[:, j * 64 : j * 64 + 64]
    first = begin("share", (Z,), x_in, x_all)
    first += begin("share", (Z,), gain, gain_all)

    def columns(j):
        return w_query.at[:, pl.ds(pl.multiple_of(j * 128, 128), 128)]

    parts = begin("split", (Z,), columns, q_all)
    parts += begin("split", (Z,), lambda j: kv_w.at[j], kv_all)
    parts += begin("share", (SIDE,), w_out, out_all)
    bulk = shards(w_gate, near0, 0)

    experts = lax.broadcasted_iota(jnp.int32, (EXPERTS, LENGTH), 0)
    hits = ids[0:1] == experts
    for k in range(1, 8):
        hits = hits | (ids[k : k + 1] == experts)
    at_row = lax.broadcasted_iota(jnp.int32, (LENGTH, LENGTH), 0)
    at_lane = lax.broadcasted_iota(jnp.int32, (LENGTH, LENGTH), 1)
    earlier = jnp.where(at_row < at_lane, 1.0, 0.0).astype(LOW)
    marks = jnp.where(hits, 1.0, 0.0)
    rank = dot(marks.astype(LOW), earlier, ((1,), (0,)))
    rank_ref[...] = jnp.where(hits, rank, -1.0).astype(jnp.int32)
    own = pl.ds(pl.multiple_of(c * 16, 16), 16)
    mine = rank_ref[own, :]
    for e in range(16):
        own_rank[e] = mine[e : e + 1]

    def taken_by(e):
        places = lax.broadcasted_iota(jnp.int32, (CAP, LENGTH), 0)
        return own_rank[e] == places

    def place_top(e, _):
        pick = jnp.where(taken_by(e), 1.0, 0.0).astype(LOW)
        sent_top[e] = dot(pick, cot[...], ((1,), (0,))).astype(LOW)
        return 0

    lax.fori_loop(0, 16, place_top, 0)

    wait(first)
    total = jnp.zeros((LENGTH, 1), F32)
    for j in range(4):
        block = x_all[j].astype(F32)
        total = total + jnp.sum(block * block, axis=1, keepdims=True)
    scale = lax.rsqrt(total / D + EPSILON)
    scale_attn[...] = scale
    residual = x_in[...].astype(F32)
    normed_own[...] = (residual * scale * gain1[...]).astype(LOW)
    wait(parts)
    part_q = jnp.zeros((LENGTH, 128), F32)
    part_kv = jnp.zeros((LENGTH, 128), F32)
    for j in range(4):
        normed = (x_all[j].astype(F32) * scale * gain_all[j, :1]).astype(LOW)
        part_q = part_q + dot(normed, q_all[j], ((1,), (0,)))
        part_kv = part_kv + dot(normed, kv_all[j], ((1,), (0,)))
    low_lane = lax.broadcasted_iota(jnp.int32, (LENGTH, 128), 1) % 64 < 32

    def turn(value, cosine, sine_part):
        other = jnp.where(low_lane, pltpu.roll(value, 96, 1), pltpu.roll(value, 32, 1))
        return (value * cosine - other * sine_part).astype(LOW)

    queries[...] = turn(part_q, cos_q[...], sin_q[...])
    kv[...] = turn(part_kv, cos_kv[...], sin_kv[...])
    keys, values = kv[:, :64], kv[:, 64:]
    segment_row = segment[...].astype(F32)
    allowed = (at_lane <= at_row) & (segment_row == as_column(segment_row))
    for h in range(2):
        span = slice(h * HEAD_DIM, h * HEAD_DIM + HEAD_DIM)
        scores = dot(queries[:, span], keys, ((1,), (1,))) * HEAD_DIM ** (-0.5)
        scores = jnp.where(allowed, scores, MASKED)
        top = jnp.max(scores, axis=1, keepdims=True)
        log_total = top + jnp.log(jnp.sum(jnp.exp(scores - top), axis=1, keepdims=True))
        weights = jnp.exp(scores - log_total)
        weights_ref[h] = weights
        attended[:, span] = dot(weights.astype(LOW), values, ((1,), (0,))).astype(LOW)
    met = begin("share", TEAM, attended, attended_all)
    bulk += shards(w_up, near1, 1)
    wait(met)
    resid = residual
    for m in range(8):
        rows_of = out_all[m // 4, (m % 4) * 128 : (m % 4) * 128 + 128]
        resid = resid + dot(attended_all[m], rows_of, ((1,), (0,)))
    resid_ref[...] = resid
    square[...] = as_row(jnp.sum(resid * resid, axis=1, keepdims=True))
    met = begin("share", (Z,), square, squares)
    bulk += shards(w_down, near2, 2)
    router_gain[...] = lax.dot_general(
        router[...].astype(F32),
        resid * gain2[...],
        (((1,), (1,)), ((), ())),
        precision=lax.Precision.HIGHEST,
        preferred_element_type=F32,
    )
    wait(met)
    row = (squares[0, :1] + squares[1, :1]) + (squares[2, :1] + squares[3, :1])
    scale = as_column(lax.rsqrt(row / D + EPSILON))
    scale_ffn[...] = scale
    normed_ffn[...] = (resid_ref[...] * scale * gain2[...]).astype(LOW)
    logit[...] = dot(router[...], normed_ffn[...], ((1,), (1,)))
    met = begin("share", (Z,), logit, logits)
    wait(met)
    sums = (logits[0] + logits[1]) + (logits[2] + logits[3])
    chosen = jnp.where(hits, sums, MASKED)
    chosen = jnp.exp(chosen - jnp.max(chosen, axis=0, keepdims=True)) * marks
    probs_ref[...] = chosen / jnp.sum(chosen, axis=0, keepdims=True)

    def place_x(e, _):
        taken = taken_by(e)
        pick = jnp.where(taken, 1.0, 0.0).astype(LOW)
        sent_x[e] = dot(pick, normed_ffn[...], ((1,), (0,))).astype(LOW)
        p = probs_ref[pl.ds(c * 16 + e, 1), :]
        p = jnp.sum(jnp.where(taken, p, 0.0), axis=1, keepdims=True)
        sent_p[e] = jnp.zeros((8, 256), F32)
        sent_p[e, :, :CAP] = jnp.transpose(jnp.broadcast_to(p, (CAP, 128)))[:8]
        return 0

    lax.fori_loop(0, 16, place_x, 0)
    wait(bulk)


def head_step(number, *operands):
    spec = pl.BlockSpec(memory_space=pltpu.VMEM)
    far = pl.BlockSpec(memory_space=pl.ANY)
    return pl.pallas_call(
        head_kernel,
        out_shape=[jax.ShapeDtypeStruct(*v) for v in HEAD_OUT],
        in_specs=[spec] * (len(operands) - 3) + [far] * 3,
        out_specs=[spec] * len(HEAD_OUT),
        scratch_shapes=[pltpu.VMEM(*v) for v in HEAD_SCRATCH]
        + [
            pltpu.SemaphoreType.DMA((56,)),
            pltpu.SemaphoreType.DMA((56,)),
            pltpu.SemaphoreType.DMA((3,)),
        ],
        compiler_params=pltpu.CompilerParams(
            collective_id=number, has_side_effects=True, vmem_limit_bytes=60 * 1024 * 1024
        ),
        name="head",
    )(*operands)


TAIL_OUT = (
    ((2, 256, 256), F32),
    ((2, 256, 256), F32),
    ((2, 256, 256), F32),
    ((256, 512), F32),
    ((256, 256), F32),
    ((256, 256), F32),
    ((512, 256), F32),
    ((32, 256), F32),
    ((8, 256), F32),
    ((512, 256), LOW),
    ((512, 256), LOW),
)
TAIL_SCRATCH = (
    ((8, 3, 128, 256), LOW),
    ((16, 32, 256), LOW),
    ((16, 8, 256), F32),
    ((16, 16, 1024), LOW),
    ((16, 8, 256), F32),
    ((512, 256), LOW),
    ((2, 16, 512), F32),
    ((8, 8, 512), F32),
    ((4, 32, 512), F32),
    ((4, 128, 256), LOW),
    ((16, 80, 256), LOW),
    ((16, 80, 256), LOW),
    ((512, 256), LOW),
    ((4, 512, 256), LOW),
    ((512, 256), F32),
    ((512, 256), LOW),
    ((16, 32, 256), LOW),
    ((32, 256), LOW),
    ((16, 8, 256), F32),
    ((16, 8, 256), F32),
    ((8, 256), F32),
    ((512, 256), LOW),
    ((4, 512, 256), LOW),
    ((512, 1024), LOW),
    ((512, 256), LOW),
    ((512, 256), LOW),
    ((8, 512), F32),
    ((8, 8, 512), F32),
    ((256, 1024), LOW),
    ((16, 16, 1024), LOW),
    ((16, 1024), LOW),
    ((8, 256), F32),
    ((512, 256), F32),
    ((512, 256), LOW),
    ((512, 256), LOW),
)
TAIL_SEMS = 224


def tail_kernel(
    home_ref, gain_own_ref, pull_ref, router_gain_ref, w_out_ref, scaled0_ref, scaled1_ref,
    kept_ref, resid_mid_ref, cot_ref, scale_ffn_ref, gain2_ref, probs_ref, router_ref,
    normed_ffn_ref, attended_all_ref, attended_ref, queries_ref, kv_ref, weights_ref,
    cos_q_ref, sin_q_ref, cos_kv_ref, sin_kv_ref, whole_ref, normed_own_ref, x_in_ref,
    scale_attn_ref, gain1_ref, own_rank_ref, grad_gate_ref, grad_up_ref, grad_down_ref,
    grad_query_ref, grad_key_ref, grad_value_ref, grad_out_ref, grad_router_ref,
    gain_sum_ref, block_out_ref, grad_input_ref, owned_ref, out_sum_ref, router_sum_ref,
    joined_sum_ref, gains_ref, home2_ref, gain_pair_ref, pulls_ref, router_pull_ref,
    out_heads_ref, back0_ref, back1_ref, mid_ref, mid_all_ref, grad_mid_ref, g_out_ref,
    out_parts_ref, out_chunk_ref, g_router_ref, router_parts_ref, router_chunk_ref,
    proj_ref, proj_all_ref, flat_ref, gn_ref, gn2_ref, pull2_ref, pulls2_ref, g_joined_ref,
    joined_parts_ref, joined_chunk_ref, gains_own_ref, moe_sum_ref, moe_ref, moe2_ref, send,
    recv,
):
    dp, z, c = (lax.axis_index(a) for a in AXES)
    y_hi, x, core = dp // 8, (dp // 2) % 4, dp % 2
    owner = c * 8 + x * 2 + z // 2
    slot = (z % 2) * 4 + y_hi * 2 + core
    barrier = pltpu.get_barrier_semaphore()
    moves = {}
    for g in (TEAM, PLANE, ALL_DP):
        for move in steps_of(g):
            full = {d: k for d, k in zip(g, move) if k}
            moves[tuple(sorted(full.items()))] = (g, move)
    for g, move in moves.values():
        pl.semaphore_signal(barrier, inc=1, device_id=goal(g, move)[1], device_id_type=MESH)
    sources = []
    for i in range(8):
        place = {
            "dp": ((i // 2) % 2) * 8 + x * 2 + i % 2,
            "row": core * 2 + i // 4,
            "col": y_hi,
        }
        mine = (place["dp"] == dp) & (place["row"] == z) & (place["col"] == c)
        sources.append(mine)

        @pl.when(jnp.logical_not(mine))
        def _(place=place):
            pl.semaphore_signal(barrier, inc=1, device_id=place, device_id_type=MESH)

    @pl.when(owner == dp)
    def _():
        pl.semaphore_wait(barrier, len(moves) + 7)

    @pl.when(owner != dp)
    def _():
        pl.semaphore_wait(barrier, len(moves) + 8)

    used = [0]

    def begin(mode, group, source, target):
        return launch(send, recv, used, mode, group, source, target)

    def wait(copies):
        for copy in copies:
            copy.wait()

    kept, owned = kept_ref, owned_ref
    first_deliver = TAIL_SEMS - 24

    def parcel(which, j, to_slot):
        return pltpu.make_async_remote_copy(
            src_ref=kept.at[j, which],
            dst_ref=owned.at[to_slot, which],
            send_sem=send.at[first_deliver + which * 8 + j],
            recv_sem=recv.at[first_deliver + which * 8 + to_slot],
            device_id={"dp": owner, "row": j % 4, "col": j // 4},
            device_id_type=MESH,
        )

    def own(j):
        return (owner == dp) & (z == j % 4) & (c == j // 4)

    def deliver(which):
        for kz, kc in ((2, 1), (2, 0), (1, 1), (3, 1), (1, 0), (3, 0), (0, 1), (0, 0)):
            j = (z + kz) % 4 + 4 * ((c + kc) % 2)

            @pl.when(own(j))
            def _(j=j):
                owned[slot, which] = kept[j, which]

            @pl.when(jnp.logical_not(own(j)))
            def _(j=j):
                parcel(which, j, slot).start()

    first = begin("swap", (SIDE,), home_ref, home2_ref)
    first += begin("share", (SIDE,), gain_own_ref, gain_pair_ref)
    first += begin("share", TEAM, pull_ref, pulls_ref)
    first += begin("share", (Z,), router_gain_ref, router_pull_ref)
    heads = begin("split", (Z,), lambda j: w_out_ref.at[j], out_heads_ref)
    back0 = begin("split", PLANE, lambda j: scaled0_ref.at[j], back0_ref)
    wait(first)
    home = home_ref[...].astype(F32) + home2_ref[...].astype(F32)
    grad_prob = jnp.concatenate([gain_pair_ref[0], gain_pair_ref[1]], axis=0)
    probs = probs_ref[...]
    inner = jnp.sum(probs * grad_prob, axis=0, keepdims=True)
    grad_logits = (probs * (grad_prob - inner)).astype(LOW)
    router_pull = (router_pull_ref[0] + router_pull_ref[1]) + (
        router_pull_ref[2] + router_pull_ref[3]
    )
    row = jnp.sum(grad_logits.astype(F32) * router_pull, axis=0, keepdims=True)
    for i in range(8):
        row = row + pulls_ref[i, :1]
    project = as_column(row) / D
    grad_normed = home + dot(grad_logits, router_ref[...], ((0,), (0,)))
    resid_mid, scale = resid_mid_ref[...], scale_ffn_ref[...]
    weighted = grad_normed * gain2_ref[...]
    grad_mid = (
        cot_ref[...].astype(F32) + scale * weighted - resid_mid * scale**3 * project
    )
    mid_ref[...] = grad_mid.astype(LOW)
    grad_mid_ref[...] = grad_mid
    gains_own_ref[...] = jnp.zeros((8, 256), F32)
    gains_own_ref[1:2] = jnp.sum(grad_normed * resid_mid * scale, axis=0, keepdims=True)
    middle = begin("share", (Z,), mid_ref, mid_all_ref)
    grad_router = dot(grad_logits, normed_ffn_ref[...], ((1,), (0,)))
    g_router_ref[...] = jnp.zeros((16, 8, 256), F32)
    for j in range(16):
        g_router_ref[j, :2] = grad_router[2 * j : 2 * j + 2]
    for j in range(4):
        g_out_ref[j * 128 : j * 128 + 128] = dot(
            attended_all_ref[4 * c + j], mid_ref[...], ((0,), (0,))
        ).astype(LOW)
    sums = begin(
        "split",
        ALL_DP,
        lambda j: g_out_ref.at[pl.ds(pl.multiple_of(j * 32, 32), 32)],
        out_parts_ref,
    )
    sums += begin("split", ALL_DP, lambda j: g_router_ref.at[j], router_parts_ref)
    deliver(0)

    wait(heads)
    wait(middle)
    grad_att = dot(mid_all_ref[0], out_heads_ref[0], ((1,), (1,)))
    for j in range(1, 4):
        grad_att = grad_att + dot(mid_all_ref[j], out_heads_ref[j], ((1,), (1,)))
    grad_att = grad_att.astype(LOW)
    product = grad_att.astype(F32) * attended_ref[...].astype(F32)
    keys, values = kv_ref[:, :64], kv_ref[:, 64:]
    grad_q = []
    grad_k = jnp.zeros((512, HEAD_DIM), F32)
    grad_v = jnp.zeros((512, HEAD_DIM), F32)
    for h in range(2):
        span = slice(h * HEAD_DIM, h * HEAD_DIM + HEAD_DIM)
        grad_h = grad_att[:, span]
        weights = weights_ref[h]
        delta = jnp.sum(product[:, span], axis=1, keepdims=True)
        grad_weights = dot(grad_h, values, ((1,), (1,)))
        grad_scores = (weights * (grad_weights - delta)).astype(LOW)
        grad_q.append(dot(grad_scores, keys, ((1,), (0,))))
        grad_k = grad_k + dot(grad_scores, queries_ref[:, span], ((0,), (0,)))
        grad_v = grad_v + dot(weights.astype(LOW), grad_h, ((0,), (0,)))
    score_scale = HEAD_DIM ** (-0.5)
    low_lane = lax.broadcasted_iota(jnp.int32, (512, 128), 1) % 64 < 32

    def turn(value, cosine, sine_part):
        other = jnp.where(low_lane, pltpu.roll(value, 96, 1), pltpu.roll(value, 32, 1))
        return (value * cosine + other * sine_part).astype(LOW)

    both = jnp.concatenate(grad_q, axis=1) * score_scale
    proj_ref[:, :128] = turn(both, cos_q_ref[...], sin_q_ref[...])
    both = jnp.concatenate([grad_k * score_scale, grad_v], axis=1)
    proj_ref[:, 128:] = turn(both, cos_kv_ref[...], sin_kv_ref[...])
    projected = begin("share", (Z,), proj_ref, proj_all_ref)
    back1 = begin("split", PLANE, lambda j: scaled1_ref.at[j], back1_ref)

    wait(sums)
    total = out_parts_ref[0].astype(F32)
    routed = router_parts_ref[0]
    for j in range(1, 16):
        total = total + out_parts_ref[j].astype(F32)
        routed = routed + router_parts_ref[j]
    out_chunk_ref[...] = total.astype(LOW)
    router_chunk_ref[...] = routed
    rest = begin("share", ALL_DP, out_chunk_ref, out_sum_ref)
    rest += begin("share", ALL_DP, router_chunk_ref, router_sum_ref)
    moe_sum_ref[...] = jnp.zeros((512, 256), F32)

    def add_half(rows_of, start):
        def one(e, _):
            places = lax.broadcasted_iota(jnp.int32, (80, 512), 0) + start
            taken = (own_rank_ref[e] == places).astype(F32).astype(LOW)
            moe_sum_ref[...] += dot(taken, rows_of[e], ((0,), (0,)))
            return 0

        lax.fori_loop(0, 16, one, 0)

    wait(back0)
    add_half(back0_ref, 0)

    wait(projected)
    for j in range(4):
        flat_ref[:, j * 128 : j * 128 + 128] = proj_all_ref[j, :, :128]
        flat_ref[:, 512 + j * 64 : 576 + j * 64] = proj_all_ref[j, :, 128:192]
        flat_ref[:, 768 + j * 64 : 832 + j * 64] = proj_all_ref[j, :, 192:]
    grad_low = dot(flat_ref[...], whole_ref[...], ((1,), (1,))).astype(LOW)
    residual, gain1 = x_in_ref[...].astype(F32), gain1_ref[...]
    gn_ref[...] = grad_low
    pull = jnp.sum(grad_low.astype(F32) * gain1 * residual, axis=1, keepdims=True)
    pull2_ref[...] = as_row(pull)
    meet = begin("swap", (SIDE,), gn_ref, gn2_ref)
    meet += begin("share", TEAM, pull2_ref, pulls2_ref)
    g_joined_ref[...] = dot(normed_own_ref[...], flat_ref[...], ((0,), (0,))).astype(LOW)
    joined = begin(
        "split",
        ALL_DP,
        lambda j: g_joined_ref.at[pl.ds(pl.multiple_of(j * 16, 16), 16)],
        joined_parts_ref,
    )
    deliver(1)
    wait(back1)
    add_half(back1_ref, 80)
    moe_ref[...] = moe_sum_ref[...].astype(LOW)
    moe = begin("swap", (SIDE,), moe_ref, moe2_ref)
    wait(meet)
    grad_normed = gn_ref[...].astype(F32) + gn2_ref[...].astype(F32)
    row = pulls2_ref[0, :1]
    for i in range(1, 8):
        row = row + pulls2_ref[i, :1]
    project = as_column(row) / D
    weighted = grad_normed * gain1
    scale = scale_attn_ref[...]
    grad_input_ref[...] = (
        grad_mid_ref[...] + scale * weighted - residual * scale**3 * project
    ).astype(LOW)
    gains_own_ref[0:1] = jnp.sum(grad_normed * residual * scale, axis=0, keepdims=True)
    wait(joined)
    total = joined_parts_ref[0].astype(F32)
    for j in range(1, 16):
        total = total + joined_parts_ref[j].astype(F32)
    joined_chunk_ref[...] = total.astype(LOW)
    rest += begin("share", ALL_DP, joined_chunk_ref, joined_sum_ref)
    rest += begin("share", ALL_DP, gains_own_ref, gains_ref)
    deliver(2)
    wait(moe)
    block_out_ref[...] = (
        resid_mid + (moe_ref[...].astype(F32) + moe2_ref[...].astype(F32))
    ).astype(LOW)
    wait(rest)
    for j in range(16):
        part = joined_sum_ref[j].astype(F32)
        at_rows = slice(16 * j, 16 * j + 16)
        grad_query_ref[at_rows] = part[:, :512]
        grad_key_ref[at_rows] = part[:, 512:768]
        grad_value_ref[at_rows] = part[:, 768:]
        grad_out_ref[32 * j : 32 * j + 32] = out_sum_ref[j].astype(F32)
        grad_router_ref[2 * j : 2 * j + 2] = router_sum_ref[j, :2]
    total = gains_ref[0]
    for j in range(1, 16):
        total = total + gains_ref[j]
    gain_sum_ref[...] = total
    for which in range(3):
        for j in range(8):

            @pl.when(jnp.logical_not(own(j)))
            def _(j=j, which=which):
                parcel(which, j, slot).wait_send()

            @pl.when(jnp.logical_not(sources[j]))
            def _(j=j, which=which):
                parcel(which, 0, j).wait_recv()

    for which, target in enumerate((grad_gate_ref, grad_up_ref, grad_down_ref)):
        for i in range(2):
            for half in range(2):
                target[i, half * 128 : half * 128 + 128] = owned[i * 4 + half, which].astype(
                    F32
                ) + owned[i * 4 + 2 + half, which].astype(F32)


def tail_step(number, *operands):
    spec = pl.BlockSpec(memory_space=pltpu.VMEM)
    return pl.pallas_call(
        tail_kernel,
        out_shape=[jax.ShapeDtypeStruct(*v) for v in TAIL_OUT],
        in_specs=[spec] * len(operands),
        out_specs=[spec] * len(TAIL_OUT),
        scratch_shapes=[pltpu.VMEM(*v) for v in TAIL_SCRATCH]
        + [pltpu.SemaphoreType.DMA((TAIL_SEMS,)), pltpu.SemaphoreType.DMA((TAIL_SEMS,))],
        compiler_params=pltpu.CompilerParams(
            collective_id=number, has_side_effects=True, vmem_limit_bytes=60 * 1024 * 1024
        ),
        name="tail",
    )(*operands)


def rope_tables(positions):
    half_dim = HEAD_DIM // 2
    exponent = jnp.arange(half_dim).astype(F32) * (2.0 / HEAD_DIM)
    angles = positions.astype(F32)[:, None] * (ROPE_BASE ** (-exponent))[None, :]
    return (jnp.cos(angles), jnp.sin(angles))


def dot(a, b, dims):
    return lax.dot_general(a, b, (dims, ((), ())), preferred_element_type=F32)


def on_device(
    x_in,
    segments,
    expert_ids,
    cotangent,
    norm_gain1,
    w_query,
    w_key,
    w_value,
    w_out,
    norm_gain2,
    w_router,
    w_gate,
    w_up,
    w_down,
):
    cosine, sine_part = rope_tables(jnp.arange(LENGTH, dtype=jnp.int32))
    idle = jnp.zeros((LENGTH, HEAD_DIM), F32)
    tables = (
        jnp.concatenate([cosine] * 4, axis=1),
        jnp.concatenate([sine_part, -sine_part] * 2, axis=1),
        jnp.concatenate([cosine, cosine, idle + 1.0], axis=1),
        jnp.concatenate([sine_part, -sine_part, idle], axis=1),
    )
    router = w_router.T
    gain1, gain2 = norm_gain1.reshape(1, 256), norm_gain2.reshape(1, 256)
    (
        attended_all,
        near_gate,
        near_up,
        near_down,
        weights,
        attended,
        queries,
        kv,
        scale_attn,
        normed_own,
        resid_mid,
        scale_ffn,
        normed_ffn,
        router_gain,
        probs,
        own_rank,
        sent_x,
        sent_top,
        sent_p,
    ) = head_step(
        2,
        x_in,
        gain1,
        gain2,
        w_query,
        w_key,
        w_value,
        w_out,
        router,
        expert_ids.T,
        segments,
        cotangent,
        *tables,
        w_gate,
        w_up,
        w_down,
    )
    pulled, gain_rows, scaled0, scaled1, kept = expert_step(
        7, sent_x, sent_top, sent_p, near_gate, near_up, near_down
    )

    taken = own_rank == jnp.arange(CAP, dtype=jnp.int32)[None, :, None]
    home = jnp.einsum("est,esd->td", taken.astype(LOW), pulled, preferred_element_type=F32)
    home = home.astype(LOW)
    gain_rows = gain_rows[:, 0, :CAP]
    own_gain = jnp.sum(jnp.where(taken, gain_rows[:, :, None], 0.0), axis=1)
    pull = jnp.sum(home.astype(F32) * norm_gain2 * resid_mid, axis=1)
    (
        grad_gate,
        grad_up,
        grad_down,
        grad_query,
        grad_key,
        grad_value,
        grad_out,
        grad_router,
        gain_sum,
        block_out,
        grad_input,
    ) = tail_step(
        11,
        home,
        own_gain,
        jnp.broadcast_to(pull[None], (8, LENGTH)),
        router_gain,
        w_out.reshape(4, 128, 256),
        scaled0,
        scaled1,
        kept,
        resid_mid,
        cotangent,
        scale_ffn,
        gain2,
        probs,
        router,
        normed_ffn,
        attended_all,
        attended,
        queries,
        kv,
        weights,
        *tables,
        jnp.concatenate([w_query, w_key, w_value], axis=1),
        normed_own,
        x_in,
        scale_attn,
        gain1,
        own_rank,
    )
    return (
        block_out,
        grad_input,
        grad_query,
        grad_key,
        grad_value,
        grad_out,
        grad_router.T,
        grad_gate,
        grad_up,
        grad_down,
        gain_sum[0],
        gain_sum[1],
    )


def solution(mesh):
    placed = (
        P("dp", "row"),
        P("dp", None),
        P("dp", None),
        P("dp", "row"),
        P("row"),
        P("row", "col"),
        P("row", "col"),
        P("row", "col"),
        P("col", "row"),
        P("row"),
        P("row", None),
        P(None, "row", "col"),
        P(None, "row", "col"),
        P(None, "col", "row"),
    )
    return jax.shard_map(
        on_device,
        mesh=mesh,
        in_specs=placed,
        out_specs=(
            P("dp", "row"),
            P("dp", "row"),
            P("row", "col"),
            P("row", "col"),
            P("row", "col"),
            P("col", "row"),
            P("row", None),
            P("dp", "row", "col"),
            P("dp", "row", "col"),
            P("dp", "col", "row"),
            P("row"),
            P("row"),
        ),
        check_vma=False,
    )
```

```python
import jax
import jax.numpy as jnp
from jax import lax
from jax.experimental import pallas as pl
from jax.experimental.pallas import tpu as pltpu
from jax.sharding import PartitionSpec as P

D = 1024
HEAD_DIM = 64
EXPERTS = 32
CAP = 160
LENGTH = 512

EPSILON = 1e-06
ROPE_BASE = 10000.0
MASKED = -1e30
F32 = jnp.float32
LOW = jnp.bfloat16
MESH = pl.DeviceIdType.MESH

AXES = ("dp", "row", "col")
CORE = ("dp", 1, 2)
X = ("dp", 2, 4)
Y_HI = ("dp", 8, 2)
Z = ("row", 1, 4)
SIDE = ("col", 1, 2)
TEAM = (Z, SIDE)
PLANE = (Z, X)
ALL_DP = (CORE, X, Y_HI)


def size_of(group):
    n = 1
    for _, _, size in group:
        n *= size
    return n


def at(direction):
    axis, weight, size = direction
    return (lax.axis_index(axis) // weight) % size


def member(group):
    index, scale = 0, 1
    for direction in group:
        index = index + at(direction) * scale
        scale *= direction[2]
    return index


def steps_of(group):
    moves = [()]
    for direction in group:
        moves = [m + (k,) for m in moves for k in range(direction[2])]

    def way(move):
        return sum(
            min(k, d[2] - k) * (2 if d == Y_HI else 1) for d, k in zip(group, move)
        )

    return sorted([m for m in moves if any(m)], key=lambda m: -way(m))


def goal(group, move):
    index, scale = 0, 1
    place = {a: lax.axis_index(a) for a in AXES}
    for direction, k in zip(group, move):
        axis, weight, size = direction
        here = at(direction)
        there = (here + k) % size
        place[axis] = place[axis] + weight * (there - here)
        index = index + there * scale
        scale *= size
    return index, place


def expert_of(x, z, c):
    return c * 16 + x * 4 + z


def expert_kernel(
    sent_x, sent_top, sent_p, own_rank, near0, near1, near2,
    home, own_gain, scaled0, scaled1, total,
    returned, gains_back, home_sum,
    slots_x, slots_top, slots_p, far0, far1, far2, pulled, gains,
    gate_w, up_w, down_w, rows_in, rows_top, hidden_s, gate_s, up_s, out_s, gate_g, up_g,
    block_s, kept, given, other,
    send, recv, send_back, recv_back, send_core, recv_core, local,
):
    dp, z, c = (lax.axis_index(a) for a in AXES)
    x, core = (dp // 2) % 4, dp % 2
    me = member(PLANE)
    near, far = (near0, near1, near2), (far0, far1, far2)
    barrier = pltpu.get_barrier_semaphore()
    steps = steps_of(PLANE)
    mate = goal((CORE,), (1,))[1]
    for move in steps:
        pl.semaphore_signal(
            barrier, inc=1, device_id=goal(PLANE, move)[1], device_id_type=MESH
        )
    pl.semaphore_signal(barrier, inc=1, device_id=mate, device_id_type=MESH)
    pl.semaphore_wait(barrier, len(steps) + 1)

    def to_mate(source, target, k):
        return pltpu.make_async_remote_copy(
            src_ref=source,
            dst_ref=target,
            send_sem=send_core.at[k],
            recv_sem=recv_core.at[k],
            device_id=mate,
            device_id_type=MESH,
        )

    swaps = [to_mate(near[i], far[i], 8 + i) for i in range(3)]
    for copy in swaps:
        copy.start()
    out_going = []
    for k, (source, target) in enumerate(
        ((sent_x, slots_x), (sent_p, slots_p), (sent_top, slots_top))
    ):
        group = []
        for i, move in enumerate(steps):
            index, place = goal(PLANE, move)
            group.append(
                pltpu.make_async_remote_copy(
                    src_ref=source.at[index],
                    dst_ref=target.at[me],
                    send_sem=send.at[k, i],
                    recv_sem=recv.at[k, i],
                    device_id=place,
                    device_id_type=MESH,
                )
            )
            group[-1].start()
        group.append(pltpu.make_async_copy(source.at[me], target.at[me], local.at[k]))
        group[-1].start()
        out_going.append(group)

    for copy in swaps:
        copy.wait()
    for which in range(3):
        for zs in range(4):
            for cs in range(2):
                for half in range(2):
                    part = jnp.where(
                        core == half, near[which][zs + 4 * cs], far[which][zs + 4 * cs]
                    )
                    if which < 2:
                        (gate_w, up_w)[which][
                            zs * 256 + half * 128 : zs * 256 + half * 128 + 128,
                            cs * 256 : cs * 256 + 256,
                        ] = part
                    else:
                        down_w[
                            cs * 256 + half * 128 : cs * 256 + half * 128 + 128,
                            zs * 256 : zs * 256 + 256,
                        ] = part
    for copy in out_going[0]:
        copy.wait()

    def forward(s, _):
        span = pl.ds(pl.multiple_of(s * CAP, CAP), CAP)
        x_rows = jnp.concatenate([slots_x[4 * s + j] for j in range(4)], axis=1)
        gate_act = dot(x_rows, gate_w[...], ((1,), (0,)))
        up_act = dot(x_rows, up_w[...], ((1,), (0,)))
        hidden = (gate_act * jax.nn.sigmoid(gate_act) * up_act).astype(LOW)
        out_s[span, :] = dot(hidden, down_w[...], ((1,), (0,)))
        rows_in[span, :] = x_rows
        hidden_s[span, :] = hidden
        gate_s[span, :] = gate_act
        up_s[span, :] = up_act
        return 0

    lax.fori_loop(0, 4, forward, 0)
    for copy in out_going[1] + out_going[2]:
        copy.wait()

    def home_of(s, j):
        place = {"dp": dp + 2 * (s - x), "row": j, "col": c}
        return place, 4 * s + j

    def go_back(s, j, from_x, from_g):
        place, index = home_of(s, j)
        return [
            pltpu.make_async_remote_copy(
                src_ref=source,
                dst_ref=target.at[me],
                send_sem=send_back.at[k, index],
                recv_sem=recv_back.at[k, me],
                device_id=place,
                device_id_type=MESH,
            )
            for k, (source, target) in enumerate(((from_x, returned), (from_g, gains_back)))
        ]

    def backward(i, _):
        s = (x + 2 + i) % 4
        span = pl.ds(pl.multiple_of(s * CAP, CAP), CAP)
        top = jnp.concatenate([slots_top[4 * s + j] for j in range(4)], axis=1).astype(F32)
        p = jnp.transpose(slots_p[4 * s])[:CAP, :1]
        gate_act, up_act, out = gate_s[span, :], up_s[span, :], out_s[span, :]
        sig = jax.nn.sigmoid(gate_act)
        slot_grad = (p * top).astype(LOW)
        hidden_grad = dot(slot_grad, down_w[...], ((1,), (1,)))
        grad_gate = (hidden_grad * up_act * sig * (1.0 + gate_act * (1.0 - sig))).astype(LOW)
        grad_up = (hidden_grad * gate_act * sig).astype(LOW)
        pull = dot(grad_gate, gate_w[...], ((1,), (1,)))
        pull = (pull + dot(grad_up, up_w[...], ((1,), (1,)))).astype(LOW)
        gain = jnp.sum(top * out, axis=1, keepdims=True)
        gains[s] = jnp.zeros((8, 256), F32)
        gains[s, :, :CAP] = jnp.transpose(jnp.broadcast_to(gain, (CAP, 128)))[:8]
        for j in range(4):
            pulled[j, s] = pull[:, j * 256 : j * 256 + 256]
        rows_top[span, :] = slot_grad
        gate_g[span, :] = grad_gate
        up_g[span, :] = grad_up
        out = (p * out).astype(LOW)
        for j in range(4):
            scaled0[4 * s + j] = out[: CAP // 2, j * 256 : j * 256 + 256]
            scaled1[4 * s + j] = out[CAP // 2 :, j * 256 : j * 256 + 256]
        for kz in (2, 1, 3, 0):
            j = (z + kz) % 4

            @pl.when((s != x) | (j != z))
            def _(j=j):
                for copy in go_back(s, j, pulled.at[j, s], gains.at[s]):
                    copy.start()

        return 0

    lax.fori_loop(0, 4, backward, 0)
    near_rows = pl.ds(pl.multiple_of(core * 128, 128), 128)
    far_rows = pl.ds(pl.multiple_of((1 - core) * 128, 128), 128)

    def block(m, _):
        wide = pl.ds(pl.multiple_of((m % 4) * 256, 256), 256)
        narrow = pl.ds(pl.multiple_of((m // 4) * 256, 256), 256)
        for which in range(3):
            if which < 2:
                left, right = rows_in[:, wide], (gate_g, up_g)[which][:, narrow]
            else:
                left, right = hidden_s[:, narrow], rows_top[:, wide]
            block_s[...] = dot(left, right, ((0,), (0,)))
            given[m, which] = block_s[far_rows, :].astype(LOW)
            kept[m, which] = block_s[near_rows, :]
        to_mate(given.at[m], other.at[m], m).start()
        return 0

    lax.fori_loop(0, 8, block, 0)
    returned[me] = pulled[z, x]
    gains_back[me] = gains[x]

    def add(m, _):
        to_mate(given.at[m], other.at[m], m).wait()
        total[m] = (kept[m] + other[m].astype(F32)).astype(LOW)
        return 0

    lax.fori_loop(0, 8, add, 0)
    home_sum[...] = jnp.zeros((LENGTH, 256), F32)

    def collect(n, _):
        sx = (x + 6 - n // 4) % 4
        sz = (z + 4 - (2 + 3 * (n % 4)) % 4) % 4
        index = 4 * sx + sz

        @pl.when(index != me)
        def _():
            for copy in go_back(sx, sz, pulled.at[0, 0], gains.at[0]):
                copy.wait_send()
            for k, (source, target) in enumerate(
                ((pulled.at[0, 0], returned), (gains.at[0], gains_back))
            ):
                pltpu.make_async_remote_copy(
                    src_ref=source,
                    dst_ref=target.at[index],
                    send_sem=send_back.at[k, index],
                    recv_sem=recv_back.at[k, index],
                    device_id=home_of(sx, sz)[0],
                    device_id_type=MESH,
                ).wait_recv()

        places = lax.broadcasted_iota(jnp.int32, (CAP, LENGTH), 0)
        taken = own_rank[index] == places
        pick = jnp.where(taken, 1.0, 0.0).astype(LOW)
        home_sum[...] += dot(pick, returned[index], ((0,), (0,)))
        gain = jnp.transpose(gains_back[index])[:CAP, :1]
        own_gain[pl.ds(index, 1), :] = jnp.sum(
            jnp.where(taken, gain, 0.0), axis=0, keepdims=True
        )
        return 0

    lax.fori_loop(0, 16, collect, 0)
    home[...] = home_sum[...].astype(LOW)


def expert_step(number, *operands):
    spec = pl.BlockSpec(memory_space=pltpu.VMEM)
    return pl.pallas_call(
        expert_kernel,
        out_shape=[
            jax.ShapeDtypeStruct((LENGTH, 256), LOW),
            jax.ShapeDtypeStruct((16, LENGTH), F32),
            jax.ShapeDtypeStruct((16, CAP // 2, 256), LOW),
            jax.ShapeDtypeStruct((16, CAP // 2, 256), LOW),
            jax.ShapeDtypeStruct((8, 3, 128, 256), LOW),
        ],
        in_specs=[spec] * 7,
        out_specs=[spec] * 5,
        scratch_shapes=[
            pltpu.VMEM((16, CAP, 256), LOW),
            pltpu.VMEM((16, 8, 256), F32),
            pltpu.VMEM((LENGTH, 256), F32),
            pltpu.VMEM((16, CAP, 256), LOW),
            pltpu.VMEM((16, CAP, 256), LOW),
            pltpu.VMEM((16, 8, 256), F32),
            pltpu.VMEM((8, 128, 256), LOW),
            pltpu.VMEM((8, 128, 256), LOW),
            pltpu.VMEM((8, 128, 256), LOW),
            pltpu.VMEM((4, 4, CAP, 256), LOW),
            pltpu.VMEM((4, 8, 256), F32),
            pltpu.VMEM((D, 512), LOW),
            pltpu.VMEM((D, 512), LOW),
            pltpu.VMEM((512, D), LOW),
            pltpu.VMEM((640, D), LOW),
            pltpu.VMEM((640, D), LOW),
            pltpu.VMEM((640, 512), LOW),
            pltpu.VMEM((640, 512), F32),
            pltpu.VMEM((640, 512), F32),
            pltpu.VMEM((640, D), F32),
            pltpu.VMEM((640, 512), LOW),
            pltpu.VMEM((640, 512), LOW),
            pltpu.VMEM((256, 256), F32),
            pltpu.VMEM((8, 3, 128, 256), F32),
            pltpu.VMEM((8, 3, 128, 256), LOW),
            pltpu.VMEM((8, 3, 128, 256), LOW),
            pltpu.SemaphoreType.DMA((3, 15)),
            pltpu.SemaphoreType.DMA((3, 15)),
            pltpu.SemaphoreType.DMA((2, 16)),
            pltpu.SemaphoreType.DMA((2, 16)),
            pltpu.SemaphoreType.DMA((11,)),
            pltpu.SemaphoreType.DMA((11,)),
            pltpu.SemaphoreType.DMA((3,)),
        ],
        compiler_params=pltpu.CompilerParams(
            collective_id=number, has_side_effects=True, vmem_limit_bytes=60 * 1024 * 1024
        ),
        name="expert",
    )(*operands)


def as_row(column):
    return jnp.transpose(jnp.broadcast_to(column, (512, 128)))[:8]


def as_column(row):
    return jnp.transpose(jnp.broadcast_to(row, (8, 512)))[:, :1]


def launch(send, recv, used, mode, group, source, target):
    me = member(group)
    copies = []
    for move in steps_of(group):
        index, place = goal(group, move)
        copies.append(
            pltpu.make_async_remote_copy(
                src_ref=source(index) if mode == "split" else source,
                dst_ref=target if mode == "swap" else target.at[me],
                send_sem=send.at[used[0]],
                recv_sem=recv.at[used[0]],
                device_id=place,
                device_id_type=MESH,
            )
        )
        used[0] += 1
        copies[-1].start()
    if mode != "swap":
        target[me] = source(me)[...] if mode == "split" else source[...]
    return copies


HEAD_OUT = (
    ((8, 512, 128), LOW),
    ((8, 128, 256), LOW),
    ((8, 128, 256), LOW),
    ((8, 128, 256), LOW),
    ((2, 512, 512), F32),
    ((512, 128), LOW),
    ((512, 128), LOW),
    ((512, 128), LOW),
    ((512, 1), F32),
    ((512, 256), LOW),
    ((512, 256), F32),
    ((512, 1), F32),
    ((512, 256), LOW),
    ((32, 512), F32),
    ((32, 512), F32),
    ((16, 1, 512), jnp.int32),
    ((16, CAP, 256), LOW),
    ((16, CAP, 256), LOW),
    ((16, 8, 256), F32),
)
HEAD_SCRATCH = (
    ((4, 512, 256), LOW),
    ((8, 256), F32),
    ((4, 8, 256), F32),
    ((4, 256, 128), LOW),
    ((4, 256, 128), LOW),
    ((4, 256, 128), LOW),
    ((2, 512, 256), LOW),
    ((8, 512), F32),
    ((4, 8, 512), F32),
    ((32, 512), F32),
    ((4, 32, 512), F32),
    ((32, 512), jnp.int32),
)


def head_kernel(
    x_in, gain1, gain2, w_query, w_key, w_value, w_out, router, ids, segment, cot,
    cos_q, sin_q, cos_kv, sin_kv, w_gate, w_up, w_down,
    attended_all, near0, near1, near2, weights_ref, attended, queries, kv, scale_attn,
    normed_own, resid_ref, scale_ffn, normed_ffn, router_gain, probs_ref, own_rank,
    sent_x, sent_top, sent_p,
    x_all, gain, gain_all, kv_w, q_all, kv_all, out_all, square, squares, logit, logits,
    rank_ref, send, recv, local,
):
    dp, z, c = (lax.axis_index(a) for a in AXES)
    x, core = (dp // 2) % 4, dp % 2
    barrier = pltpu.get_barrier_semaphore()
    team = steps_of(TEAM)
    for move in team:
        pl.semaphore_signal(
            barrier, inc=1, device_id=goal(TEAM, move)[1], device_id_type=MESH
        )
    pl.semaphore_wait(barrier, len(team))
    used = [0]

    def begin(mode, group, source, target):
        return launch(send, recv, used, mode, group, source, target)

    def wait(copies):
        for copy in copies:
            copy.wait()

    def shards(w, target, k):
        half = pl.ds(pl.multiple_of(core * 128, 128), 128)
        me = member(TEAM)
        copies = []
        for move in team:
            place = goal(TEAM, move)[1]
            copies.append(
                pltpu.make_async_remote_copy(
                    src_ref=w.at[expert_of(x, place["row"], place["col"]), half, :],
                    dst_ref=target.at[me],
                    send_sem=send.at[used[0]],
                    recv_sem=recv.at[used[0]],
                    device_id=place,
                    device_id_type=MESH,
                )
            )
            used[0] += 1
        copies.append(
            pltpu.make_async_copy(
                w.at[expert_of(x, z, c), half, :], target.at[me], local.at[k]
            )
        )
        for copy in copies:
            copy.start()
        return copies

    gain[...] = jnp.broadcast_to(gain1[...], (8, 256))
    for j in range(4):
        kv_w[j, :, :64] = w_key[:, j * 64 : j * 64 + 64]
        kv_w[j, :, 64:] = w_value[:, j * 64 : j * 64 + 64]
    first = begin("share", (Z,), x_in, x_all)
    first += begin("share", (Z,), gain, gain_all)

    def columns(j):
        return w_query.at[:, pl.ds(pl.multiple_of(j * 128, 128), 128)]

    parts = begin("split", (Z,), columns, q_all)
    parts += begin("split", (Z,), lambda j: kv_w.at[j], kv_all)
    parts += begin("share", (SIDE,), w_out, out_all)
    bulk = shards(w_gate, near0, 0)

    experts = lax.broadcasted_iota(jnp.int32, (EXPERTS, LENGTH), 0)
    hits = ids[0:1] == experts
    for k in range(1, 8):
        hits = hits | (ids[k : k + 1] == experts)
    at_row = lax.broadcasted_iota(jnp.int32, (LENGTH, LENGTH), 0)
    at_lane = lax.broadcasted_iota(jnp.int32, (LENGTH, LENGTH), 1)
    earlier = jnp.where(at_row < at_lane, 1.0, 0.0).astype(LOW)
    marks = jnp.where(hits, 1.0, 0.0)
    rank = dot(marks.astype(LOW), earlier, ((1,), (0,)))
    rank_ref[...] = jnp.where(hits, rank, -1.0).astype(jnp.int32)
    own = pl.ds(pl.multiple_of(c * 16, 16), 16)
    mine = rank_ref[own, :]
    for e in range(16):
        own_rank[e] = mine[e : e + 1]

    def taken_by(e):
        places = lax.broadcasted_iota(jnp.int32, (CAP, LENGTH), 0)
        return own_rank[e] == places

    def place_top(e, _):
        pick = jnp.where(taken_by(e), 1.0, 0.0).astype(LOW)
        sent_top[e] = dot(pick, cot[...], ((1,), (0,))).astype(LOW)
        return 0

    lax.fori_loop(0, 16, place_top, 0)

    wait(first)
    total = jnp.zeros((LENGTH, 1), F32)
    for j in range(4):
        block = x_all[j].astype(F32)
        total = total + jnp.sum(block * block, axis=1, keepdims=True)
    scale = lax.rsqrt(total / D + EPSILON)
    scale_attn[...] = scale
    residual = x_in[...].astype(F32)
    normed_own[...] = (residual * scale * gain1[...]).astype(LOW)
    wait(parts)
    part_q = jnp.zeros((LENGTH, 128), F32)
    part_kv = jnp.zeros((LENGTH, 128), F32)
    for j in range(4):
        normed = (x_all[j].astype(F32) * scale * gain_all[j, :1]).astype(LOW)
        part_q = part_q + dot(normed, q_all[j], ((1,), (0,)))
        part_kv = part_kv + dot(normed, kv_all[j], ((1,), (0,)))
    low_lane = lax.broadcasted_iota(jnp.int32, (LENGTH, 128), 1) % 64 < 32

    def turn(value, cosine, sine_part):
        other = jnp.where(low_lane, pltpu.roll(value, 96, 1), pltpu.roll(value, 32, 1))
        return (value * cosine - other * sine_part).astype(LOW)

    queries[...] = turn(part_q, cos_q[...], sin_q[...])
    kv[...] = turn(part_kv, cos_kv[...], sin_kv[...])
    keys, values = kv[:, :64], kv[:, 64:]
    segment_row = segment[...].astype(F32)
    allowed = (at_lane <= at_row) & (segment_row == as_column(segment_row))
    for h in range(2):
        span = slice(h * HEAD_DIM, h * HEAD_DIM + HEAD_DIM)
        scores = dot(queries[:, span], keys, ((1,), (1,))) * HEAD_DIM ** (-0.5)
        scores = jnp.where(allowed, scores, MASKED)
        top = jnp.max(scores, axis=1, keepdims=True)
        log_total = top + jnp.log(jnp.sum(jnp.exp(scores - top), axis=1, keepdims=True))
        weights = jnp.exp(scores - log_total)
        weights_ref[h] = weights
        attended[:, span] = dot(weights.astype(LOW), values, ((1,), (0,))).astype(LOW)
    met = begin("share", TEAM, attended, attended_all)
    bulk += shards(w_up, near1, 1)
    wait(met)
    resid = residual
    for m in range(8):
        rows_of = out_all[m // 4, (m % 4) * 128 : (m % 4) * 128 + 128]
        resid = resid + dot(attended_all[m], rows_of, ((1,), (0,)))
    resid_ref[...] = resid
    square[...] = as_row(jnp.sum(resid * resid, axis=1, keepdims=True))
    met = begin("share", (Z,), square, squares)
    bulk += shards(w_down, near2, 2)
    router_gain[...] = lax.dot_general(
        router[...].astype(F32),
        resid * gain2[...],
        (((1,), (1,)), ((), ())),
        precision=lax.Precision.HIGHEST,
        preferred_element_type=F32,
    )
    wait(met)
    row = (squares[0, :1] + squares[1, :1]) + (squares[2, :1] + squares[3, :1])
    scale = as_column(lax.rsqrt(row / D + EPSILON))
    scale_ffn[...] = scale
    normed_ffn[...] = (resid_ref[...] * scale * gain2[...]).astype(LOW)
    logit[...] = dot(router[...], normed_ffn[...], ((1,), (1,)))
    met = begin("share", (Z,), logit, logits)
    wait(met)
    sums = (logits[0] + logits[1]) + (logits[2] + logits[3])
    chosen = jnp.where(hits, sums, MASKED)
    chosen = jnp.exp(chosen - jnp.max(chosen, axis=0, keepdims=True)) * marks
    probs_ref[...] = chosen / jnp.sum(chosen, axis=0, keepdims=True)

    def place_x(e, _):
        taken = taken_by(e)
        pick = jnp.where(taken, 1.0, 0.0).astype(LOW)
        sent_x[e] = dot(pick, normed_ffn[...], ((1,), (0,))).astype(LOW)
        p = probs_ref[pl.ds(c * 16 + e, 1), :]
        p = jnp.sum(jnp.where(taken, p, 0.0), axis=1, keepdims=True)
        sent_p[e] = jnp.zeros((8, 256), F32)
        sent_p[e, :, :CAP] = jnp.transpose(jnp.broadcast_to(p, (CAP, 128)))[:8]
        return 0

    lax.fori_loop(0, 16, place_x, 0)
    wait(bulk)


def head_step(number, *operands):
    spec = pl.BlockSpec(memory_space=pltpu.VMEM)
    far = pl.BlockSpec(memory_space=pl.ANY)
    return pl.pallas_call(
        head_kernel,
        out_shape=[jax.ShapeDtypeStruct(*v) for v in HEAD_OUT],
        in_specs=[spec] * (len(operands) - 3) + [far] * 3,
        out_specs=[spec] * len(HEAD_OUT),
        scratch_shapes=[pltpu.VMEM(*v) for v in HEAD_SCRATCH]
        + [
            pltpu.SemaphoreType.DMA((56,)),
            pltpu.SemaphoreType.DMA((56,)),
            pltpu.SemaphoreType.DMA((3,)),
        ],
        compiler_params=pltpu.CompilerParams(
            collective_id=number, has_side_effects=True, vmem_limit_bytes=60 * 1024 * 1024
        ),
        name="head",
    )(*operands)


TAIL_OUT = (
    ((8, 3, 128, 256), LOW),
    ((16, 32, 256), LOW),
    ((16, 8, 256), F32),
    ((16, 16, 1024), LOW),
    ((16, 8, 256), F32),
    ((512, 256), LOW),
    ((512, 256), LOW),
)
TAIL_SCRATCH = (
    ((8, 512), F32),
    ((512, 256), LOW),
    ((2, 16, 512), F32),
    ((8, 8, 512), F32),
    ((4, 32, 512), F32),
    ((4, 128, 256), LOW),
    ((16, 80, 256), LOW),
    ((16, 80, 256), LOW),
    ((512, 256), LOW),
    ((4, 512, 256), LOW),
    ((512, 256), F32),
    ((512, 256), LOW),
    ((16, 32, 256), LOW),
    ((32, 256), LOW),
    ((16, 8, 256), F32),
    ((16, 8, 256), F32),
    ((8, 256), F32),
    ((512, 256), LOW),
    ((4, 512, 256), LOW),
    ((512, 1024), LOW),
    ((512, 256), LOW),
    ((512, 256), LOW),
    ((8, 512), F32),
    ((8, 8, 512), F32),
    ((256, 1024), LOW),
    ((16, 16, 1024), LOW),
    ((16, 1024), LOW),
    ((8, 256), F32),
    ((512, 256), F32),
    ((512, 256), LOW),
    ((512, 256), LOW),
)
TAIL_SEMS = 224


def tail_kernel(
    home_ref, gain_own_ref, router_gain_ref, w_out_ref, scaled0_ref, scaled1_ref, kept_ref,
    resid_mid_ref, cot_ref, scale_ffn_ref, gain2_ref, probs_ref, router_ref, normed_ffn_ref,
    attended_all_ref, attended_ref, queries_ref, kv_ref, weights_ref, cos_q_ref, sin_q_ref,
    cos_kv_ref, sin_kv_ref, whole_ref, normed_own_ref, x_in_ref, scale_attn_ref, gain1_ref,
    own_rank_ref, owned_ref, out_sum_ref, router_sum_ref, joined_sum_ref, gains_ref,
    block_out_ref, grad_input_ref, pull_ref, home2_ref, gain_pair_ref, pulls_ref,
    router_pull_ref, out_heads_ref, back0_ref, back1_ref, mid_ref, mid_all_ref,
    grad_mid_ref, g_out_ref, out_parts_ref, out_chunk_ref, g_router_ref, router_parts_ref,
    router_chunk_ref, proj_ref, proj_all_ref, flat_ref, gn_ref, gn2_ref, pull2_ref,
    pulls2_ref, g_joined_ref, joined_parts_ref, joined_chunk_ref, gains_own_ref,
    moe_sum_ref, moe_ref, moe2_ref, send, recv,
):
    dp, z, c = (lax.axis_index(a) for a in AXES)
    y_hi, x, core = dp // 8, (dp // 2) % 4, dp % 2
    owner = c * 8 + x * 2 + z // 2
    slot = (z % 2) * 4 + y_hi * 2 + core
    barrier = pltpu.get_barrier_semaphore()
    moves = {}
    for g in (TEAM, PLANE, ALL_DP):
        for move in steps_of(g):
            full = {d: k for d, k in zip(g, move) if k}
            moves[tuple(sorted(full.items()))] = (g, move)
    for g, move in moves.values():
        pl.semaphore_signal(barrier, inc=1, device_id=goal(g, move)[1], device_id_type=MESH)
    sources = []
    for i in range(8):
        place = {
            "dp": ((i // 2) % 2) * 8 + x * 2 + i % 2,
            "row": core * 2 + i // 4,
            "col": y_hi,
        }
        mine = (place["dp"] == dp) & (place["row"] == z) & (place["col"] == c)
        sources.append(mine)

        @pl.when(jnp.logical_not(mine))
        def _(place=place):
            pl.semaphore_signal(barrier, inc=1, device_id=place, device_id_type=MESH)

    @pl.when(owner == dp)
    def _():
        pl.semaphore_wait(barrier, len(moves) + 7)

    @pl.when(owner != dp)
    def _():
        pl.semaphore_wait(barrier, len(moves) + 8)

    used = [0]

    def begin(mode, group, source, target):
        return launch(send, recv, used, mode, group, source, target)

    def wait(copies):
        for copy in copies:
            copy.wait()

    kept, owned = kept_ref, owned_ref
    first_deliver = TAIL_SEMS - 24

    def parcel(which, j, to_slot):
        return pltpu.make_async_remote_copy(
            src_ref=kept.at[j, which],
            dst_ref=owned.at[to_slot, which],
            send_sem=send.at[first_deliver + which * 8 + j],
            recv_sem=recv.at[first_deliver + which * 8 + to_slot],
            device_id={"dp": owner, "row": j % 4, "col": j // 4},
            device_id_type=MESH,
        )

    def own(j):
        return (owner == dp) & (z == j % 4) & (c == j // 4)

    def deliver(which):
        for kz, kc in ((2, 1), (2, 0), (1, 1), (3, 1), (1, 0), (3, 0), (0, 1), (0, 0)):
            j = (z + kz) % 4 + 4 * ((c + kc) % 2)

            @pl.when(own(j))
            def _(j=j):
                owned[slot, which] = kept[j, which]

            @pl.when(jnp.logical_not(own(j)))
            def _(j=j):
                parcel(which, j, slot).start()

    first = begin("swap", (SIDE,), home_ref, home2_ref)
    first += begin("share", (SIDE,), gain_own_ref, gain_pair_ref)
    first += begin("share", (Z,), router_gain_ref, router_pull_ref)
    pull = jnp.sum(
        home_ref[...].astype(F32) * gain2_ref[...] * resid_mid_ref[...], axis=1, keepdims=True
    )
    pull_ref[...] = as_row(pull)
    first += begin("share", TEAM, pull_ref, pulls_ref)
    heads = begin("split", (Z,), lambda j: w_out_ref.at[j], out_heads_ref)
    back0 = begin("split", PLANE, lambda j: scaled0_ref.at[j], back0_ref)
    deliver(0)
    wait(first)
    home = home_ref[...].astype(F32) + home2_ref[...].astype(F32)
    grad_prob = jnp.concatenate([gain_pair_ref[0], gain_pair_ref[1]], axis=0)
    probs = probs_ref[...]
    inner = jnp.sum(probs * grad_prob, axis=0, keepdims=True)
    grad_logits = (probs * (grad_prob - inner)).astype(LOW)
    router_pull = (router_pull_ref[0] + router_pull_ref[1]) + (
        router_pull_ref[2] + router_pull_ref[3]
    )
    row = jnp.sum(grad_logits.astype(F32) * router_pull, axis=0, keepdims=True)
    for i in range(8):
        row = row + pulls_ref[i, :1]
    project = as_column(row) / D
    grad_normed = home + dot(grad_logits, router_ref[...], ((0,), (0,)))
    resid_mid, scale = resid_mid_ref[...], scale_ffn_ref[...]
    weighted = grad_normed * gain2_ref[...]
    grad_mid = (
        cot_ref[...].astype(F32) + scale * weighted - resid_mid * scale**3 * project
    )
    mid_ref[...] = grad_mid.astype(LOW)
    grad_mid_ref[...] = grad_mid
    gains_own_ref[...] = jnp.zeros((8, 256), F32)
    gains_own_ref[1:2] = jnp.sum(grad_normed * resid_mid * scale, axis=0, keepdims=True)
    middle = begin("share", (Z,), mid_ref, mid_all_ref)
    grad_router = dot(grad_logits, normed_ffn_ref[...], ((1,), (0,)))
    g_router_ref[...] = jnp.zeros((16, 8, 256), F32)
    for j in range(16):
        g_router_ref[j, :2] = grad_router[2 * j : 2 * j + 2]
    for j in range(4):
        g_out_ref[j * 128 : j * 128 + 128] = dot(
            attended_all_ref[4 * c + j], mid_ref[...], ((0,), (0,))
        ).astype(LOW)
    sums = begin(
        "split",
        ALL_DP,
        lambda j: g_out_ref.at[pl.ds(pl.multiple_of(j * 32, 32), 32)],
        out_parts_ref,
    )
    sums += begin("split", ALL_DP, lambda j: g_router_ref.at[j], router_parts_ref)
    deliver(1)

    wait(heads)
    wait(middle)
    grad_att = dot(mid_all_ref[0], out_heads_ref[0], ((1,), (1,)))
    for j in range(1, 4):
        grad_att = grad_att + dot(mid_all_ref[j], out_heads_ref[j], ((1,), (1,)))
    grad_att = grad_att.astype(LOW)
    product = grad_att.astype(F32) * attended_ref[...].astype(F32)
    keys, values = kv_ref[:, :64], kv_ref[:, 64:]
    grad_q = []
    grad_k = jnp.zeros((512, HEAD_DIM), F32)
    grad_v = jnp.zeros((512, HEAD_DIM), F32)
    for h in range(2):
        span = slice(h * HEAD_DIM, h * HEAD_DIM + HEAD_DIM)
        grad_h = grad_att[:, span]
        weights = weights_ref[h]
        delta = jnp.sum(product[:, span], axis=1, keepdims=True)
        grad_weights = dot(grad_h, values, ((1,), (1,)))
        grad_scores = (weights * (grad_weights - delta)).astype(LOW)
        grad_q.append(dot(grad_scores, keys, ((1,), (0,))))
        grad_k = grad_k + dot(grad_scores, queries_ref[:, span], ((0,), (0,)))
        grad_v = grad_v + dot(weights.astype(LOW), grad_h, ((0,), (0,)))
    score_scale = HEAD_DIM ** (-0.5)
    low_lane = lax.broadcasted_iota(jnp.int32, (512, 128), 1) % 64 < 32

    def turn(value, cosine, sine_part):
        other = jnp.where(low_lane, pltpu.roll(value, 96, 1), pltpu.roll(value, 32, 1))
        return (value * cosine + other * sine_part).astype(LOW)

    both = jnp.concatenate(grad_q, axis=1) * score_scale
    proj_ref[:, :128] = turn(both, cos_q_ref[...], sin_q_ref[...])
    both = jnp.concatenate([grad_k * score_scale, grad_v], axis=1)
    proj_ref[:, 128:] = turn(both, cos_kv_ref[...], sin_kv_ref[...])
    projected = begin("share", (Z,), proj_ref, proj_all_ref)
    back1 = begin("split", PLANE, lambda j: scaled1_ref.at[j], back1_ref)

    wait(sums)
    total = out_parts_ref[0].astype(F32)
    routed = router_parts_ref[0]
    for j in range(1, 16):
        total = total + out_parts_ref[j].astype(F32)
        routed = routed + router_parts_ref[j]
    out_chunk_ref[...] = total.astype(LOW)
    router_chunk_ref[...] = routed
    rest = begin("share", ALL_DP, out_chunk_ref, out_sum_ref)
    rest += begin("share", ALL_DP, router_chunk_ref, router_sum_ref)
    moe_sum_ref[...] = jnp.zeros((512, 256), F32)

    def add_half(rows_of, start):
        def one(e, _):
            places = lax.broadcasted_iota(jnp.int32, (80, 512), 0) + start
            taken = (own_rank_ref[e] == places).astype(F32).astype(LOW)
            moe_sum_ref[...] += dot(taken, rows_of[e], ((0,), (0,)))
            return 0

        lax.fori_loop(0, 16, one, 0)

    wait(back0)
    add_half(back0_ref, 0)

    wait(projected)
    for j in range(4):
        flat_ref[:, j * 128 : j * 128 + 128] = proj_all_ref[j, :, :128]
        flat_ref[:, 512 + j * 64 : 576 + j * 64] = proj_all_ref[j, :, 128:192]
        flat_ref[:, 768 + j * 64 : 832 + j * 64] = proj_all_ref[j, :, 192:]
    grad_low = dot(flat_ref[...], whole_ref[...], ((1,), (1,))).astype(LOW)
    residual, gain1 = x_in_ref[...].astype(F32), gain1_ref[...]
    gn_ref[...] = grad_low
    pull = jnp.sum(grad_low.astype(F32) * gain1 * residual, axis=1, keepdims=True)
    pull2_ref[...] = as_row(pull)
    meet = begin("swap", (SIDE,), gn_ref, gn2_ref)
    meet += begin("share", TEAM, pull2_ref, pulls2_ref)
    g_joined_ref[...] = dot(normed_own_ref[...], flat_ref[...], ((0,), (0,))).astype(LOW)
    joined = begin(
        "split",
        ALL_DP,
        lambda j: g_joined_ref.at[pl.ds(pl.multiple_of(j * 16, 16), 16)],
        joined_parts_ref,
    )
    deliver(2)
    wait(back1)
    add_half(back1_ref, 80)
    moe_ref[...] = moe_sum_ref[...].astype(LOW)
    moe = begin("swap", (SIDE,), moe_ref, moe2_ref)
    wait(meet)
    grad_normed = gn_ref[...].astype(F32) + gn2_ref[...].astype(F32)
    row = pulls2_ref[0, :1]
    for i in range(1, 8):
        row = row + pulls2_ref[i, :1]
    project = as_column(row) / D
    weighted = grad_normed * gain1
    scale = scale_attn_ref[...]
    grad_input_ref[...] = (
        grad_mid_ref[...] + scale * weighted - residual * scale**3 * project
    ).astype(LOW)
    gains_own_ref[0:1] = jnp.sum(grad_normed * residual * scale, axis=0, keepdims=True)
    wait(joined)
    total = joined_parts_ref[0].astype(F32)
    for j in range(1, 16):
        total = total + joined_parts_ref[j].astype(F32)
    joined_chunk_ref[...] = total.astype(LOW)
    rest += begin("share", ALL_DP, joined_chunk_ref, joined_sum_ref)
    rest += begin("share", ALL_DP, gains_own_ref, gains_ref)
    wait(moe)
    block_out_ref[...] = (
        resid_mid + (moe_ref[...].astype(F32) + moe2_ref[...].astype(F32))
    ).astype(LOW)
    wait(rest)
    for which in range(3):
        for j in range(8):

            @pl.when(jnp.logical_not(own(j)))
            def _(j=j, which=which):
                parcel(which, j, slot).wait_send()

            @pl.when(jnp.logical_not(sources[j]))
            def _(j=j, which=which):
                parcel(which, 0, j).wait_recv()


def finish_kernel(
    owned, out_sum, router_sum, joined_sum, gains, block_in, grad_in,
    grad_gate, grad_up, grad_down, grad_query, grad_key, grad_value, grad_out, grad_router,
    gain_sum, block_out, grad_input,
):
    block_out[...] = block_in[...]
    grad_input[...] = grad_in[...]
    for j in range(16):
        part = joined_sum[j].astype(F32)
        at_rows = slice(16 * j, 16 * j + 16)
        grad_query[at_rows] = part[:, :512]
        grad_key[at_rows] = part[:, 512:768]
        grad_value[at_rows] = part[:, 768:]
        grad_out[32 * j : 32 * j + 32] = out_sum[j].astype(F32)
        grad_router[2 * j : 2 * j + 2] = router_sum[j, :2]
    total = gains[0]
    for j in range(1, 16):
        total = total + gains[j]
    gain_sum[...] = total
    for which, target in enumerate((grad_gate, grad_up, grad_down)):
        for i in range(2):
            for half in range(2):
                target[i, half * 128 : half * 128 + 128] = owned[i * 4 + half, which].astype(
                    F32
                ) + owned[i * 4 + 2 + half, which].astype(F32)


def finish_step(*operands):
    spec = pl.BlockSpec(memory_space=pltpu.VMEM)
    shapes = (
        [((2, 256, 256), F32)] * 3
        + [((256, 512), F32), ((256, 256), F32), ((256, 256), F32), ((512, 256), F32)]
        + [((32, 256), F32), ((8, 256), F32), ((512, 256), LOW), ((512, 256), LOW)]
    )
    return pl.pallas_call(
        finish_kernel,
        out_shape=[jax.ShapeDtypeStruct(*v) for v in shapes],
        in_specs=[spec] * 7,
        out_specs=[spec] * 11,
        compiler_params=pltpu.CompilerParams(vmem_limit_bytes=40 * 1024 * 1024),
        name="finish",
    )(*operands)


def tail_step(number, *operands):
    spec = pl.BlockSpec(memory_space=pltpu.VMEM)
    return pl.pallas_call(
        tail_kernel,
        out_shape=[jax.ShapeDtypeStruct(*v) for v in TAIL_OUT],
        in_specs=[spec] * len(operands),
        out_specs=[spec] * len(TAIL_OUT),
        scratch_shapes=[pltpu.VMEM(*v) for v in TAIL_SCRATCH]
        + [pltpu.SemaphoreType.DMA((TAIL_SEMS,)), pltpu.SemaphoreType.DMA((TAIL_SEMS,))],
        compiler_params=pltpu.CompilerParams(
            collective_id=number, has_side_effects=True, vmem_limit_bytes=60 * 1024 * 1024
        ),
        name="tail",
    )(*operands)


def rope_tables(positions):
    half_dim = HEAD_DIM // 2
    exponent = jnp.arange(half_dim).astype(F32) * (2.0 / HEAD_DIM)
    angles = positions.astype(F32)[:, None] * (ROPE_BASE ** (-exponent))[None, :]
    return (jnp.cos(angles), jnp.sin(angles))


def dot(a, b, dims):
    return lax.dot_general(a, b, (dims, ((), ())), preferred_element_type=F32)


def on_device(
    x_in,
    segments,
    expert_ids,
    cotangent,
    norm_gain1,
    w_query,
    w_key,
    w_value,
    w_out,
    norm_gain2,
    w_router,
    w_gate,
    w_up,
    w_down,
):
    cosine, sine_part = rope_tables(jnp.arange(LENGTH, dtype=jnp.int32))
    idle = jnp.zeros((LENGTH, HEAD_DIM), F32)
    tables = (
        jnp.concatenate([cosine] * 4, axis=1),
        jnp.concatenate([sine_part, -sine_part] * 2, axis=1),
        jnp.concatenate([cosine, cosine, idle + 1.0], axis=1),
        jnp.concatenate([sine_part, -sine_part, idle], axis=1),
    )
    router = w_router.T
    gain1, gain2 = norm_gain1.reshape(1, 256), norm_gain2.reshape(1, 256)
    (
        attended_all,
        near_gate,
        near_up,
        near_down,
        weights,
        attended,
        queries,
        kv,
        scale_attn,
        normed_own,
        resid_mid,
        scale_ffn,
        normed_ffn,
        router_gain,
        probs,
        own_rank,
        sent_x,
        sent_top,
        sent_p,
    ) = head_step(
        2,
        x_in,
        gain1,
        gain2,
        w_query,
        w_key,
        w_value,
        w_out,
        router,
        expert_ids.T,
        segments,
        cotangent,
        *tables,
        w_gate,
        w_up,
        w_down,
    )
    home, own_gain, scaled0, scaled1, kept = expert_step(
        7, sent_x, sent_top, sent_p, own_rank, near_gate, near_up, near_down
    )

    (
        grad_gate,
        grad_up,
        grad_down,
        grad_query,
        grad_key,
        grad_value,
        grad_out,
        grad_router,
        gain_sum,
        block_out,
        grad_input,
    ) = finish_step(*tail_step(
        11,
        home,
        own_gain,
        router_gain,
        w_out.reshape(4, 128, 256),
        scaled0,
        scaled1,
        kept,
        resid_mid,
        cotangent,
        scale_ffn,
        gain2,
        probs,
        router,
        normed_ffn,
        attended_all,
        attended,
        queries,
        kv,
        weights,
        *tables,
        jnp.concatenate([w_query, w_key, w_value], axis=1),
        normed_own,
        x_in,
        scale_attn,
        gain1,
        own_rank,
    ))
    return (
        block_out,
        grad_input,
        grad_query,
        grad_key,
        grad_value,
        grad_out,
        grad_router.T,
        grad_gate,
        grad_up,
        grad_down,
        gain_sum[0],
        gain_sum[1],
    )


def solution(mesh):
    placed = (
        P("dp", "row"),
        P("dp", None),
        P("dp", None),
        P("dp", "row"),
        P("row"),
        P("row", "col"),
        P("row", "col"),
        P("row", "col"),
        P("col", "row"),
        P("row"),
        P("row", None),
        P(None, "row", "col"),
        P(None, "row", "col"),
        P(None, "col", "row"),
    )
    return jax.shard_map(
        on_device,
        mesh=mesh,
        in_specs=placed,
        out_specs=(
            P("dp", "row"),
            P("dp", "row"),
            P("row", "col"),
            P("row", "col"),
            P("row", "col"),
            P("col", "row"),
            P("row", None),
            P("dp", "row", "col"),
            P("dp", "row", "col"),
            P("dp", "col", "row"),
            P("row"),
            P("row"),
        ),
        check_vma=False,
    )
```

```python
import jax
import jax.numpy as jnp
import numpy as np
from jax import lax
from jax.experimental import pallas as pl
from jax.experimental.pallas import tpu as pltpu
from jax.sharding import PartitionSpec as P

D = 1024
HEAD_DIM = 64
EXPERTS = 32
CAP = 160
LENGTH = 512

EPSILON = 1e-06
ROPE_BASE = 10000.0
MASKED = -1e30
F32 = jnp.float32
LOW = jnp.bfloat16
MESH = pl.DeviceIdType.MESH

AXES = ("dp", "row", "col")
CORE = ("dp", 1, 2)
X = ("dp", 2, 4)
Y_HI = ("dp", 8, 2)
Z = ("row", 1, 4)
SIDE = ("col", 1, 2)
TEAM = (Z, SIDE)
PLANE = (Z, X)
ALL_DP = (CORE, X, Y_HI)


def size_of(group):
    n = 1
    for _, _, size in group:
        n *= size
    return n


def at(direction):
    axis, weight, size = direction
    return (lax.axis_index(axis) // weight) % size


def member(group):
    index, scale = 0, 1
    for direction in group:
        index = index + at(direction) * scale
        scale *= direction[2]
    return index


def steps_of(group):
    moves = [()]
    for direction in group:
        moves = [m + (k,) for m in moves for k in range(direction[2])]

    def way(move):
        return sum(
            min(k, d[2] - k) * (2 if d == Y_HI else 1) for d, k in zip(group, move)
        )

    return sorted([m for m in moves if any(m)], key=lambda m: -way(m))


def goal(group, move):
    index, scale = 0, 1
    place = {a: lax.axis_index(a) for a in AXES}
    for direction, k in zip(group, move):
        axis, weight, size = direction
        here = at(direction)
        there = (here + k) % size
        place[axis] = place[axis] + weight * (there - here)
        index = index + there * scale
        scale *= size
    return index, place


def expert_of(x, z, c):
    return c * 16 + x * 4 + z


def expert_kernel(
    sent_x, sent_top, sent_p, own_rank, near0, near1, near2,
    home, own_gain, scaled0, scaled1, total,
    returned, gains_back, home_sum,
    slots_x, slots_top, slots_p, far0, far1, far2, pulled, gains,
    gate_w, up_w, down_w, rows_in, rows_top, hidden_s, gate_s, up_s, out_s, gate_g, up_g,
    block_s, kept, given, other,
    send, recv, send_back, recv_back, send_core, recv_core, local,
):
    dp, z, c = (lax.axis_index(a) for a in AXES)
    x, core = (dp // 2) % 4, dp % 2
    me = member(PLANE)
    near, far = (near0, near1, near2), (far0, far1, far2)
    barrier = pltpu.get_barrier_semaphore()
    steps = steps_of(PLANE)
    mate = goal((CORE,), (1,))[1]
    for move in steps:
        pl.semaphore_signal(
            barrier, inc=1, device_id=goal(PLANE, move)[1], device_id_type=MESH
        )
    pl.semaphore_signal(barrier, inc=1, device_id=mate, device_id_type=MESH)
    pl.semaphore_wait(barrier, len(steps) + 1)

    def to_mate(source, target, k):
        return pltpu.make_async_remote_copy(
            src_ref=source,
            dst_ref=target,
            send_sem=send_core.at[k],
            recv_sem=recv_core.at[k],
            device_id=mate,
            device_id_type=MESH,
        )

    swaps = [to_mate(near[i], far[i], 8 + i) for i in range(3)]
    for copy in swaps:
        copy.start()
    out_going = []
    for k, (source, target) in enumerate(
        ((sent_x, slots_x), (sent_p, slots_p), (sent_top, slots_top))
    ):
        group = []
        for i, move in enumerate(steps):
            index, place = goal(PLANE, move)
            group.append(
                pltpu.make_async_remote_copy(
                    src_ref=source.at[index],
                    dst_ref=target.at[me],
                    send_sem=send.at[k, i],
                    recv_sem=recv.at[k, i],
                    device_id=place,
                    device_id_type=MESH,
                )
            )
            group[-1].start()
        group.append(pltpu.make_async_copy(source.at[me], target.at[me], local.at[k]))
        group[-1].start()
        out_going.append(group)

    for copy in swaps:
        copy.wait()
    for which in range(3):
        for zs in range(4):
            for cs in range(2):
                for half in range(2):
                    part = jnp.where(
                        core == half, near[which][zs + 4 * cs], far[which][zs + 4 * cs]
                    )
                    if which < 2:
                        (gate_w, up_w)[which][
                            zs * 256 + half * 128 : zs * 256 + half * 128 + 128,
                            cs * 256 : cs * 256 + 256,
                        ] = part
                    else:
                        down_w[
                            cs * 256 + half * 128 : cs * 256 + half * 128 + 128,
                            zs * 256 : zs * 256 + 256,
                        ] = part
    for copy in out_going[0]:
        copy.wait()

    def forward(s, _):
        span = pl.ds(pl.multiple_of(s * CAP, CAP), CAP)
        x_rows = jnp.concatenate([slots_x[4 * s + j] for j in range(4)], axis=1)
        gate_act = dot(x_rows, gate_w[...], ((1,), (0,)))
        up_act = dot(x_rows, up_w[...], ((1,), (0,)))
        hidden = (gate_act * jax.nn.sigmoid(gate_act) * up_act).astype(LOW)
        out_s[span, :] = dot(hidden, down_w[...], ((1,), (0,)))
        rows_in[span, :] = x_rows
        hidden_s[span, :] = hidden
        gate_s[span, :] = gate_act
        up_s[span, :] = up_act
        return 0

    lax.fori_loop(0, 4, forward, 0)
    for copy in out_going[1] + out_going[2]:
        copy.wait()

    def home_of(s, j):
        place = {"dp": dp + 2 * (s - x), "row": j, "col": c}
        return place, 4 * s + j

    def go_back(s, j, from_x, from_g):
        place, index = home_of(s, j)
        return [
            pltpu.make_async_remote_copy(
                src_ref=source,
                dst_ref=target.at[me],
                send_sem=send_back.at[k, index],
                recv_sem=recv_back.at[k, me],
                device_id=place,
                device_id_type=MESH,
            )
            for k, (source, target) in enumerate(((from_x, returned), (from_g, gains_back)))
        ]

    def backward(i, _):
        s = (x + 2 + i) % 4
        span = pl.ds(pl.multiple_of(s * CAP, CAP), CAP)
        top = jnp.concatenate([slots_top[4 * s + j] for j in range(4)], axis=1).astype(F32)
        p = jnp.transpose(slots_p[4 * s])[:CAP, :1]
        gate_act, up_act, out = gate_s[span, :], up_s[span, :], out_s[span, :]
        sig = jax.nn.sigmoid(gate_act)
        slot_grad = (p * top).astype(LOW)
        hidden_grad = dot(slot_grad, down_w[...], ((1,), (1,)))
        grad_gate = (hidden_grad * up_act * sig * (1.0 + gate_act * (1.0 - sig))).astype(LOW)
        grad_up = (hidden_grad * gate_act * sig).astype(LOW)
        pull = dot(grad_gate, gate_w[...], ((1,), (1,)))
        pull = (pull + dot(grad_up, up_w[...], ((1,), (1,)))).astype(LOW)
        gain = jnp.sum(top * out, axis=1, keepdims=True)
        gains[s] = jnp.zeros((8, 256), F32)
        gains[s, :, :CAP] = jnp.transpose(jnp.broadcast_to(gain, (CAP, 128)))[:8]
        for j in range(4):
            pulled[j, s] = pull[:, j * 256 : j * 256 + 256]
        rows_top[span, :] = slot_grad
        gate_g[span, :] = grad_gate
        up_g[span, :] = grad_up
        out = (p * out).astype(LOW)
        for j in range(4):
            scaled0[4 * s + j] = out[: CAP // 2, j * 256 : j * 256 + 256]
            scaled1[4 * s + j] = out[CAP // 2 :, j * 256 : j * 256 + 256]
        for kz in (2, 1, 3, 0):
            j = (z + kz) % 4

            @pl.when((s != x) | (j != z))
            def _(j=j):
                for copy in go_back(s, j, pulled.at[j, s], gains.at[s]):
                    copy.start()

        return 0

    lax.fori_loop(0, 4, backward, 0)
    near_rows = pl.ds(pl.multiple_of(core * 128, 128), 128)
    far_rows = pl.ds(pl.multiple_of((1 - core) * 128, 128), 128)

    def block(m, _):
        wide = pl.ds(pl.multiple_of((m % 4) * 256, 256), 256)
        narrow = pl.ds(pl.multiple_of((m // 4) * 256, 256), 256)
        for which in range(3):
            if which < 2:
                left, right = rows_in[:, wide], (gate_g, up_g)[which][:, narrow]
            else:
                left, right = hidden_s[:, narrow], rows_top[:, wide]
            block_s[...] = dot(left, right, ((0,), (0,)))
            given[m, which] = block_s[far_rows, :].astype(LOW)
            kept[m, which] = block_s[near_rows, :]
        to_mate(given.at[m], other.at[m], m).start()
        return 0

    lax.fori_loop(0, 8, block, 0)
    returned[me] = pulled[z, x]
    gains_back[me] = gains[x]

    def add(m, _):
        to_mate(given.at[m], other.at[m], m).wait()
        total[m] = (kept[m] + other[m].astype(F32)).astype(LOW)
        return 0

    lax.fori_loop(0, 8, add, 0)
    home_sum[...] = jnp.zeros((LENGTH, 256), F32)

    def collect(n, _):
        sx = (x + 6 - n // 4) % 4
        sz = (z + 4 - (2 + 3 * (n % 4)) % 4) % 4
        index = 4 * sx + sz

        @pl.when(index != me)
        def _():
            for copy in go_back(sx, sz, pulled.at[0, 0], gains.at[0]):
                copy.wait_send()
            for k, (source, target) in enumerate(
                ((pulled.at[0, 0], returned), (gains.at[0], gains_back))
            ):
                pltpu.make_async_remote_copy(
                    src_ref=source,
                    dst_ref=target.at[index],
                    send_sem=send_back.at[k, index],
                    recv_sem=recv_back.at[k, index],
                    device_id=home_of(sx, sz)[0],
                    device_id_type=MESH,
                ).wait_recv()

        places = lax.broadcasted_iota(jnp.int32, (CAP, LENGTH), 0)
        taken = own_rank[index] == places
        pick = jnp.where(taken, 1.0, 0.0).astype(LOW)
        home_sum[...] += dot(pick, returned[index], ((0,), (0,)))
        gain = jnp.transpose(gains_back[index])[:CAP, :1]
        own_gain[pl.ds(index, 1), :] = jnp.sum(
            jnp.where(taken, gain, 0.0), axis=0, keepdims=True
        )
        return 0

    lax.fori_loop(0, 16, collect, 0)
    home[...] = home_sum[...].astype(LOW)


def expert_step(number, *operands):
    spec = pl.BlockSpec(memory_space=pltpu.VMEM)
    return pl.pallas_call(
        expert_kernel,
        out_shape=[
            jax.ShapeDtypeStruct((LENGTH, 256), LOW),
            jax.ShapeDtypeStruct((16, LENGTH), F32),
            jax.ShapeDtypeStruct((16, CAP // 2, 256), LOW),
            jax.ShapeDtypeStruct((16, CAP // 2, 256), LOW),
            jax.ShapeDtypeStruct((8, 3, 128, 256), LOW),
        ],
        in_specs=[spec] * 7,
        out_specs=[spec] * 5,
        scratch_shapes=[
            pltpu.VMEM((16, CAP, 256), LOW),
            pltpu.VMEM((16, 8, 256), F32),
            pltpu.VMEM((LENGTH, 256), F32),
            pltpu.VMEM((16, CAP, 256), LOW),
            pltpu.VMEM((16, CAP, 256), LOW),
            pltpu.VMEM((16, 8, 256), F32),
            pltpu.VMEM((8, 128, 256), LOW),
            pltpu.VMEM((8, 128, 256), LOW),
            pltpu.VMEM((8, 128, 256), LOW),
            pltpu.VMEM((4, 4, CAP, 256), LOW),
            pltpu.VMEM((4, 8, 256), F32),
            pltpu.VMEM((D, 512), LOW),
            pltpu.VMEM((D, 512), LOW),
            pltpu.VMEM((512, D), LOW),
            pltpu.VMEM((640, D), LOW),
            pltpu.VMEM((640, D), LOW),
            pltpu.VMEM((640, 512), LOW),
            pltpu.VMEM((640, 512), F32),
            pltpu.VMEM((640, 512), F32),
            pltpu.VMEM((640, D), F32),
            pltpu.VMEM((640, 512), LOW),
            pltpu.VMEM((640, 512), LOW),
            pltpu.VMEM((256, 256), F32),
            pltpu.VMEM((8, 3, 128, 256), F32),
            pltpu.VMEM((8, 3, 128, 256), LOW),
            pltpu.VMEM((8, 3, 128, 256), LOW),
            pltpu.SemaphoreType.DMA((3, 15)),
            pltpu.SemaphoreType.DMA((3, 15)),
            pltpu.SemaphoreType.DMA((2, 16)),
            pltpu.SemaphoreType.DMA((2, 16)),
            pltpu.SemaphoreType.DMA((11,)),
            pltpu.SemaphoreType.DMA((11,)),
            pltpu.SemaphoreType.DMA((3,)),
        ],
        compiler_params=pltpu.CompilerParams(
            collective_id=number, has_side_effects=True, vmem_limit_bytes=60 * 1024 * 1024
        ),
        name="expert",
    )(*operands)


def as_row(column):
    return jnp.transpose(jnp.broadcast_to(column, (512, 128)))[:8]


def as_column(row):
    return jnp.transpose(jnp.broadcast_to(row, (8, 512)))[:, :1]


def launch(send, recv, used, mode, group, source, target):
    me = member(group)
    copies = []
    for move in steps_of(group):
        index, place = goal(group, move)
        copies.append(
            pltpu.make_async_remote_copy(
                src_ref=source(index) if mode == "split" else source,
                dst_ref=target if mode == "swap" else target.at[me],
                send_sem=send.at[used[0]],
                recv_sem=recv.at[used[0]],
                device_id=place,
                device_id_type=MESH,
            )
        )
        used[0] += 1
        copies[-1].start()
    if mode != "swap":
        target[me] = source(me)[...] if mode == "split" else source[...]
    return copies


HEAD_OUT = (
    ((8, 512, 128), LOW),
    ((8, 128, 256), LOW),
    ((8, 128, 256), LOW),
    ((8, 128, 256), LOW),
    ((2, 512, 512), F32),
    ((512, 128), LOW),
    ((512, 128), LOW),
    ((512, 128), LOW),
    ((512, 1), F32),
    ((512, 256), LOW),
    ((512, 256), F32),
    ((512, 1), F32),
    ((512, 256), LOW),
    ((32, 512), F32),
    ((32, 512), F32),
    ((16, 1, 512), jnp.int32),
    ((16, CAP, 256), LOW),
    ((16, CAP, 256), LOW),
    ((16, 8, 256), F32),
)
HEAD_SCRATCH = (
    ((4, 512, 256), LOW),
    ((8, 256), F32),
    ((4, 8, 256), F32),
    ((4, 256, 128), LOW),
    ((4, 256, 128), LOW),
    ((4, 256, 128), LOW),
    ((2, 512, 256), LOW),
    ((8, 512), F32),
    ((4, 8, 512), F32),
    ((32, 512), F32),
    ((4, 32, 512), F32),
    ((32, 512), jnp.int32),
)


def head_kernel(
    x_in, gain1, gain2, w_query, w_key, w_value, w_out, router, ids, segment, cot,
    cos_q, sin_q, cos_kv, sin_kv, w_gate, w_up, w_down,
    attended_all, near0, near1, near2, weights_ref, attended, queries, kv, scale_attn,
    normed_own, resid_ref, scale_ffn, normed_ffn, router_gain, probs_ref, own_rank,
    sent_x, sent_top, sent_p,
    x_all, gain, gain_all, kv_w, q_all, kv_all, out_all, square, squares, logit, logits,
    rank_ref, send, recv, local,
):
    dp, z, c = (lax.axis_index(a) for a in AXES)
    x, core = (dp // 2) % 4, dp % 2
    barrier = pltpu.get_barrier_semaphore()
    team = steps_of(TEAM)
    for move in team:
        pl.semaphore_signal(
            barrier, inc=1, device_id=goal(TEAM, move)[1], device_id_type=MESH
        )
    pl.semaphore_wait(barrier, len(team))
    used = [0]

    def begin(mode, group, source, target):
        return launch(send, recv, used, mode, group, source, target)

    def wait(copies):
        for copy in copies:
            copy.wait()

    def shards(w, target, k):
        half = pl.ds(pl.multiple_of(core * 128, 128), 128)
        me = member(TEAM)
        copies = []
        for move in team:
            place = goal(TEAM, move)[1]
            copies.append(
                pltpu.make_async_remote_copy(
                    src_ref=w.at[expert_of(x, place["row"], place["col"]), half, :],
                    dst_ref=target.at[me],
                    send_sem=send.at[used[0]],
                    recv_sem=recv.at[used[0]],
                    device_id=place,
                    device_id_type=MESH,
                )
            )
            used[0] += 1
        copies.append(
            pltpu.make_async_copy(
                w.at[expert_of(x, z, c), half, :], target.at[me], local.at[k]
            )
        )
        for copy in copies:
            copy.start()
        return copies

    gain[...] = jnp.broadcast_to(gain1[...], (8, 256))
    for j in range(4):
        kv_w[j, :, :64] = w_key[:, j * 64 : j * 64 + 64]
        kv_w[j, :, 64:] = w_value[:, j * 64 : j * 64 + 64]
    first = begin("share", (Z,), x_in, x_all)
    first += begin("share", (Z,), gain, gain_all)

    def columns(j):
        return w_query.at[:, pl.ds(pl.multiple_of(j * 128, 128), 128)]

    parts = begin("split", (Z,), columns, q_all)
    parts += begin("split", (Z,), lambda j: kv_w.at[j], kv_all)
    parts += begin("share", (SIDE,), w_out, out_all)
    bulk = shards(w_gate, near0, 0)

    experts = lax.broadcasted_iota(jnp.int32, (EXPERTS, LENGTH), 0)
    hits = ids[0:1] == experts
    for k in range(1, 8):
        hits = hits | (ids[k : k + 1] == experts)
    at_row = lax.broadcasted_iota(jnp.int32, (LENGTH, LENGTH), 0)
    at_lane = lax.broadcasted_iota(jnp.int32, (LENGTH, LENGTH), 1)
    earlier = jnp.where(at_row < at_lane, 1.0, 0.0).astype(LOW)
    marks = jnp.where(hits, 1.0, 0.0)
    rank = dot(marks.astype(LOW), earlier, ((1,), (0,)))
    rank_ref[...] = jnp.where(hits, rank, -1.0).astype(jnp.int32)
    own = pl.ds(pl.multiple_of(c * 16, 16), 16)
    mine = rank_ref[own, :]
    for e in range(16):
        own_rank[e] = mine[e : e + 1]

    def taken_by(e):
        places = lax.broadcasted_iota(jnp.int32, (CAP, LENGTH), 0)
        return own_rank[e] == places

    def place_top(e, _):
        pick = jnp.where(taken_by(e), 1.0, 0.0).astype(LOW)
        sent_top[e] = dot(pick, cot[...], ((1,), (0,))).astype(LOW)
        return 0

    lax.fori_loop(0, 16, place_top, 0)

    wait(first)
    total = jnp.zeros((LENGTH, 1), F32)
    for j in range(4):
        block = x_all[j].astype(F32)
        total = total + jnp.sum(block * block, axis=1, keepdims=True)
    scale = lax.rsqrt(total / D + EPSILON)
    scale_attn[...] = scale
    residual = x_in[...].astype(F32)
    normed_own[...] = (residual * scale * gain1[...]).astype(LOW)
    wait(parts)
    part_q = jnp.zeros((LENGTH, 128), F32)
    part_kv = jnp.zeros((LENGTH, 128), F32)
    for j in range(4):
        normed = (x_all[j].astype(F32) * scale * gain_all[j, :1]).astype(LOW)
        part_q = part_q + dot(normed, q_all[j], ((1,), (0,)))
        part_kv = part_kv + dot(normed, kv_all[j], ((1,), (0,)))
    low_lane = lax.broadcasted_iota(jnp.int32, (LENGTH, 128), 1) % 64 < 32

    def turn(value, cosine, sine_part):
        other = jnp.where(low_lane, pltpu.roll(value, 96, 1), pltpu.roll(value, 32, 1))
        return (value * cosine - other * sine_part).astype(LOW)

    queries[...] = turn(part_q, cos_q[...], sin_q[...])
    kv[...] = turn(part_kv, cos_kv[...], sin_kv[...])
    keys, values = kv[:, :64], kv[:, 64:]
    segment_row = segment[...].astype(F32)
    allowed = (at_lane <= at_row) & (segment_row == as_column(segment_row))
    for h in range(2):
        span = slice(h * HEAD_DIM, h * HEAD_DIM + HEAD_DIM)
        scores = dot(queries[:, span], keys, ((1,), (1,))) * HEAD_DIM ** (-0.5)
        scores = jnp.where(allowed, scores, MASKED)
        top = jnp.max(scores, axis=1, keepdims=True)
        log_total = top + jnp.log(jnp.sum(jnp.exp(scores - top), axis=1, keepdims=True))
        weights = jnp.exp(scores - log_total)
        weights_ref[h] = weights
        attended[:, span] = dot(weights.astype(LOW), values, ((1,), (0,))).astype(LOW)
    met = begin("share", TEAM, attended, attended_all)
    bulk += shards(w_up, near1, 1)
    wait(met)
    resid = residual
    for m in range(8):
        rows_of = out_all[m // 4, (m % 4) * 128 : (m % 4) * 128 + 128]
        resid = resid + dot(attended_all[m], rows_of, ((1,), (0,)))
    resid_ref[...] = resid
    square[...] = as_row(jnp.sum(resid * resid, axis=1, keepdims=True))
    met = begin("share", (Z,), square, squares)
    bulk += shards(w_down, near2, 2)
    router_gain[...] = lax.dot_general(
        router[...].astype(F32),
        resid * gain2[...],
        (((1,), (1,)), ((), ())),
        precision=lax.Precision.HIGHEST,
        preferred_element_type=F32,
    )
    wait(met)
    row = (squares[0, :1] + squares[1, :1]) + (squares[2, :1] + squares[3, :1])
    scale = as_column(lax.rsqrt(row / D + EPSILON))
    scale_ffn[...] = scale
    normed_ffn[...] = (resid_ref[...] * scale * gain2[...]).astype(LOW)
    logit[...] = dot(router[...], normed_ffn[...], ((1,), (1,)))
    met = begin("share", (Z,), logit, logits)
    wait(met)
    sums = (logits[0] + logits[1]) + (logits[2] + logits[3])
    chosen = jnp.where(hits, sums, MASKED)
    chosen = jnp.exp(chosen - jnp.max(chosen, axis=0, keepdims=True)) * marks
    probs_ref[...] = chosen / jnp.sum(chosen, axis=0, keepdims=True)

    def place_x(e, _):
        taken = taken_by(e)
        pick = jnp.where(taken, 1.0, 0.0).astype(LOW)
        sent_x[e] = dot(pick, normed_ffn[...], ((1,), (0,))).astype(LOW)
        p = probs_ref[pl.ds(c * 16 + e, 1), :]
        p = jnp.sum(jnp.where(taken, p, 0.0), axis=1, keepdims=True)
        sent_p[e] = jnp.zeros((8, 256), F32)
        sent_p[e, :, :CAP] = jnp.transpose(jnp.broadcast_to(p, (CAP, 128)))[:8]
        return 0

    lax.fori_loop(0, 16, place_x, 0)
    wait(bulk)


def head_step(number, *operands):
    spec = pl.BlockSpec(memory_space=pltpu.VMEM)
    far = pl.BlockSpec(memory_space=pl.ANY)
    return pl.pallas_call(
        head_kernel,
        out_shape=[jax.ShapeDtypeStruct(*v) for v in HEAD_OUT],
        in_specs=[spec] * (len(operands) - 3) + [far] * 3,
        out_specs=[spec] * len(HEAD_OUT),
        scratch_shapes=[pltpu.VMEM(*v) for v in HEAD_SCRATCH]
        + [
            pltpu.SemaphoreType.DMA((56,)),
            pltpu.SemaphoreType.DMA((56,)),
            pltpu.SemaphoreType.DMA((3,)),
        ],
        compiler_params=pltpu.CompilerParams(
            collective_id=number, has_side_effects=True, vmem_limit_bytes=60 * 1024 * 1024
        ),
        name="head",
    )(*operands)


TAIL_OUT = (
    ((8, 3, 128, 256), LOW),
    ((16, 32, 256), LOW),
    ((16, 8, 256), F32),
    ((16, 16, 1024), LOW),
    ((16, 8, 256), F32),
    ((512, 256), LOW),
    ((512, 256), LOW),
)
TAIL_SCRATCH = (
    ((8, 512), F32),
    ((512, 256), LOW),
    ((2, 16, 512), F32),
    ((8, 8, 512), F32),
    ((4, 32, 512), F32),
    ((4, 128, 256), LOW),
    ((16, 80, 256), LOW),
    ((16, 80, 256), LOW),
    ((512, 256), LOW),
    ((4, 512, 256), LOW),
    ((512, 256), F32),
    ((512, 256), LOW),
    ((16, 32, 256), LOW),
    ((32, 256), LOW),
    ((16, 8, 256), F32),
    ((16, 8, 256), F32),
    ((8, 256), F32),
    ((512, 256), LOW),
    ((4, 512, 256), LOW),
    ((512, 1024), LOW),
    ((512, 256), LOW),
    ((512, 256), LOW),
    ((8, 512), F32),
    ((8, 8, 512), F32),
    ((256, 1024), LOW),
    ((16, 16, 1024), LOW),
    ((16, 1024), LOW),
    ((8, 256), F32),
    ((512, 256), F32),
    ((512, 256), LOW),
    ((512, 256), LOW),
)
TAIL_SEMS = 224


def tail_kernel(
    home_ref, gain_own_ref, router_gain_ref, w_out_ref, scaled0_ref, scaled1_ref, kept_ref,
    resid_mid_ref, cot_ref, scale_ffn_ref, gain2_ref, probs_ref, router_ref, normed_ffn_ref,
    attended_all_ref, attended_ref, queries_ref, kv_ref, weights_ref, cos_q_ref, sin_q_ref,
    cos_kv_ref, sin_kv_ref, whole_ref, normed_own_ref, x_in_ref, scale_attn_ref, gain1_ref,
    own_rank_ref, owned_ref, out_sum_ref, router_sum_ref, joined_sum_ref, gains_ref,
    block_out_ref, grad_input_ref, pull_ref, home2_ref, gain_pair_ref, pulls_ref,
    router_pull_ref, out_heads_ref, back0_ref, back1_ref, mid_ref, mid_all_ref,
    grad_mid_ref, g_out_ref, out_parts_ref, out_chunk_ref, g_router_ref, router_parts_ref,
    router_chunk_ref, proj_ref, proj_all_ref, flat_ref, gn_ref, gn2_ref, pull2_ref,
    pulls2_ref, g_joined_ref, joined_parts_ref, joined_chunk_ref, gains_own_ref,
    moe_sum_ref, moe_ref, moe2_ref, send, recv,
):
    dp, z, c = (lax.axis_index(a) for a in AXES)
    y_hi, x, core = dp // 8, (dp // 2) % 4, dp % 2
    owner = c * 8 + x * 2 + z // 2
    slot = (z % 2) * 4 + y_hi * 2 + core
    barrier = pltpu.get_barrier_semaphore()
    moves = {}
    for g in (TEAM, PLANE, ALL_DP):
        for move in steps_of(g):
            full = {d: k for d, k in zip(g, move) if k}
            moves[tuple(sorted(full.items()))] = (g, move)
    for g, move in moves.values():
        pl.semaphore_signal(barrier, inc=1, device_id=goal(g, move)[1], device_id_type=MESH)
    sources = []
    for i in range(8):
        place = {
            "dp": ((i // 2) % 2) * 8 + x * 2 + i % 2,
            "row": core * 2 + i // 4,
            "col": y_hi,
        }
        mine = (place["dp"] == dp) & (place["row"] == z) & (place["col"] == c)
        sources.append(mine)

        @pl.when(jnp.logical_not(mine))
        def _(place=place):
            pl.semaphore_signal(barrier, inc=1, device_id=place, device_id_type=MESH)

    @pl.when(owner == dp)
    def _():
        pl.semaphore_wait(barrier, len(moves) + 7)

    @pl.when(owner != dp)
    def _():
        pl.semaphore_wait(barrier, len(moves) + 8)

    used = [0]

    def begin(mode, group, source, target):
        return launch(send, recv, used, mode, group, source, target)

    def wait(copies):
        for copy in copies:
            copy.wait()

    kept, owned = kept_ref, owned_ref
    first_deliver = TAIL_SEMS - 24

    def parcel(which, j, to_slot):
        return pltpu.make_async_remote_copy(
            src_ref=kept.at[j, which],
            dst_ref=owned.at[to_slot, which],
            send_sem=send.at[first_deliver + which * 8 + j],
            recv_sem=recv.at[first_deliver + which * 8 + to_slot],
            device_id={"dp": owner, "row": j % 4, "col": j // 4},
            device_id_type=MESH,
        )

    def own(j):
        return (owner == dp) & (z == j % 4) & (c == j // 4)

    def deliver(which):
        for kz, kc in ((2, 1), (2, 0), (1, 1), (3, 1), (1, 0), (3, 0), (0, 1), (0, 0)):
            j = (z + kz) % 4 + 4 * ((c + kc) % 2)

            @pl.when(own(j))
            def _(j=j):
                owned[slot, which] = kept[j, which]

            @pl.when(jnp.logical_not(own(j)))
            def _(j=j):
                parcel(which, j, slot).start()

    first = begin("swap", (SIDE,), home_ref, home2_ref)
    first += begin("share", (SIDE,), gain_own_ref, gain_pair_ref)
    first += begin("share", (Z,), router_gain_ref, router_pull_ref)
    pull = jnp.sum(
        home_ref[...].astype(F32) * gain2_ref[...] * resid_mid_ref[...], axis=1, keepdims=True
    )
    pull_ref[...] = as_row(pull)
    first += begin("share", TEAM, pull_ref, pulls_ref)
    heads = begin("split", (Z,), lambda j: w_out_ref.at[j], out_heads_ref)
    back0 = begin("split", PLANE, lambda j: scaled0_ref.at[j], back0_ref)
    deliver(0)
    wait(first)
    home = home_ref[...].astype(F32) + home2_ref[...].astype(F32)
    grad_prob = jnp.concatenate([gain_pair_ref[0], gain_pair_ref[1]], axis=0)
    probs = probs_ref[...]
    inner = jnp.sum(probs * grad_prob, axis=0, keepdims=True)
    grad_logits = (probs * (grad_prob - inner)).astype(LOW)
    router_pull = (router_pull_ref[0] + router_pull_ref[1]) + (
        router_pull_ref[2] + router_pull_ref[3]
    )
    row = jnp.sum(grad_logits.astype(F32) * router_pull, axis=0, keepdims=True)
    for i in range(8):
        row = row + pulls_ref[i, :1]
    project = as_column(row) / D
    grad_normed = home + dot(grad_logits, router_ref[...], ((0,), (0,)))
    resid_mid, scale = resid_mid_ref[...], scale_ffn_ref[...]
    weighted = grad_normed * gain2_ref[...]
    grad_mid = (
        cot_ref[...].astype(F32) + scale * weighted - resid_mid * scale**3 * project
    )
    mid_ref[...] = grad_mid.astype(LOW)
    grad_mid_ref[...] = grad_mid
    gains_own_ref[...] = jnp.zeros((8, 256), F32)
    gains_own_ref[1:2] = jnp.sum(grad_normed * resid_mid * scale, axis=0, keepdims=True)
    middle = begin("share", (Z,), mid_ref, mid_all_ref)
    grad_router = dot(grad_logits, normed_ffn_ref[...], ((1,), (0,)))
    g_router_ref[...] = jnp.zeros((16, 8, 256), F32)
    for j in range(16):
        g_router_ref[j, :2] = grad_router[2 * j : 2 * j + 2]
    for j in range(4):
        g_out_ref[j * 128 : j * 128 + 128] = dot(
            attended_all_ref[4 * c + j], mid_ref[...], ((0,), (0,))
        ).astype(LOW)
    sums = begin(
        "split",
        ALL_DP,
        lambda j: g_out_ref.at[pl.ds(pl.multiple_of(j * 32, 32), 32)],
        out_parts_ref,
    )
    sums += begin("split", ALL_DP, lambda j: g_router_ref.at[j], router_parts_ref)
    deliver(1)

    wait(heads)
    wait(middle)
    grad_att = dot(mid_all_ref[0], out_heads_ref[0], ((1,), (1,)))
    for j in range(1, 4):
        grad_att = grad_att + dot(mid_all_ref[j], out_heads_ref[j], ((1,), (1,)))
    grad_att = grad_att.astype(LOW)
    product = grad_att.astype(F32) * attended_ref[...].astype(F32)
    keys, values = kv_ref[:, :64], kv_ref[:, 64:]
    grad_q = []
    grad_k = jnp.zeros((512, HEAD_DIM), F32)
    grad_v = jnp.zeros((512, HEAD_DIM), F32)
    for h in range(2):
        span = slice(h * HEAD_DIM, h * HEAD_DIM + HEAD_DIM)
        grad_h = grad_att[:, span]
        weights = weights_ref[h]
        delta = jnp.sum(product[:, span], axis=1, keepdims=True)
        grad_weights = dot(grad_h, values, ((1,), (1,)))
        grad_scores = (weights * (grad_weights - delta)).astype(LOW)
        grad_q.append(dot(grad_scores, keys, ((1,), (0,))))
        grad_k = grad_k + dot(grad_scores, queries_ref[:, span], ((0,), (0,)))
        grad_v = grad_v + dot(weights.astype(LOW), grad_h, ((0,), (0,)))
    score_scale = HEAD_DIM ** (-0.5)
    low_lane = lax.broadcasted_iota(jnp.int32, (512, 128), 1) % 64 < 32

    def turn(value, cosine, sine_part):
        other = jnp.where(low_lane, pltpu.roll(value, 96, 1), pltpu.roll(value, 32, 1))
        return (value * cosine + other * sine_part).astype(LOW)

    both = jnp.concatenate(grad_q, axis=1) * score_scale
    proj_ref[:, :128] = turn(both, cos_q_ref[...], sin_q_ref[...])
    both = jnp.concatenate([grad_k * score_scale, grad_v], axis=1)
    proj_ref[:, 128:] = turn(both, cos_kv_ref[...], sin_kv_ref[...])
    projected = begin("share", (Z,), proj_ref, proj_all_ref)
    back1 = begin("split", PLANE, lambda j: scaled1_ref.at[j], back1_ref)

    wait(sums)
    total = out_parts_ref[0].astype(F32)
    routed = router_parts_ref[0]
    for j in range(1, 16):
        total = total + out_parts_ref[j].astype(F32)
        routed = routed + router_parts_ref[j]
    out_chunk_ref[...] = total.astype(LOW)
    router_chunk_ref[...] = routed
    rest = begin("share", ALL_DP, out_chunk_ref, out_sum_ref)
    rest += begin("share", ALL_DP, router_chunk_ref, router_sum_ref)
    moe_sum_ref[...] = jnp.zeros((512, 256), F32)

    def add_half(rows_of, start):
        def one(e, _):
            places = lax.broadcasted_iota(jnp.int32, (80, 512), 0) + start
            taken = (own_rank_ref[e] == places).astype(F32).astype(LOW)
            moe_sum_ref[...] += dot(taken, rows_of[e], ((0,), (0,)))
            return 0

        lax.fori_loop(0, 16, one, 0)

    wait(back0)
    add_half(back0_ref, 0)

    wait(projected)
    for j in range(4):
        flat_ref[:, j * 128 : j * 128 + 128] = proj_all_ref[j, :, :128]
        flat_ref[:, 512 + j * 64 : 576 + j * 64] = proj_all_ref[j, :, 128:192]
        flat_ref[:, 768 + j * 64 : 832 + j * 64] = proj_all_ref[j, :, 192:]
    grad_low = dot(flat_ref[...], whole_ref[...], ((1,), (1,))).astype(LOW)
    residual, gain1 = x_in_ref[...].astype(F32), gain1_ref[...]
    gn_ref[...] = grad_low
    pull = jnp.sum(grad_low.astype(F32) * gain1 * residual, axis=1, keepdims=True)
    pull2_ref[...] = as_row(pull)
    meet = begin("swap", (SIDE,), gn_ref, gn2_ref)
    meet += begin("share", TEAM, pull2_ref, pulls2_ref)
    g_joined_ref[...] = dot(normed_own_ref[...], flat_ref[...], ((0,), (0,))).astype(LOW)
    joined = begin(
        "split",
        ALL_DP,
        lambda j: g_joined_ref.at[pl.ds(pl.multiple_of(j * 16, 16), 16)],
        joined_parts_ref,
    )
    deliver(2)
    wait(back1)
    add_half(back1_ref, 80)
    moe_ref[...] = moe_sum_ref[...].astype(LOW)
    moe = begin("swap", (SIDE,), moe_ref, moe2_ref)
    wait(meet)
    grad_normed = gn_ref[...].astype(F32) + gn2_ref[...].astype(F32)
    row = pulls2_ref[0, :1]
    for i in range(1, 8):
        row = row + pulls2_ref[i, :1]
    project = as_column(row) / D
    weighted = grad_normed * gain1
    scale = scale_attn_ref[...]
    grad_input_ref[...] = (
        grad_mid_ref[...] + scale * weighted - residual * scale**3 * project
    ).astype(LOW)
    gains_own_ref[0:1] = jnp.sum(grad_normed * residual * scale, axis=0, keepdims=True)
    wait(joined)
    total = joined_parts_ref[0].astype(F32)
    for j in range(1, 16):
        total = total + joined_parts_ref[j].astype(F32)
    joined_chunk_ref[...] = total.astype(LOW)
    rest += begin("share", ALL_DP, joined_chunk_ref, joined_sum_ref)
    rest += begin("share", ALL_DP, gains_own_ref, gains_ref)
    wait(moe)
    block_out_ref[...] = (
        resid_mid + (moe_ref[...].astype(F32) + moe2_ref[...].astype(F32))
    ).astype(LOW)
    wait(rest)
    for which in range(3):
        for j in range(8):

            @pl.when(jnp.logical_not(own(j)))
            def _(j=j, which=which):
                parcel(which, j, slot).wait_send()

            @pl.when(jnp.logical_not(sources[j]))
            def _(j=j, which=which):
                parcel(which, 0, j).wait_recv()


def finish_kernel(
    owned, out_sum, router_sum, joined_sum, gains, block_in, grad_in,
    grad_gate, grad_up, grad_down, grad_query, grad_key, grad_value, grad_out, grad_router,
    gain_sum, block_out, grad_input,
):
    block_out[...] = block_in[...]
    grad_input[...] = grad_in[...]
    for j in range(16):
        part = joined_sum[j].astype(F32)
        at_rows = slice(16 * j, 16 * j + 16)
        grad_query[at_rows] = part[:, :512]
        grad_key[at_rows] = part[:, 512:768]
        grad_value[at_rows] = part[:, 768:]
        grad_out[32 * j : 32 * j + 32] = out_sum[j].astype(F32)
        grad_router[2 * j : 2 * j + 2] = router_sum[j, :2]
    total = gains[0]
    for j in range(1, 16):
        total = total + gains[j]
    gain_sum[...] = total
    for which, target in enumerate((grad_gate, grad_up, grad_down)):
        for i in range(2):
            for half in range(2):
                target[i, half * 128 : half * 128 + 128] = owned[i * 4 + half, which].astype(
                    F32
                ) + owned[i * 4 + 2 + half, which].astype(F32)


def finish_step(*operands):
    spec = pl.BlockSpec(memory_space=pltpu.VMEM)
    shapes = (
        [((2, 256, 256), F32)] * 3
        + [((256, 512), F32), ((256, 256), F32), ((256, 256), F32), ((512, 256), F32)]
        + [((32, 256), F32), ((8, 256), F32), ((512, 256), LOW), ((512, 256), LOW)]
    )
    return pl.pallas_call(
        finish_kernel,
        out_shape=[jax.ShapeDtypeStruct(*v) for v in shapes],
        in_specs=[spec] * 7,
        out_specs=[spec] * 11,
        compiler_params=pltpu.CompilerParams(vmem_limit_bytes=63 * 1024 * 1024),
        name="finish",
    )(*operands)


def tail_step(number, *operands):
    spec = pl.BlockSpec(memory_space=pltpu.VMEM)
    return pl.pallas_call(
        tail_kernel,
        out_shape=[jax.ShapeDtypeStruct(*v) for v in TAIL_OUT],
        in_specs=[spec] * len(operands),
        out_specs=[spec] * len(TAIL_OUT),
        scratch_shapes=[pltpu.VMEM(*v) for v in TAIL_SCRATCH]
        + [pltpu.SemaphoreType.DMA((TAIL_SEMS,)), pltpu.SemaphoreType.DMA((TAIL_SEMS,))],
        compiler_params=pltpu.CompilerParams(
            collective_id=number, has_side_effects=True, vmem_limit_bytes=60 * 1024 * 1024
        ),
        name="tail",
    )(*operands)


def rope_tables():
    half_dim = HEAD_DIM // 2
    exponent = np.arange(half_dim).astype(np.float32) * np.float32(2.0 / HEAD_DIM)
    rates = np.power(np.float32(ROPE_BASE), -exponent).astype(np.float32)
    angles = np.arange(LENGTH).astype(np.float32)[:, None] * rates[None, :]
    cosine = np.cos(angles.astype(np.float64)).astype(np.float32)
    sine_part = np.sin(angles.astype(np.float64)).astype(np.float32)
    idle = np.zeros((LENGTH, HEAD_DIM), np.float32)
    return (
        np.concatenate([cosine] * 4, axis=1),
        np.concatenate([sine_part, -sine_part] * 2, axis=1),
        np.concatenate([cosine, cosine, idle + 1.0], axis=1),
        np.concatenate([sine_part, -sine_part, idle], axis=1),
    )


def dot(a, b, dims):
    return lax.dot_general(a, b, (dims, ((), ())), preferred_element_type=F32)


def on_device(
    x_in,
    segments,
    expert_ids,
    cotangent,
    norm_gain1,
    w_query,
    w_key,
    w_value,
    w_out,
    norm_gain2,
    w_router,
    w_gate,
    w_up,
    w_down,
):
    tables = [jnp.asarray(t, F32) for t in rope_tables()]
    router = w_router.T
    gain1, gain2 = norm_gain1.reshape(1, 256), norm_gain2.reshape(1, 256)
    (
        attended_all,
        near_gate,
        near_up,
        near_down,
        weights,
        attended,
        queries,
        kv,
        scale_attn,
        normed_own,
        resid_mid,
        scale_ffn,
        normed_ffn,
        router_gain,
        probs,
        own_rank,
        sent_x,
        sent_top,
        sent_p,
    ) = head_step(
        2,
        x_in,
        gain1,
        gain2,
        w_query,
        w_key,
        w_value,
        w_out,
        router,
        expert_ids.T,
        segments,
        cotangent,
        *tables,
        w_gate,
        w_up,
        w_down,
    )
    home, own_gain, scaled0, scaled1, kept = expert_step(
        7, sent_x, sent_top, sent_p, own_rank, near_gate, near_up, near_down
    )

    (
        grad_gate,
        grad_up,
        grad_down,
        grad_query,
        grad_key,
        grad_value,
        grad_out,
        grad_router,
        gain_sum,
        block_out,
        grad_input,
    ) = finish_step(*tail_step(
        11,
        home,
        own_gain,
        router_gain,
        w_out.reshape(4, 128, 256),
        scaled0,
        scaled1,
        kept,
        resid_mid,
        cotangent,
        scale_ffn,
        gain2,
        probs,
        router,
        normed_ffn,
        attended_all,
        attended,
        queries,
        kv,
        weights,
        *tables,
        jnp.concatenate([w_query, w_key, w_value], axis=1),
        normed_own,
        x_in,
        scale_attn,
        gain1,
        own_rank,
    ))
    return (
        block_out,
        grad_input,
        grad_query,
        grad_key,
        grad_value,
        grad_out,
        grad_router.T,
        grad_gate,
        grad_up,
        grad_down,
        gain_sum[0],
        gain_sum[1],
    )


def solution(mesh):
    placed = (
        P("dp", "row"),
        P("dp", None),
        P("dp", None),
        P("dp", "row"),
        P("row"),
        P("row", "col"),
        P("row", "col"),
        P("row", "col"),
        P("col", "row"),
        P("row"),
        P("row", None),
        P(None, "row", "col"),
        P(None, "row", "col"),
        P(None, "col", "row"),
    )
    return jax.shard_map(
        on_device,
        mesh=mesh,
        in_specs=placed,
        out_specs=(
            P("dp", "row"),
            P("dp", "row"),
            P("row", "col"),
            P("row", "col"),
            P("row", "col"),
            P("col", "row"),
            P("row", None),
            P("dp", "row", "col"),
            P("dp", "row", "col"),
            P("dp", "col", "row"),
            P("row"),
            P("row"),
        ),
        check_vma=False,
    )
```

```python
import jax
import jax.numpy as jnp
import numpy as np
from jax import lax
from jax.experimental import pallas as pl
from jax.experimental.pallas import tpu as pltpu
from jax.sharding import PartitionSpec as P

D = 1024
HEAD_DIM = 64
EXPERTS = 32
CAP = 160
LENGTH = 512

EPSILON = 1e-06
ROPE_BASE = 10000.0
MASKED = -1e30
F32 = jnp.float32
LOW = jnp.bfloat16
MESH = pl.DeviceIdType.MESH

AXES = ("dp", "row", "col")
CORE = ("dp", 1, 2)
X = ("dp", 2, 4)
Y_HI = ("dp", 8, 2)
Z = ("row", 1, 4)
SIDE = ("col", 1, 2)
TEAM = (Z, SIDE)
PLANE = (Z, X)
ALL_DP = (CORE, X, Y_HI)


def size_of(group):
    n = 1
    for _, _, size in group:
        n *= size
    return n


def at(direction):
    axis, weight, size = direction
    return (lax.axis_index(axis) // weight) % size


def member(group):
    index, scale = 0, 1
    for direction in group:
        index = index + at(direction) * scale
        scale *= direction[2]
    return index


def steps_of(group):
    moves = [()]
    for direction in group:
        moves = [m + (k,) for m in moves for k in range(direction[2])]

    def way(move):
        return sum(
            min(k, d[2] - k) * (2 if d == Y_HI else 1) for d, k in zip(group, move)
        )

    return sorted([m for m in moves if any(m)], key=lambda m: -way(m))


def goal(group, move):
    index, scale = 0, 1
    place = {a: lax.axis_index(a) for a in AXES}
    for direction, k in zip(group, move):
        axis, weight, size = direction
        here = at(direction)
        there = (here + k) % size
        place[axis] = place[axis] + weight * (there - here)
        index = index + there * scale
        scale *= size
    return index, place


def expert_of(x, z, c):
    return c * 16 + x * 4 + z


def expert_kernel(
    sent_x, sent_top, sent_p, own_rank, near0, near1, near2,
    home, own_gain, scaled0, scaled1, total,
    returned, gains_back, home_sum,
    slots_x, slots_top, slots_p, far0, far1, far2, pulled, gains,
    gate_w, up_w, down_w, rows_in, rows_top, hidden_s, gate_s, up_s, out_s, gate_g, up_g,
    block_s, kept, given, other,
    send, recv, send_back, recv_back, send_core, recv_core, local,
):
    dp, z, c = (lax.axis_index(a) for a in AXES)
    x, core = (dp // 2) % 4, dp % 2
    me = member(PLANE)
    near, far = (near0, near1, near2), (far0, far1, far2)
    barrier = pltpu.get_barrier_semaphore()
    steps = steps_of(PLANE)
    mate = goal((CORE,), (1,))[1]
    for move in steps:
        pl.semaphore_signal(
            barrier, inc=1, device_id=goal(PLANE, move)[1], device_id_type=MESH
        )
    pl.semaphore_signal(barrier, inc=1, device_id=mate, device_id_type=MESH)
    pl.semaphore_wait(barrier, len(steps) + 1)

    def to_mate(source, target, k):
        return pltpu.make_async_remote_copy(
            src_ref=source,
            dst_ref=target,
            send_sem=send_core.at[k],
            recv_sem=recv_core.at[k],
            device_id=mate,
            device_id_type=MESH,
        )

    swaps = [to_mate(near[i], far[i], 8 + i) for i in range(3)]
    for copy in swaps:
        copy.start()
    out_going = []
    for k, (source, target) in enumerate(
        ((sent_x, slots_x), (sent_p, slots_p), (sent_top, slots_top))
    ):
        group = []
        for i, move in enumerate(steps):
            index, place = goal(PLANE, move)
            group.append(
                pltpu.make_async_remote_copy(
                    src_ref=source.at[index],
                    dst_ref=target.at[me],
                    send_sem=send.at[k, i],
                    recv_sem=recv.at[k, i],
                    device_id=place,
                    device_id_type=MESH,
                )
            )
            group[-1].start()
        group.append(pltpu.make_async_copy(source.at[me], target.at[me], local.at[k]))
        group[-1].start()
        out_going.append(group)

    for copy in swaps:
        copy.wait()
    for which in range(3):
        for zs in range(4):
            for cs in range(2):
                for half in range(2):
                    part = jnp.where(
                        core == half, near[which][zs + 4 * cs], far[which][zs + 4 * cs]
                    )
                    if which < 2:
                        (gate_w, up_w)[which][
                            zs * 256 + half * 128 : zs * 256 + half * 128 + 128,
                            cs * 256 : cs * 256 + 256,
                        ] = part
                    else:
                        down_w[
                            cs * 256 + half * 128 : cs * 256 + half * 128 + 128,
                            zs * 256 : zs * 256 + 256,
                        ] = part
    for copy in out_going[0]:
        copy.wait()

    def forward(s, _):
        span = pl.ds(pl.multiple_of(s * CAP, CAP), CAP)
        x_rows = jnp.concatenate([slots_x[4 * s + j] for j in range(4)], axis=1)
        gate_act = dot(x_rows, gate_w[...], ((1,), (0,)))
        up_act = dot(x_rows, up_w[...], ((1,), (0,)))
        hidden = (gate_act * jax.nn.sigmoid(gate_act) * up_act).astype(LOW)
        out_s[span, :] = dot(hidden, down_w[...], ((1,), (0,)))
        rows_in[span, :] = x_rows
        hidden_s[span, :] = hidden
        gate_s[span, :] = gate_act
        up_s[span, :] = up_act
        return 0

    lax.fori_loop(0, 4, forward, 0)
    for copy in out_going[1]:
        copy.wait()
    early = [copy for copy, move in zip(out_going[2], steps) if move[1] == 2]
    late = [copy for copy, move in zip(out_going[2], steps) if move[1] != 2]
    late.append(out_going[2][-1])

    def home_of(s, j):
        place = {"dp": dp + 2 * (s - x), "row": j, "col": c}
        return place, 4 * s + j

    def go_back(s, j, from_x, from_g):
        place, index = home_of(s, j)
        return [
            pltpu.make_async_remote_copy(
                src_ref=source,
                dst_ref=target.at[me],
                send_sem=send_back.at[k, index],
                recv_sem=recv_back.at[k, me],
                device_id=place,
                device_id_type=MESH,
            )
            for k, (source, target) in enumerate(((from_x, returned), (from_g, gains_back)))
        ]

    def backward(i, _):
        s = (x + 2 + i) % 4

        @pl.when(i == 0)
        def _():
            for copy in early:
                copy.wait()

        @pl.when(i == 1)
        def _():
            for copy in late:
                copy.wait()

        span = pl.ds(pl.multiple_of(s * CAP, CAP), CAP)
        top = jnp.concatenate([slots_top[4 * s + j] for j in range(4)], axis=1).astype(F32)
        p = jnp.transpose(slots_p[4 * s])[:CAP, :1]
        gate_act, up_act, out = gate_s[span, :], up_s[span, :], out_s[span, :]
        sig = jax.nn.sigmoid(gate_act)
        slot_grad = (p * top).astype(LOW)
        hidden_grad = dot(slot_grad, down_w[...], ((1,), (1,)))
        grad_gate = (hidden_grad * up_act * sig * (1.0 + gate_act * (1.0 - sig))).astype(LOW)
        grad_up = (hidden_grad * gate_act * sig).astype(LOW)
        pull = dot(grad_gate, gate_w[...], ((1,), (1,)))
        pull = (pull + dot(grad_up, up_w[...], ((1,), (1,)))).astype(LOW)
        gain = jnp.sum(top * out, axis=1, keepdims=True)
        gains[s] = jnp.zeros((8, 256), F32)
        gains[s, :, :CAP] = jnp.transpose(jnp.broadcast_to(gain, (CAP, 128)))[:8]
        for j in range(4):
            pulled[j, s] = pull[:, j * 256 : j * 256 + 256]
        rows_top[span, :] = slot_grad
        gate_g[span, :] = grad_gate
        up_g[span, :] = grad_up
        out = (p * out).astype(LOW)
        for j in range(4):
            scaled0[4 * s + j] = out[: CAP // 2, j * 256 : j * 256 + 256]
            scaled1[4 * s + j] = out[CAP // 2 :, j * 256 : j * 256 + 256]
        for kz in (2, 1, 3, 0):
            j = (z + kz) % 4

            @pl.when((s != x) | (j != z))
            def _(j=j):
                for copy in go_back(s, j, pulled.at[j, s], gains.at[s]):
                    copy.start()

        return 0

    lax.fori_loop(0, 4, backward, 0)
    near_rows = pl.ds(pl.multiple_of(core * 128, 128), 128)
    far_rows = pl.ds(pl.multiple_of((1 - core) * 128, 128), 128)

    def block(m, _):
        wide = pl.ds(pl.multiple_of((m % 4) * 256, 256), 256)
        narrow = pl.ds(pl.multiple_of((m // 4) * 256, 256), 256)
        for which in range(3):
            if which < 2:
                left, right = rows_in[:, wide], (gate_g, up_g)[which][:, narrow]
            else:
                left, right = hidden_s[:, narrow], rows_top[:, wide]
            block_s[...] = dot(left, right, ((0,), (0,)))
            given[m, which] = block_s[far_rows, :].astype(LOW)
            kept[m, which] = block_s[near_rows, :]
        to_mate(given.at[m], other.at[m], m).start()
        return 0

    lax.fori_loop(0, 8, block, 0)
    returned[me] = pulled[z, x]
    gains_back[me] = gains[x]

    def add(m, _):
        to_mate(given.at[m], other.at[m], m).wait()
        total[m] = (kept[m] + other[m].astype(F32)).astype(LOW)
        return 0

    lax.fori_loop(0, 8, add, 0)
    home_sum[...] = jnp.zeros((LENGTH, 256), F32)

    def collect(n, _):
        sx = (x + 6 - n // 4) % 4
        sz = (z + 4 - (2 + 3 * (n % 4)) % 4) % 4
        index = 4 * sx + sz

        @pl.when(index != me)
        def _():
            for copy in go_back(sx, sz, pulled.at[0, 0], gains.at[0]):
                copy.wait_send()
            for k, (source, target) in enumerate(
                ((pulled.at[0, 0], returned), (gains.at[0], gains_back))
            ):
                pltpu.make_async_remote_copy(
                    src_ref=source,
                    dst_ref=target.at[index],
                    send_sem=send_back.at[k, index],
                    recv_sem=recv_back.at[k, index],
                    device_id=home_of(sx, sz)[0],
                    device_id_type=MESH,
                ).wait_recv()

        places = lax.broadcasted_iota(jnp.int32, (CAP, LENGTH), 0)
        taken = own_rank[index] == places
        pick = jnp.where(taken, 1.0, 0.0).astype(LOW)
        home_sum[...] += dot(pick, returned[index], ((0,), (0,)))
        gain = jnp.transpose(gains_back[index])[:CAP, :1]
        own_gain[pl.ds(index, 1), :] = jnp.sum(
            jnp.where(taken, gain, 0.0), axis=0, keepdims=True
        )
        return 0

    lax.fori_loop(0, 16, collect, 0)
    home[...] = home_sum[...].astype(LOW)


def expert_step(number, *operands):
    spec = pl.BlockSpec(memory_space=pltpu.VMEM)
    return pl.pallas_call(
        expert_kernel,
        out_shape=[
            jax.ShapeDtypeStruct((LENGTH, 256), LOW),
            jax.ShapeDtypeStruct((16, LENGTH), F32),
            jax.ShapeDtypeStruct((16, CAP // 2, 256), LOW),
            jax.ShapeDtypeStruct((16, CAP // 2, 256), LOW),
            jax.ShapeDtypeStruct((8, 3, 128, 256), LOW),
        ],
        in_specs=[spec] * 7,
        out_specs=[spec] * 5,
        scratch_shapes=[
            pltpu.VMEM((16, CAP, 256), LOW),
            pltpu.VMEM((16, 8, 256), F32),
            pltpu.VMEM((LENGTH, 256), F32),
            pltpu.VMEM((16, CAP, 256), LOW),
            pltpu.VMEM((16, CAP, 256), LOW),
            pltpu.VMEM((16, 8, 256), F32),
            pltpu.VMEM((8, 128, 256), LOW),
            pltpu.VMEM((8, 128, 256), LOW),
            pltpu.VMEM((8, 128, 256), LOW),
            pltpu.VMEM((4, 4, CAP, 256), LOW),
            pltpu.VMEM((4, 8, 256), F32),
            pltpu.VMEM((D, 512), LOW),
            pltpu.VMEM((D, 512), LOW),
            pltpu.VMEM((512, D), LOW),
            pltpu.VMEM((640, D), LOW),
            pltpu.VMEM((640, D), LOW),
            pltpu.VMEM((640, 512), LOW),
            pltpu.VMEM((640, 512), F32),
            pltpu.VMEM((640, 512), F32),
            pltpu.VMEM((640, D), F32),
            pltpu.VMEM((640, 512), LOW),
            pltpu.VMEM((640, 512), LOW),
            pltpu.VMEM((256, 256), F32),
            pltpu.VMEM((8, 3, 128, 256), F32),
            pltpu.VMEM((8, 3, 128, 256), LOW),
            pltpu.VMEM((8, 3, 128, 256), LOW),
            pltpu.SemaphoreType.DMA((3, 15)),
            pltpu.SemaphoreType.DMA((3, 15)),
            pltpu.SemaphoreType.DMA((2, 16)),
            pltpu.SemaphoreType.DMA((2, 16)),
            pltpu.SemaphoreType.DMA((11,)),
            pltpu.SemaphoreType.DMA((11,)),
            pltpu.SemaphoreType.DMA((3,)),
        ],
        compiler_params=pltpu.CompilerParams(
            collective_id=number, has_side_effects=True, vmem_limit_bytes=60 * 1024 * 1024
        ),
        name="expert",
    )(*operands)


def as_row(column):
    return jnp.transpose(jnp.broadcast_to(column, (512, 128)))[:8]


def as_column(row):
    return jnp.transpose(jnp.broadcast_to(row, (8, 512)))[:, :1]


def launch(send, recv, used, mode, group, source, target):
    me = member(group)
    copies = []
    for move in steps_of(group):
        index, place = goal(group, move)
        copies.append(
            pltpu.make_async_remote_copy(
                src_ref=source(index) if mode == "split" else source,
                dst_ref=target if mode == "swap" else target.at[me],
                send_sem=send.at[used[0]],
                recv_sem=recv.at[used[0]],
                device_id=place,
                device_id_type=MESH,
            )
        )
        used[0] += 1
        copies[-1].start()
    if mode != "swap":
        target[me] = source(me)[...] if mode == "split" else source[...]
    return copies


HEAD_OUT = (
    ((8, 512, 128), LOW),
    ((8, 128, 256), LOW),
    ((8, 128, 256), LOW),
    ((8, 128, 256), LOW),
    ((2, 512, 512), F32),
    ((512, 128), LOW),
    ((512, 128), LOW),
    ((512, 128), LOW),
    ((512, 1), F32),
    ((512, 256), LOW),
    ((512, 256), F32),
    ((512, 1), F32),
    ((512, 256), LOW),
    ((32, 512), F32),
    ((32, 512), F32),
    ((16, 1, 512), jnp.int32),
    ((16, CAP, 256), LOW),
    ((16, CAP, 256), LOW),
    ((16, 8, 256), F32),
)
HEAD_SCRATCH = (
    ((4, 512, 256), LOW),
    ((8, 256), F32),
    ((4, 8, 256), F32),
    ((4, 256, 128), LOW),
    ((4, 256, 128), LOW),
    ((4, 256, 128), LOW),
    ((2, 512, 256), LOW),
    ((8, 512), F32),
    ((4, 8, 512), F32),
    ((32, 512), F32),
    ((4, 32, 512), F32),
    ((32, 512), jnp.int32),
)


def head_kernel(
    x_in, gain1, gain2, w_query, w_key, w_value, w_out, router, ids, segment, cot,
    cos_q, sin_q, cos_kv, sin_kv, w_gate, w_up, w_down,
    attended_all, near0, near1, near2, weights_ref, attended, queries, kv, scale_attn,
    normed_own, resid_ref, scale_ffn, normed_ffn, router_gain, probs_ref, own_rank,
    sent_x, sent_top, sent_p,
    x_all, gain, gain_all, kv_w, q_all, kv_all, out_all, square, squares, logit, logits,
    rank_ref, send, recv, local,
):
    dp, z, c = (lax.axis_index(a) for a in AXES)
    x, core = (dp // 2) % 4, dp % 2
    barrier = pltpu.get_barrier_semaphore()
    team = steps_of(TEAM)
    for move in team:
        pl.semaphore_signal(
            barrier, inc=1, device_id=goal(TEAM, move)[1], device_id_type=MESH
        )
    pl.semaphore_wait(barrier, len(team))
    used = [0]

    def begin(mode, group, source, target):
        return launch(send, recv, used, mode, group, source, target)

    def wait(copies):
        for copy in copies:
            copy.wait()

    def shards(w, target, k):
        half = pl.ds(pl.multiple_of(core * 128, 128), 128)
        me = member(TEAM)
        copies = []
        for move in team:
            place = goal(TEAM, move)[1]
            copies.append(
                pltpu.make_async_remote_copy(
                    src_ref=w.at[expert_of(x, place["row"], place["col"]), half, :],
                    dst_ref=target.at[me],
                    send_sem=send.at[used[0]],
                    recv_sem=recv.at[used[0]],
                    device_id=place,
                    device_id_type=MESH,
                )
            )
            used[0] += 1
        copies.append(
            pltpu.make_async_copy(
                w.at[expert_of(x, z, c), half, :], target.at[me], local.at[k]
            )
        )
        for copy in copies:
            copy.start()
        return copies

    gain[...] = jnp.broadcast_to(gain1[...], (8, 256))
    for j in range(4):
        kv_w[j, :, :64] = w_key[:, j * 64 : j * 64 + 64]
        kv_w[j, :, 64:] = w_value[:, j * 64 : j * 64 + 64]
    first = begin("share", (Z,), x_in, x_all)
    first += begin("share", (Z,), gain, gain_all)

    def columns(j):
        return w_query.at[:, pl.ds(pl.multiple_of(j * 128, 128), 128)]

    parts = begin("split", (Z,), columns, q_all)
    parts += begin("split", (Z,), lambda j: kv_w.at[j], kv_all)
    parts += begin("share", (SIDE,), w_out, out_all)
    bulk = shards(w_gate, near0, 0)

    experts = lax.broadcasted_iota(jnp.int32, (EXPERTS, LENGTH), 0)
    hits = ids[0:1] == experts
    for k in range(1, 8):
        hits = hits | (ids[k : k + 1] == experts)
    at_row = lax.broadcasted_iota(jnp.int32, (LENGTH, LENGTH), 0)
    at_lane = lax.broadcasted_iota(jnp.int32, (LENGTH, LENGTH), 1)
    earlier = jnp.where(at_row < at_lane, 1.0, 0.0).astype(LOW)
    marks = jnp.where(hits, 1.0, 0.0)
    rank = dot(marks.astype(LOW), earlier, ((1,), (0,)))
    rank_ref[...] = jnp.where(hits, rank, -1.0).astype(jnp.int32)
    own = pl.ds(pl.multiple_of(c * 16, 16), 16)
    mine = rank_ref[own, :]
    for e in range(16):
        own_rank[e] = mine[e : e + 1]

    def taken_by(e):
        places = lax.broadcasted_iota(jnp.int32, (CAP, LENGTH), 0)
        return own_rank[e] == places

    def place_top(e, _):
        pick = jnp.where(taken_by(e), 1.0, 0.0).astype(LOW)
        sent_top[e] = dot(pick, cot[...], ((1,), (0,))).astype(LOW)
        return 0

    lax.fori_loop(0, 16, place_top, 0)

    wait(first)
    total = jnp.zeros((LENGTH, 1), F32)
    for j in range(4):
        block = x_all[j].astype(F32)
        total = total + jnp.sum(block * block, axis=1, keepdims=True)
    scale = lax.rsqrt(total / D + EPSILON)
    scale_attn[...] = scale
    residual = x_in[...].astype(F32)
    normed_own[...] = (residual * scale * gain1[...]).astype(LOW)
    wait(parts)
    part_q = jnp.zeros((LENGTH, 128), F32)
    part_kv = jnp.zeros((LENGTH, 128), F32)
    for j in range(4):
        normed = (x_all[j].astype(F32) * scale * gain_all[j, :1]).astype(LOW)
        part_q = part_q + dot(normed, q_all[j], ((1,), (0,)))
        part_kv = part_kv + dot(normed, kv_all[j], ((1,), (0,)))
    low_lane = lax.broadcasted_iota(jnp.int32, (LENGTH, 128), 1) % 64 < 32

    def turn(value, cosine, sine_part):
        other = jnp.where(low_lane, pltpu.roll(value, 96, 1), pltpu.roll(value, 32, 1))
        return (value * cosine - other * sine_part).astype(LOW)

    queries[...] = turn(part_q, cos_q[...], sin_q[...])
    kv[...] = turn(part_kv, cos_kv[...], sin_kv[...])
    keys, values = kv[:, :64], kv[:, 64:]
    segment_row = segment[...].astype(F32)
    allowed = (at_lane <= at_row) & (segment_row == as_column(segment_row))
    for h in range(2):
        span = slice(h * HEAD_DIM, h * HEAD_DIM + HEAD_DIM)
        scores = dot(queries[:, span], keys, ((1,), (1,))) * HEAD_DIM ** (-0.5)
        scores = jnp.where(allowed, scores, MASKED)
        top = jnp.max(scores, axis=1, keepdims=True)
        log_total = top + jnp.log(jnp.sum(jnp.exp(scores - top), axis=1, keepdims=True))
        weights = jnp.exp(scores - log_total)
        weights_ref[h] = weights
        attended[:, span] = dot(weights.astype(LOW), values, ((1,), (0,))).astype(LOW)
    met = begin("share", TEAM, attended, attended_all)
    bulk += shards(w_up, near1, 1)
    wait(met)
    resid = residual
    for m in range(8):
        rows_of = out_all[m // 4, (m % 4) * 128 : (m % 4) * 128 + 128]
        resid = resid + dot(attended_all[m], rows_of, ((1,), (0,)))
    resid_ref[...] = resid
    square[...] = as_row(jnp.sum(resid * resid, axis=1, keepdims=True))
    met = begin("share", (Z,), square, squares)
    bulk += shards(w_down, near2, 2)
    router_gain[...] = lax.dot_general(
        router[...].astype(F32),
        resid * gain2[...],
        (((1,), (1,)), ((), ())),
        precision=lax.Precision.HIGHEST,
        preferred_element_type=F32,
    )
    wait(met)
    row = (squares[0, :1] + squares[1, :1]) + (squares[2, :1] + squares[3, :1])
    scale = as_column(lax.rsqrt(row / D + EPSILON))
    scale_ffn[...] = scale
    normed_ffn[...] = (resid_ref[...] * scale * gain2[...]).astype(LOW)
    logit[...] = dot(router[...], normed_ffn[...], ((1,), (1,)))
    met = begin("share", (Z,), logit, logits)
    wait(met)
    sums = (logits[0] + logits[1]) + (logits[2] + logits[3])
    chosen = jnp.where(hits, sums, MASKED)
    chosen = jnp.exp(chosen - jnp.max(chosen, axis=0, keepdims=True)) * marks
    probs_ref[...] = chosen / jnp.sum(chosen, axis=0, keepdims=True)

    def place_x(e, _):
        taken = taken_by(e)
        pick = jnp.where(taken, 1.0, 0.0).astype(LOW)
        sent_x[e] = dot(pick, normed_ffn[...], ((1,), (0,))).astype(LOW)
        p = probs_ref[pl.ds(c * 16 + e, 1), :]
        p = jnp.sum(jnp.where(taken, p, 0.0), axis=1, keepdims=True)
        sent_p[e] = jnp.zeros((8, 256), F32)
        sent_p[e, :, :CAP] = jnp.transpose(jnp.broadcast_to(p, (CAP, 128)))[:8]
        return 0

    lax.fori_loop(0, 16, place_x, 0)
    wait(bulk)


def head_step(number, *operands):
    spec = pl.BlockSpec(memory_space=pltpu.VMEM)
    far = pl.BlockSpec(memory_space=pl.ANY)
    return pl.pallas_call(
        head_kernel,
        out_shape=[jax.ShapeDtypeStruct(*v) for v in HEAD_OUT],
        in_specs=[spec] * (len(operands) - 3) + [far] * 3,
        out_specs=[spec] * len(HEAD_OUT),
        scratch_shapes=[pltpu.VMEM(*v) for v in HEAD_SCRATCH]
        + [
            pltpu.SemaphoreType.DMA((56,)),
            pltpu.SemaphoreType.DMA((56,)),
            pltpu.SemaphoreType.DMA((3,)),
        ],
        compiler_params=pltpu.CompilerParams(
            collective_id=number, has_side_effects=True, vmem_limit_bytes=60 * 1024 * 1024
        ),
        name="head",
    )(*operands)


TAIL_OUT = (
    ((8, 3, 128, 256), LOW),
    ((16, 32, 256), LOW),
    ((16, 8, 256), F32),
    ((16, 16, 1024), LOW),
    ((16, 8, 256), F32),
    ((512, 256), LOW),
    ((512, 256), LOW),
)
TAIL_SCRATCH = (
    ((8, 512), F32),
    ((512, 256), LOW),
    ((2, 16, 512), F32),
    ((8, 8, 512), F32),
    ((4, 32, 512), F32),
    ((4, 128, 256), LOW),
    ((16, 80, 256), LOW),
    ((16, 80, 256), LOW),
    ((512, 256), LOW),
    ((4, 512, 256), LOW),
    ((512, 256), F32),
    ((512, 256), LOW),
    ((16, 32, 256), LOW),
    ((32, 256), LOW),
    ((16, 8, 256), F32),
    ((16, 8, 256), F32),
    ((8, 256), F32),
    ((512, 256), LOW),
    ((4, 512, 256), LOW),
    ((512, 1024), LOW),
    ((512, 256), LOW),
    ((512, 256), LOW),
    ((8, 512), F32),
    ((8, 8, 512), F32),
    ((256, 1024), LOW),
    ((16, 16, 1024), LOW),
    ((16, 1024), LOW),
    ((8, 256), F32),
    ((512, 256), F32),
    ((512, 256), LOW),
    ((512, 256), LOW),
)
TAIL_SEMS = 224


def tail_kernel(
    home_ref, gain_own_ref, router_gain_ref, w_out_ref, scaled0_ref, scaled1_ref, kept_ref,
    resid_mid_ref, cot_ref, scale_ffn_ref, gain2_ref, probs_ref, router_ref, normed_ffn_ref,
    attended_all_ref, attended_ref, queries_ref, kv_ref, weights_ref, cos_q_ref, sin_q_ref,
    cos_kv_ref, sin_kv_ref, whole_ref, normed_own_ref, x_in_ref, scale_attn_ref, gain1_ref,
    own_rank_ref, owned_ref, out_sum_ref, router_sum_ref, joined_sum_ref, gains_ref,
    block_out_ref, grad_input_ref, pull_ref, home2_ref, gain_pair_ref, pulls_ref,
    router_pull_ref, out_heads_ref, back0_ref, back1_ref, mid_ref, mid_all_ref,
    grad_mid_ref, g_out_ref, out_parts_ref, out_chunk_ref, g_router_ref, router_parts_ref,
    router_chunk_ref, proj_ref, proj_all_ref, flat_ref, gn_ref, gn2_ref, pull2_ref,
    pulls2_ref, g_joined_ref, joined_parts_ref, joined_chunk_ref, gains_own_ref,
    moe_sum_ref, moe_ref, moe2_ref, send, recv,
):
    dp, z, c = (lax.axis_index(a) for a in AXES)
    y_hi, x, core = dp // 8, (dp // 2) % 4, dp % 2
    owner = c * 8 + x * 2 + z // 2
    slot = (z % 2) * 4 + y_hi * 2 + core
    barrier = pltpu.get_barrier_semaphore()
    moves = {}
    for g in (TEAM, PLANE, ALL_DP):
        for move in steps_of(g):
            full = {d: k for d, k in zip(g, move) if k}
            moves[tuple(sorted(full.items()))] = (g, move)
    for g, move in moves.values():
        pl.semaphore_signal(barrier, inc=1, device_id=goal(g, move)[1], device_id_type=MESH)
    sources = []
    for i in range(8):
        place = {
            "dp": ((i // 2) % 2) * 8 + x * 2 + i % 2,
            "row": core * 2 + i // 4,
            "col": y_hi,
        }
        mine = (place["dp"] == dp) & (place["row"] == z) & (place["col"] == c)
        sources.append(mine)

        @pl.when(jnp.logical_not(mine))
        def _(place=place):
            pl.semaphore_signal(barrier, inc=1, device_id=place, device_id_type=MESH)

    @pl.when(owner == dp)
    def _():
        pl.semaphore_wait(barrier, len(moves) + 7)

    @pl.when(owner != dp)
    def _():
        pl.semaphore_wait(barrier, len(moves) + 8)

    used = [0]

    def begin(mode, group, source, target):
        return launch(send, recv, used, mode, group, source, target)

    def wait(copies):
        for copy in copies:
            copy.wait()

    kept, owned = kept_ref, owned_ref
    first_deliver = TAIL_SEMS - 24

    def parcel(which, j, to_slot):
        return pltpu.make_async_remote_copy(
            src_ref=kept.at[j, which],
            dst_ref=owned.at[to_slot, which],
            send_sem=send.at[first_deliver + which * 8 + j],
            recv_sem=recv.at[first_deliver + which * 8 + to_slot],
            device_id={"dp": owner, "row": j % 4, "col": j // 4},
            device_id_type=MESH,
        )

    def own(j):
        return (owner == dp) & (z == j % 4) & (c == j // 4)

    def deliver(which):
        for kz, kc in ((2, 1), (2, 0), (1, 1), (3, 1), (1, 0), (3, 0), (0, 1), (0, 0)):
            j = (z + kz) % 4 + 4 * ((c + kc) % 2)

            @pl.when(own(j))
            def _(j=j):
                owned[slot, which] = kept[j, which]

            @pl.when(jnp.logical_not(own(j)))
            def _(j=j):
                parcel(which, j, slot).start()

    first = begin("swap", (SIDE,), home_ref, home2_ref)
    first += begin("share", (SIDE,), gain_own_ref, gain_pair_ref)
    first += begin("share", (Z,), router_gain_ref, router_pull_ref)
    pull = jnp.sum(
        home_ref[...].astype(F32) * gain2_ref[...] * resid_mid_ref[...], axis=1, keepdims=True
    )
    pull_ref[...] = as_row(pull)
    first += begin("share", TEAM, pull_ref, pulls_ref)
    heads = begin("split", (Z,), lambda j: w_out_ref.at[j], out_heads_ref)
    back0 = begin("split", PLANE, lambda j: scaled0_ref.at[j], back0_ref)
    deliver(0)
    wait(first)
    home = home_ref[...].astype(F32) + home2_ref[...].astype(F32)
    grad_prob = jnp.concatenate([gain_pair_ref[0], gain_pair_ref[1]], axis=0)
    probs = probs_ref[...]
    inner = jnp.sum(probs * grad_prob, axis=0, keepdims=True)
    grad_logits = (probs * (grad_prob - inner)).astype(LOW)
    router_pull = (router_pull_ref[0] + router_pull_ref[1]) + (
        router_pull_ref[2] + router_pull_ref[3]
    )
    row = jnp.sum(grad_logits.astype(F32) * router_pull, axis=0, keepdims=True)
    for i in range(8):
        row = row + pulls_ref[i, :1]
    project = as_column(row) / D
    grad_normed = home + dot(grad_logits, router_ref[...], ((0,), (0,)))
    resid_mid, scale = resid_mid_ref[...], scale_ffn_ref[...]
    weighted = grad_normed * gain2_ref[...]
    grad_mid = (
        cot_ref[...].astype(F32) + scale * weighted - resid_mid * scale**3 * project
    )
    mid_ref[...] = grad_mid.astype(LOW)
    grad_mid_ref[...] = grad_mid
    gains_own_ref[...] = jnp.zeros((8, 256), F32)
    gains_own_ref[1:2] = jnp.sum(grad_normed * resid_mid * scale, axis=0, keepdims=True)
    middle = begin("share", (Z,), mid_ref, mid_all_ref)
    grad_router = dot(grad_logits, normed_ffn_ref[...], ((1,), (0,)))
    g_router_ref[...] = jnp.zeros((16, 8, 256), F32)
    for j in range(16):
        g_router_ref[j, :2] = grad_router[2 * j : 2 * j + 2]
    for j in range(4):
        g_out_ref[j * 128 : j * 128 + 128] = dot(
            attended_all_ref[4 * c + j], mid_ref[...], ((0,), (0,))
        ).astype(LOW)
    sums = begin(
        "split",
        ALL_DP,
        lambda j: g_out_ref.at[pl.ds(pl.multiple_of(j * 32, 32), 32)],
        out_parts_ref,
    )
    sums += begin("split", ALL_DP, lambda j: g_router_ref.at[j], router_parts_ref)
    deliver(1)

    wait(heads)
    wait(middle)
    grad_att = dot(mid_all_ref[0], out_heads_ref[0], ((1,), (1,)))
    for j in range(1, 4):
        grad_att = grad_att + dot(mid_all_ref[j], out_heads_ref[j], ((1,), (1,)))
    grad_att = grad_att.astype(LOW)
    product = grad_att.astype(F32) * attended_ref[...].astype(F32)
    keys, values = kv_ref[:, :64], kv_ref[:, 64:]
    grad_q = []
    grad_k = jnp.zeros((512, HEAD_DIM), F32)
    grad_v = jnp.zeros((512, HEAD_DIM), F32)
    for h in range(2):
        span = slice(h * HEAD_DIM, h * HEAD_DIM + HEAD_DIM)
        grad_h = grad_att[:, span]
        weights = weights_ref[h]
        delta = jnp.sum(product[:, span], axis=1, keepdims=True)
        grad_weights = dot(grad_h, values, ((1,), (1,)))
        grad_scores = (weights * (grad_weights - delta)).astype(LOW)
        grad_q.append(dot(grad_scores, keys, ((1,), (0,))))
        grad_k = grad_k + dot(grad_scores, queries_ref[:, span], ((0,), (0,)))
        grad_v = grad_v + dot(weights.astype(LOW), grad_h, ((0,), (0,)))
    score_scale = HEAD_DIM ** (-0.5)
    low_lane = lax.broadcasted_iota(jnp.int32, (512, 128), 1) % 64 < 32

    def turn(value, cosine, sine_part):
        other = jnp.where(low_lane, pltpu.roll(value, 96, 1), pltpu.roll(value, 32, 1))
        return (value * cosine + other * sine_part).astype(LOW)

    both = jnp.concatenate(grad_q, axis=1) * score_scale
    proj_ref[:, :128] = turn(both, cos_q_ref[...], sin_q_ref[...])
    both = jnp.concatenate([grad_k * score_scale, grad_v], axis=1)
    proj_ref[:, 128:] = turn(both, cos_kv_ref[...], sin_kv_ref[...])
    projected = begin("share", (Z,), proj_ref, proj_all_ref)
    back1 = begin("split", PLANE, lambda j: scaled1_ref.at[j], back1_ref)

    wait(sums)
    total = out_parts_ref[0].astype(F32)
    routed = router_parts_ref[0]
    for j in range(1, 16):
        total = total + out_parts_ref[j].astype(F32)
        routed = routed + router_parts_ref[j]
    out_chunk_ref[...] = total.astype(LOW)
    router_chunk_ref[...] = routed
    rest = begin("share", ALL_DP, out_chunk_ref, out_sum_ref)
    rest += begin("share", ALL_DP, router_chunk_ref, router_sum_ref)
    moe_sum_ref[...] = jnp.zeros((512, 256), F32)

    def add_half(rows_of, start):
        def one(e, _):
            places = lax.broadcasted_iota(jnp.int32, (80, 512), 0) + start
            taken = (own_rank_ref[e] == places).astype(F32).astype(LOW)
            moe_sum_ref[...] += dot(taken, rows_of[e], ((0,), (0,)))
            return 0

        lax.fori_loop(0, 16, one, 0)

    wait(back0)
    add_half(back0_ref, 0)

    wait(projected)
    for j in range(4):
        flat_ref[:, j * 128 : j * 128 + 128] = proj_all_ref[j, :, :128]
        flat_ref[:, 512 + j * 64 : 576 + j * 64] = proj_all_ref[j, :, 128:192]
        flat_ref[:, 768 + j * 64 : 832 + j * 64] = proj_all_ref[j, :, 192:]
    grad_low = dot(flat_ref[...], whole_ref[...], ((1,), (1,))).astype(LOW)
    residual, gain1 = x_in_ref[...].astype(F32), gain1_ref[...]
    gn_ref[...] = grad_low
    pull = jnp.sum(grad_low.astype(F32) * gain1 * residual, axis=1, keepdims=True)
    pull2_ref[...] = as_row(pull)
    meet = begin("swap", (SIDE,), gn_ref, gn2_ref)
    meet += begin("share", TEAM, pull2_ref, pulls2_ref)
    g_joined_ref[...] = dot(normed_own_ref[...], flat_ref[...], ((0,), (0,))).astype(LOW)
    joined = begin(
        "split",
        ALL_DP,
        lambda j: g_joined_ref.at[pl.ds(pl.multiple_of(j * 16, 16), 16)],
        joined_parts_ref,
    )
    deliver(2)
    wait(back1)
    add_half(back1_ref, 80)
    moe_ref[...] = moe_sum_ref[...].astype(LOW)
    moe = begin("swap", (SIDE,), moe_ref, moe2_ref)
    wait(meet)
    grad_normed = gn_ref[...].astype(F32) + gn2_ref[...].astype(F32)
    row = pulls2_ref[0, :1]
    for i in range(1, 8):
        row = row + pulls2_ref[i, :1]
    project = as_column(row) / D
    weighted = grad_normed * gain1
    scale = scale_attn_ref[...]
    grad_input_ref[...] = (
        grad_mid_ref[...] + scale * weighted - residual * scale**3 * project
    ).astype(LOW)
    gains_own_ref[0:1] = jnp.sum(grad_normed * residual * scale, axis=0, keepdims=True)
    wait(joined)
    total = joined_parts_ref[0].astype(F32)
    for j in range(1, 16):
        total = total + joined_parts_ref[j].astype(F32)
    joined_chunk_ref[...] = total.astype(LOW)
    rest += begin("share", ALL_DP, joined_chunk_ref, joined_sum_ref)
    rest += begin("share", ALL_DP, gains_own_ref, gains_ref)
    wait(moe)
    block_out_ref[...] = (
        resid_mid + (moe_ref[...].astype(F32) + moe2_ref[...].astype(F32))
    ).astype(LOW)
    wait(rest)
    for which in range(3):
        for j in range(8):

            @pl.when(jnp.logical_not(own(j)))
            def _(j=j, which=which):
                parcel(which, j, slot).wait_send()

            @pl.when(jnp.logical_not(sources[j]))
            def _(j=j, which=which):
                parcel(which, 0, j).wait_recv()


def finish_kernel(
    owned, out_sum, router_sum, joined_sum, gains, block_in, grad_in,
    grad_gate, grad_up, grad_down, grad_query, grad_key, grad_value, grad_out, grad_router,
    gain_sum, block_out, grad_input,
):
    block_out[...] = block_in[...]
    grad_input[...] = grad_in[...]
    for j in range(16):
        part = joined_sum[j].astype(F32)
        at_rows = slice(16 * j, 16 * j + 16)
        grad_query[at_rows] = part[:, :512]
        grad_key[at_rows] = part[:, 512:768]
        grad_value[at_rows] = part[:, 768:]
        grad_out[32 * j : 32 * j + 32] = out_sum[j].astype(F32)
        grad_router[2 * j : 2 * j + 2] = router_sum[j, :2]
    total = gains[0]
    for j in range(1, 16):
        total = total + gains[j]
    gain_sum[...] = total
    for which, target in enumerate((grad_gate, grad_up, grad_down)):
        for i in range(2):
            for half in range(2):
                target[i, half * 128 : half * 128 + 128] = owned[i * 4 + half, which].astype(
                    F32
                ) + owned[i * 4 + 2 + half, which].astype(F32)


def finish_step(*operands):
    spec = pl.BlockSpec(memory_space=pltpu.VMEM)
    shapes = (
        [((2, 256, 256), F32)] * 3
        + [((256, 512), F32), ((256, 256), F32), ((256, 256), F32), ((512, 256), F32)]
        + [((32, 256), F32), ((8, 256), F32), ((512, 256), LOW), ((512, 256), LOW)]
    )
    return pl.pallas_call(
        finish_kernel,
        out_shape=[jax.ShapeDtypeStruct(*v) for v in shapes],
        in_specs=[spec] * 7,
        out_specs=[spec] * 11,
        compiler_params=pltpu.CompilerParams(vmem_limit_bytes=63 * 1024 * 1024),
        name="finish",
    )(*operands)


def tail_step(number, *operands):
    spec = pl.BlockSpec(memory_space=pltpu.VMEM)
    return pl.pallas_call(
        tail_kernel,
        out_shape=[jax.ShapeDtypeStruct(*v) for v in TAIL_OUT],
        in_specs=[spec] * len(operands),
        out_specs=[spec] * len(TAIL_OUT),
        scratch_shapes=[pltpu.VMEM(*v) for v in TAIL_SCRATCH]
        + [pltpu.SemaphoreType.DMA((TAIL_SEMS,)), pltpu.SemaphoreType.DMA((TAIL_SEMS,))],
        compiler_params=pltpu.CompilerParams(
            collective_id=number, has_side_effects=True, vmem_limit_bytes=60 * 1024 * 1024
        ),
        name="tail",
    )(*operands)


def rope_tables():
    half_dim = HEAD_DIM // 2
    exponent = np.arange(half_dim).astype(np.float32) * np.float32(2.0 / HEAD_DIM)
    rates = np.power(np.float32(ROPE_BASE), -exponent).astype(np.float32)
    angles = np.arange(LENGTH).astype(np.float32)[:, None] * rates[None, :]
    cosine = np.cos(angles.astype(np.float64)).astype(np.float32)
    sine_part = np.sin(angles.astype(np.float64)).astype(np.float32)
    idle = np.zeros((LENGTH, HEAD_DIM), np.float32)
    return (
        np.concatenate([cosine] * 4, axis=1),
        np.concatenate([sine_part, -sine_part] * 2, axis=1),
        np.concatenate([cosine, cosine, idle + 1.0], axis=1),
        np.concatenate([sine_part, -sine_part, idle], axis=1),
    )


def dot(a, b, dims):
    return lax.dot_general(a, b, (dims, ((), ())), preferred_element_type=F32)


def on_device(
    x_in,
    segments,
    expert_ids,
    cotangent,
    norm_gain1,
    w_query,
    w_key,
    w_value,
    w_out,
    norm_gain2,
    w_router,
    w_gate,
    w_up,
    w_down,
):
    tables = [jnp.asarray(t, F32) for t in rope_tables()]
    router = w_router.T
    gain1, gain2 = norm_gain1.reshape(1, 256), norm_gain2.reshape(1, 256)
    (
        attended_all,
        near_gate,
        near_up,
        near_down,
        weights,
        attended,
        queries,
        kv,
        scale_attn,
        normed_own,
        resid_mid,
        scale_ffn,
        normed_ffn,
        router_gain,
        probs,
        own_rank,
        sent_x,
        sent_top,
        sent_p,
    ) = head_step(
        2,
        x_in,
        gain1,
        gain2,
        w_query,
        w_key,
        w_value,
        w_out,
        router,
        expert_ids.T,
        segments,
        cotangent,
        *tables,
        w_gate,
        w_up,
        w_down,
    )
    home, own_gain, scaled0, scaled1, kept = expert_step(
        7, sent_x, sent_top, sent_p, own_rank, near_gate, near_up, near_down
    )

    (
        grad_gate,
        grad_up,
        grad_down,
        grad_query,
        grad_key,
        grad_value,
        grad_out,
        grad_router,
        gain_sum,
        block_out,
        grad_input,
    ) = finish_step(*tail_step(
        11,
        home,
        own_gain,
        router_gain,
        w_out.reshape(4, 128, 256),
        scaled0,
        scaled1,
        kept,
        resid_mid,
        cotangent,
        scale_ffn,
        gain2,
        probs,
        router,
        normed_ffn,
        attended_all,
        attended,
        queries,
        kv,
        weights,
        *tables,
        jnp.concatenate([w_query, w_key, w_value], axis=1),
        normed_own,
        x_in,
        scale_attn,
        gain1,
        own_rank,
    ))
    return (
        block_out,
        grad_input,
        grad_query,
        grad_key,
        grad_value,
        grad_out,
        grad_router.T,
        grad_gate,
        grad_up,
        grad_down,
        gain_sum[0],
        gain_sum[1],
    )


def solution(mesh):
    placed = (
        P("dp", "row"),
        P("dp", None),
        P("dp", None),
        P("dp", "row"),
        P("row"),
        P("row", "col"),
        P("row", "col"),
        P("row", "col"),
        P("col", "row"),
        P("row"),
        P("row", None),
        P(None, "row", "col"),
        P(None, "row", "col"),
        P(None, "col", "row"),
    )
    return jax.shard_map(
        on_device,
        mesh=mesh,
        in_specs=placed,
        out_specs=(
            P("dp", "row"),
            P("dp", "row"),
            P("row", "col"),
            P("row", "col"),
            P("row", "col"),
            P("col", "row"),
            P("row", None),
            P("dp", "row", "col"),
            P("dp", "row", "col"),
            P("dp", "col", "row"),
            P("row"),
            P("row"),
        ),
        check_vma=False,
    )
```
